32 devices in a mesh: gx: 16 (over z, y, x), gy: 2 (over core).
Axes of the slice: x: 2, y: 2, z: 4, core: 2. Of those that a mesh axis runs over, the one named last changes fastest.
Arguments:
- features: bfloat16 [16, 2, 8, 128, 256], P('gx', 'gy'), may hold values from -6 to 6
- kernel_weight: bfloat16 [27, 256, 256], P(None, 'gy'), may hold values from -0.109375 to 0.109375
- channel_bias: float32 [256], replicated, may hold values from -3 to 3
- send_list: int32 [16, 2, 2], P('gx', 'gy'), may hold values from 0 to 7
- rule_source: int32 [16, 2, 27, 4], P('gx', 'gy'), may hold values from 0 to 23
- rule_target: int32 [16, 2, 27, 4], P('gx', 'gy'), may hold values from 0 to 7
- live_counts: int32 [16, 2, 27], P('gx', 'gy'), may hold values from 1 to 4, as said below
- out_grad: bfloat16 [16, 2, 8, 128, 256], P('gx', 'gy'), may hold values from -6 to 6
Outputs:
- outputs: bfloat16 [16, 2, 8, 128, 256], P('gx', 'gy')
- feat_grad: bfloat16 [16, 2, 8, 128, 256], P('gx', 'gy')
- weight_grad: float32 [27, 256, 256], P(None, 'gy')
The draws below stay inside these ranges and needn't reach their ends.
Inputs may be any that keep to these rules, and one draw needn't show every extreme that they name: `rule_source`: index into the device's block table of its 8 own blocks followed by 2 blocks from each of the eight directions. `rule_target`: an own block of the device. `send_list`: an own block of the device; a block may appear more than once. `live_counts`: slots from this count up to 3 are padding whose indices carry no meaning.
All inputs are finite; a program needn't handle non-finite values.
Results may differ from the reference program's by a relative error of at most 0.007.
Values may be sent and summed in bfloat16 or wider, within the bound.
A program may use at most 128 MiB of HBM per device.

```python
import jax
import jax.numpy as jnp
from jax import lax

C = 256
KVOL = 27
ROWS = 128
BLK = 8
HB = 2
P_SIZE = 4
N_GX = 16
N_GY = 2


def draw_live_counts(key, part):
    first_key, second_key, third_key = jax.random.split(key, 3)
    density = jax.random.randint(first_key, (N_GX, N_GY, 1), 1, 3)
    base_count = jax.random.randint(second_key, (N_GX, N_GY, KVOL), 1, 3)
    counts = jnp.minimum(density * base_count, P_SIZE).reshape(-1)
    position = jax.random.randint(third_key, (), 0, N_GX * N_GY * KVOL)
    counts = counts.at[position].set(P_SIZE)
    return counts.reshape(N_GX, N_GY, KVOL).astype(jnp.int32)


def place_ends(result, stream_key, smallest, high):
    dims = result.shape
    spot = [jax.random.randint(jax.random.fold_in(stream_key, axis), (), 0, dims[axis]) for axis in range(len(dims))]
    result = result.at[tuple(spot)].set(smallest)
    longest = dims.index(max(dims))
    spot[longest] = (spot[longest] + 1) % dims[longest]
    return result.at[tuple(spot)].set(high)


def block_scale(stream_key, dims, shards, low, high):
    loudness = 1.0
    for axis_at, blocks in shards:
        draws = jax.random.uniform(jax.random.fold_in(jax.random.fold_in(stream_key, 6), axis_at), (blocks,), jnp.float32, low / len(shards), high / len(shards))
        loudness = loudness * jnp.repeat(jnp.exp(draws), dims[axis_at] // blocks).reshape((-1,) + (1,) * (len(dims) - 1 - axis_at))
    return loudness


def centred(stream_key, shape, scale, reach, shards=(), kind=jnp.bfloat16):
    loudness = block_scale(stream_key, shape, shards, -0.22, 0.18) if shards else 1.0
    result = jax.random.normal(stream_key, shape, jnp.float32) * scale * loudness
    return jnp.minimum(jnp.maximum(result, -reach), reach).astype(kind)


def setup_inputs(seed: int = 0) -> dict:
    keys = jax.random.split(jax.random.key(seed), 9)
    return {
        "features": centred(keys[0], (N_GX, N_GY, BLK, ROWS, C), 1.0, 6.0, ((0, 16), (1, 2))),
        "kernel_weight": centred(keys[1], (KVOL, C, C), (C * KVOL * P_SIZE // BLK) ** -0.5, 0.109375, ((1, 2),)),
        "channel_bias": centred(keys[2], (C,), 0.5, 3.0, (), jnp.float32),
        "send_list": place_ends(jax.random.randint(keys[3], (N_GX, N_GY, HB), 0, BLK), jax.random.fold_in(keys[3], 1), 0, BLK - 1).astype(jnp.int32),
        "rule_source": place_ends(jax.random.randint(keys[4], (N_GX, N_GY, KVOL, P_SIZE), 0, BLK + 8 * HB), jax.random.fold_in(keys[4], 1), 0, (BLK + 8 * HB) - 1).astype(jnp.int32),
        "rule_target": place_ends(jax.random.randint(keys[5], (N_GX, N_GY, KVOL, P_SIZE), 0, BLK), jax.random.fold_in(keys[5], 1), 0, BLK - 1).astype(jnp.int32),
        "live_counts": draw_live_counts(jax.random.fold_in(keys[8], 71), 0),
        "out_grad": centred(keys[7], (N_GX, N_GY, BLK, ROWS, C), 1.0, 6.0, ((0, 16), (1, 2))),
    }


def device_pass(feats, neighbour, kernel_weight, channel_bias, rule_source, rule_target, live_counts, out_grad):
    blocks = feats.shape[0]
    rows_per = feats.shape[1]
    width = feats.shape[2]
    block_table = jnp.concatenate([feats, neighbour.reshape((-1, rows_per, width))], axis=0)
    total_blocks = block_table.shape[0]
    kvol, slots = rule_source.shape
    slot_index = jnp.arange(slots, dtype=jnp.int32)
    live_two = slot_index[None, :] < live_counts[:, None]
    live_mask = live_two.reshape(-1)
    sources = rule_source.reshape(-1)
    targets = rule_target.reshape(-1)
    gathered = block_table[sources].reshape(kvol, slots, rows_per, width)
    products = jnp.einsum("kprc,kcd->kprd", gathered.astype(jnp.float32), kernel_weight.astype(jnp.float32))
    products = products.reshape(kvol * slots, rows_per, width)
    scatter_out = ((targets[None, :] == jnp.arange(blocks, dtype=jnp.int32)[:, None]) & live_mask[None, :]).astype(jnp.float32)
    preact = jnp.einsum("bq,qrd->brd", scatter_out, products, precision=lax.Precision.HIGHEST) + channel_bias
    outputs = jax.nn.silu(preact).astype(jnp.bfloat16)
    sigmoid_vals = jax.nn.sigmoid(preact)
    dpre = (out_grad.astype(jnp.float32) * sigmoid_vals * (1.0 + preact * (1.0 - sigmoid_vals))).astype(jnp.bfloat16)
    picked = dpre[targets].reshape(kvol, slots, rows_per, width)
    picked_live = jnp.where(live_two[:, :, None, None], picked, jnp.zeros_like(picked))
    backs = jnp.einsum("kprd,kcd->kprc", picked.astype(jnp.float32), kernel_weight.astype(jnp.float32))
    backs = backs.reshape(kvol * slots, rows_per, width)
    scatter_in = ((sources[None, :] == jnp.arange(total_blocks, dtype=jnp.int32)[:, None]) & live_mask[None, :]).astype(jnp.float32)
    table_grad = jnp.einsum("tq,qrc->trc", scatter_in, backs, precision=lax.Precision.HIGHEST)
    wpart = jnp.einsum("kprc,kprd->kcd", gathered.astype(jnp.float32), picked_live.astype(jnp.float32))
    wpart = lax.optimization_barrier(wpart.astype(jnp.bfloat16)).astype(jnp.float32)
    return outputs, table_grad[:blocks], table_grad[blocks:].reshape((8, -1, rows_per, width)), wpart


def reference(features, kernel_weight, channel_bias, send_list, rule_source, rule_target, live_counts, out_grad):
    grid_x = features.shape[0]
    grid_y = features.shape[1]
    boundary = jax.vmap(jax.vmap(lambda block_feats, chosen: block_feats[chosen]))(features, send_list)
    padded = jnp.pad(boundary, ((1, 1), (1, 1), (0, 0), (0, 0), (0, 0)))
    directions = [(shift_x, shift_y) for shift_x in (-1, 0, 1) for shift_y in (-1, 0, 1) if not (shift_x == 0 and shift_y == 0)]
    neighbour = jnp.stack([padded[1 + shift_x:1 + shift_x + grid_x, 1 + shift_y:1 + shift_y + grid_y] for shift_x, shift_y in directions], axis=2)
    devices = grid_x * grid_y

    def flatten(array):
        return array.reshape((devices,) + array.shape[2:])

    def one_device(carry, items):
        outs, own, halo_part, wpart = device_pass(items[0], items[1], kernel_weight, channel_bias, items[2], items[3], items[4], items[5])
        return carry + wpart, (outs, own, halo_part)

    start_grad = jnp.zeros(kernel_weight.shape, jnp.float32)
    weight_sum, (outputs, own_grad, halo_grad) = lax.scan(one_device, start_grad, (flatten(features), flatten(neighbour), flatten(rule_source), flatten(rule_target), flatten(live_counts), flatten(out_grad)))
    halo_grad = halo_grad.reshape((grid_x, grid_y) + halo_grad.shape[1:])
    returned = jnp.zeros(boundary.shape, jnp.float32)
    for direction_index, (shift_x, shift_y) in enumerate(directions):
        padded_grad = jnp.pad(halo_grad[:, :, direction_index], ((1, 1), (1, 1), (0, 0), (0, 0), (0, 0)))
        returned = returned + padded_grad[1 - shift_x:1 - shift_x + grid_x, 1 - shift_y:1 - shift_y + grid_y]
    blocks = features.shape[2]
    placement = (send_list[:, :, None, :] == jnp.arange(blocks, dtype=jnp.int32)[:, None]).astype(jnp.float32)
    feat_grad = own_grad.reshape(features.shape) + jnp.einsum("xybh,xyhrc->xybrc", placement, returned, precision=lax.Precision.HIGHEST)
    weight_grad = weight_sum * (1.0 / features.shape[3])
    return outputs.reshape(features.shape), feat_grad.astype(jnp.bfloat16), weight_grad
```

```python
import functools

import jax
import jax.numpy as jnp
from jax import lax
from jax.experimental import pallas as pl
from jax.experimental.pallas import tpu as pltpu
from jax.sharding import PartitionSpec as P

MESH = pl.DeviceIdType.MESH
VMEM = pltpu.VMEM
SMEM = pltpu.SMEM
LANES = 128
TILE = 16
KINDS = (2, 0, 1, 3, 0, 1, 0, 1, 0)
WAVES = (0,) * 9
STAGGER = 1
HALO_AT = 4
UNROLL = 9
VMEM_BYTES = 28 * 1024 * 1024
EXCHANGE_BYTES = 28 * 1024 * 1024

LINE_KINDS = (
    'Axrri', 'Ayrri', 'Axrri', 'Axrri', 'Byr', 'Axrri', 'Ayrri', 'Axrri',
    'Byr', 'Axrri', 'Axrri', 'Axrri', 'Byr', 'Ayrri', 'Ayrri', 'Axrri',
    'Axrri', 'Ayrri', 'Bxr', 'Byr', 'Axrri', 'Ayrri', 'Ayrri', 'Ayrri',
    'Ayrri', 'Byr', 'Ayrri',
)
LINE_ORDERS = (
(
    0, 10, 20, 60, 30, 130, 50, 140, 70, 170, 90, 210, 100, 1, 41, 220,
    110, 230, 150, 81, 21, 160, 240, 200, 31, 2, 121, 260, 11, 61, 51, 131,
    71, 181, 141, 91, 22, 171, 101, 211, 111, 221, 151, 32, 191, 231, 161, 241,
    201, 12, 261, 42, 62, 52, 270, 82, 132, 72, 251, 122, 142, 92, 172, 102,
    3, 212, 112, 23, 222, 152, 232, 33, 162, 242, 202, 13, 262, 63, 53, 73,
    192, 93, 252, 4, 103, 24, 113, 34, 133, 143, 14, 43, 153, 64, 83, 163,
    54, 123, 173, 74, 182, 203, 94, 193, 213, 104, 253, 223, 114, 233, 134, 243,
    271, 144, 263, 44, 154, 84, 164, 6, 124, 174, 183, 204, 194, 214, 254, 224,
    234, 244, 264, 45, 16, 26, 85, 7, 66, 36, 125, 136, 184, 56, 195, 146,
    76, 255, 176, 17, 96, 27, 216, 46, 67, 106, 37, 226, 86, 185, 137, 116,
    236, 126, 57, 147, 156, 246, 77, 177, 166, 266, 196, 97, 217, 206, 256, 107,
    227, 186, 117, 237, 157, 247, 167, 267, 207,
),
(
    0, 10, 40, 20, 60, 30, 130, 80, 50, 140, 70, 170, 120, 90, 210, 100,
    1, 180, 220, 110, 230, 150, 190, 21, 160, 240, 200, 31, 250, 260, 11, 61,
    51, 131, 71, 141, 2, 91, 171, 22, 101, 211, 111, 221, 151, 32, 231, 161,
    241, 201, 12, 261, 270, 62, 52, 72, 92, 102, 112, 132, 142, 152, 162, 172,
    202, 212, 222, 232, 242, 262, 5, 25, 35, 271, 15, 65, 55, 75, 95, 6,
    105, 115, 26, 135, 16, 145, 36, 155, 165, 175, 205, 215, 66, 7, 225, 235,
    27, 245, 136, 265, 17, 56, 146, 46, 37, 76, 176, 86, 96, 216, 126, 67,
    106, 226, 196, 137, 116, 236, 256, 57, 147, 156, 246, 47, 77, 177, 166, 266,
    87, 97, 217, 206, 127, 107, 227, 186, 117, 237, 197, 157, 247, 257, 167, 267,
    187, 207,
),
)


def greet_neighbours(barrier, me_x, me_y, nx, ny):
    total = 0
    for sx, sy in ((-1, 0), (1, 0), (0, -1), (0, 1)):
        x, y = me_x + sx, me_y + sy
        there = (x >= 0) & (x < nx) & (y >= 0) & (y < ny)

        @pl.when(there)
        def _():
            pl.semaphore_signal(barrier, inc=1, device_id=(x, y), device_id_type=MESH)

        total = total + there.astype(jnp.int32)
    return total


def greet_column(barrier, me_x, me_y, ny):
    for step in range(1, ny):
        pl.semaphore_signal(
            barrier, inc=1, device_id=(me_x, lax.rem(me_y + step, ny)), device_id_type=MESH
        )
    return ny - 1


def exists(index, count):
    return (index >= 0) & (index < count)


def exchange_kernel(
    nx, ny, send_ref, feats_ref, weight_ref, halo_ref, full_ref, feats, lsem, xsend, xrecv, hsend, hrecv, wsend, wrecv
):
    me_x, me_y = lax.axis_index("gx"), lax.axis_index("gy")
    barrier = pltpu.get_barrier_semaphore()
    expected = greet_neighbours(barrier, me_x, me_y, nx, ny) + greet_column(
        barrier, me_x, me_y, ny
    )
    load = pltpu.make_async_copy(feats_ref, feats, lsem.at[0])
    load.start()
    keep = pltpu.make_async_copy(weight_ref, full_ref.at[:, me_y], lsem.at[1])
    keep.start()
    load.wait()
    for s in range(halo_ref.shape[1]):
        halo_ref[4, s] = feats[send_ref[s]]
    pl.semaphore_wait(barrier, expected)

    def x_copy(a, device_x):
        return pltpu.make_async_remote_copy(
            src_ref=halo_ref.at[4],
            dst_ref=halo_ref.at[3 * a + 1],
            send_sem=xsend.at[a // 2],
            recv_sem=xrecv.at[a // 2],
            device_id=(device_x, me_y),
            device_id_type=MESH,
        )

    def y_copy(a, b, device_y):
        return pltpu.make_async_remote_copy(
            src_ref=halo_ref.at[3 * a + 1],
            dst_ref=halo_ref.at[3 * a + b],
            send_sem=hsend.at[a, b // 2],
            recv_sem=hrecv.at[a, b // 2],
            device_id=(me_x, device_y),
            device_id_type=MESH,
        )

    def weight_copy(step, owner):
        return pltpu.make_async_remote_copy(
            src_ref=weight_ref,
            dst_ref=full_ref.at[:, owner],
            send_sem=wsend.at[step],
            recv_sem=wrecv.at[step],
            device_id=(me_x, lax.rem(me_y + step, ny)),
            device_id_type=MESH,
        )

    def to_column(a, act):
        for b in (0, 2):
            target = me_y + 1 - b

            @pl.when(exists(target, ny))
            def _():
                act(y_copy(a, b, target))

    for a in (0, 2):
        target = me_x + 1 - a

        @pl.when(exists(target, nx))
        def _():
            x_copy(a, target).start()

    to_column(1, lambda copy: copy.start())
    for step in range(1, ny):
        weight_copy(step, me_y).start()
    blank = jnp.zeros(halo_ref.shape[1:], halo_ref.dtype)
    for a in (0, 2):
        here = exists(me_x + a - 1, nx)

        @pl.when(jnp.logical_not(here))
        def _():
            halo_ref[3 * a + 1] = blank

        @pl.when(here)
        def _():
            x_copy(a, me_x + a - 1).wait_recv()
            to_column(a, lambda copy: copy.start())

    for a in range(3):
        for b in (0, 2):
            there = exists(me_x + a - 1, nx) & exists(me_y + b - 1, ny)

            @pl.when(jnp.logical_not(there))
            def _():
                halo_ref[3 * a + b] = blank

            @pl.when(there)
            def _():
                y_copy(a, b, me_y + b - 1).wait_recv()

        @pl.when(exists(me_x + a - 1, nx))
        def _():
            to_column(a, lambda copy: copy.wait_send())

    for a in (0, 2):
        target = me_x + 1 - a

        @pl.when(exists(target, nx))
        def _():
            x_copy(a, target).wait_send()

    for step in range(1, ny):
        weight_copy(step, lax.rem(me_y - step + ny, ny)).wait_recv()
        weight_copy(step, me_y).wait_send()
    keep.wait()


def compute_kernel(
    source_ref,
    target_ref,
    count_ref,
    feats_ref,
    halo_ref,
    weight_ref,
    bias_ref,
    cot_ref,
    out_ref,
    own_ref,
    borrowed_ref,
    wpart_ref,
    table,
    turned,
    pre,
    dpre,
    grad,
):
    blocks, rows, width = feats_ref.shape
    slots = source_ref.shape[0]
    kvol = weight_ref.shape[0]
    total_blocks = grad.shape[0] - 1
    shared_count = halo_ref.shape[1]
    ny, tiles = wpart_ref.shape[:2]
    share = width // ny
    share_tiles = share // TILE
    places = [(b, feats_ref.at[b]) for b in range(blocks)]
    at = blocks
    for d in range(9):
        if d != 4:
            for s in range(shared_count):
                places.append((at, halo_ref.at[d, s]))
                at += 1
    for t, ref in places:
        value = ref[...]
        table[t] = value
        turned[t] = value.T
    for b in range(blocks):
        pre[b] = jnp.broadcast_to(bias_ref[...], (rows, width))
    for t in range(total_blocks):
        grad[t] = jnp.zeros((rows, width), jnp.float32)
    pre[blocks] = jnp.zeros((rows, width), jnp.float32)
    grad[total_blocks] = jnp.zeros((rows, width), jnp.float32)
    dpre[blocks] = jnp.zeros((rows, width), dpre.dtype)

    def rules(k):
        live = count_ref[k]
        sources = [source_ref[q, k] for q in range(slots)]
        targets = [target_ref[q, k] for q in range(slots)]
        reads = [jnp.where(q < live, v, 0) for q, v in enumerate(sources)]
        spread = [jnp.where(q < live, v, total_blocks) for q, v in enumerate(sources)]
        targets = [jnp.where(q < live, v, blocks) for q, v in enumerate(targets)]
        return reads, spread, targets

    def forward(k, carry):
        reads, _, targets = rules(k)
        taken = jnp.concatenate([table[s] for s in reads], axis=0)
        made = jnp.dot(taken, weight_ref[k], preferred_element_type=jnp.float32)
        for q, target in enumerate(targets):
            pre[target] += made[q * rows : (q + 1) * rows]
        return carry

    lax.fori_loop(0, kvol, forward, 0, unroll=UNROLL)

    def activate(b, carry):
        value = pre[b]
        sig = jax.nn.sigmoid(value)
        out_ref[b] = (value * sig).astype(out_ref.dtype)
        dpre[b] = (cot_ref[b].astype(jnp.float32) * sig * (1.0 + value * (1.0 - sig))).astype(
            dpre.dtype
        )
        return carry

    lax.fori_loop(0, blocks, activate, 0)

    line = len(wpart_ref.shape) == 5
    filled = 2 * kvol * share_tiles
    if not line and filled < tiles:
        for y in range(ny):
            wpart_ref[y, filled:] = jnp.zeros((tiles - filled, TILE, LANES), wpart_ref.dtype)

    def backward(k, carry):
        reads, spread, targets = rules(k)
        pulled = jnp.concatenate([dpre[t] for t in targets], axis=0)
        taken = jnp.concatenate([turned[s] for s in reads], axis=1)
        part = jnp.dot(taken, pulled, preferred_element_type=jnp.float32).astype(wpart_ref.dtype)
        if line:
            for y in range(ny):
                wpart_ref[y, k] = part[y * share : (y + 1) * share].reshape(wpart_ref.shape[2:])
        else:
            for y in range(ny):
                for h in range(width // LANES):
                    piece = part[y * share : (y + 1) * share, h * LANES : (h + 1) * LANES]
                    wpart_ref[y, pl.ds((h * kvol + k) * share_tiles, share_tiles)] = piece.reshape(
                        share_tiles, TILE, LANES
                    )
        back = lax.dot_general(
            pulled, weight_ref[k], (((1,), (1,)), ((), ())), preferred_element_type=jnp.float32
        )
        for q, source in enumerate(spread):
            grad[source] += back[q * rows : (q + 1) * rows]
        return carry

    lax.fori_loop(0, kvol, backward, 0, unroll=UNROLL)
    for b in range(blocks):
        own_ref[b] = grad[b]
    at = blocks
    for d in range(9):
        for s in range(shared_count):
            if d == 4:
                borrowed_ref[d, s] = jnp.zeros((rows, width), borrowed_ref.dtype)
            else:
                borrowed_ref[d, s] = grad[at].astype(borrowed_ref.dtype)
                at += 1


def reduce_kernel(
    nx,
    ny,
    wpart_ref,
    borrowed_ref,
    sum_ref,
    returned_ref,
    work,
    yland,
    xland,
    side_land,
    column,
    x_land,
    ysend,
    yrecv,
    rsend,
    rrecv,
    gsend,
    grecv,
    hsend,
    hrecv,
    bsend,
    brecv,
):
    me_x, me_y = lax.axis_index("gx"), lax.axis_index("gy")
    groups = work.shape[0]
    steps = nx.bit_length() - 1
    bits = [lax.rem(me_x // (1 << b), 2) for b in range(steps)]
    partners = [me_x + (1 - 2 * bits[b]) * (1 << b) for b in range(steps)]

    barrier = pltpu.get_barrier_semaphore()
    expected = greet_neighbours(barrier, me_x, me_y, nx, ny) + greet_column(
        barrier, me_x, me_y, ny
    )
    for b in range(steps):
        pl.semaphore_signal(barrier, inc=1, device_id=(partners[b], me_y), device_id_type=MESH)
    pl.semaphore_wait(barrier, expected + steps)

    def side_copy(a, b):
        return pltpu.make_async_remote_copy(
            src_ref=borrowed_ref.at[3 * a + b],
            dst_ref=side_land.at[a, b // 2],
            send_sem=hsend.at[a, b // 2],
            recv_sem=hrecv.at[a, b // 2],
            device_id=(me_x, me_y + b - 1),
            device_id_type=MESH,
        )

    def back_copy(a):
        return pltpu.make_async_remote_copy(
            src_ref=column.at[a // 2],
            dst_ref=x_land.at[a // 2],
            send_sem=bsend.at[a // 2],
            recv_sem=brecv.at[a // 2],
            device_id=(me_x + a - 1, me_y),
            device_id_type=MESH,
        )

    def sides(act, sign):
        for a in range(3):
            for b in (0, 2):

                @pl.when(exists(me_x + a - 1, nx) & exists(me_y + sign * (b - 1), ny))
                def _():
                    act(a, b)

    def column_copy(step, g):
        other = lax.rem(me_y + step, ny)
        return pltpu.make_async_remote_copy(
            src_ref=wpart_ref.at[other, g],
            dst_ref=yland.at[step - 1, g],
            send_sem=ysend.at[step - 1, g],
            recv_sem=yrecv.at[step - 1, g],
            device_id=(me_x, other),
            device_id_type=MESH,
        )

    late = list(range(2, steps))
    kinds = [[0, 1] + late, [1, 0] + late, late + [0, 1], late + [1, 0]]
    orders = [kinds[kind] for kind in KINDS]
    starts = []
    for g in range(groups):
        at = [0]
        for s in range(steps):
            at.append(at[-1] + bits[orders[g][s]] * (nx >> (s + 1)))
        starts.append(at)

    def scatter_copy(g, s):
        half = nx >> (s + 1)
        bit = bits[orders[g][s]]
        away = starts[g][s] + (1 - bit) * half
        return pltpu.make_async_remote_copy(
            src_ref=work.at[g, pl.ds(away, half)],
            dst_ref=xland.at[g, pl.ds(nx - 2 * half, half)],
            send_sem=rsend.at[s, g],
            recv_sem=rrecv.at[s, g],
            device_id=(partners[orders[g][s]], me_y),
            device_id_type=MESH,
        )

    def gather_copy(g, s, landing):
        half = nx >> (s + 1)
        bit = bits[orders[g][s]]
        mine = starts[g][s + 1]
        place = starts[g][s] + (1 - bit) * half if landing else mine
        return pltpu.make_async_remote_copy(
            src_ref=sum_ref.at[g, pl.ds(mine, half)],
            dst_ref=sum_ref.at[g, pl.ds(place, half)],
            send_sem=gsend.at[s, g],
            recv_sem=grecv.at[s, g],
            device_id=(partners[orders[g][s]], me_y),
            device_id_type=MESH,
        )

    for g in range(groups):
        for step in range(1, ny):
            column_copy(step, g).start()
    sides(lambda a, b: side_copy(a, b).start(), 1)

    def begin(g):
        value = wpart_ref[me_y, g].astype(jnp.float32)
        for step in range(1, ny):
            column_copy(step, g).wait_recv()
            value = value + yland[step - 1, g].astype(jnp.float32)
        work[g] = value.astype(work.dtype)
        scatter_copy(g, 0).start()

    def scatter(g, s):
        half = nx >> (s + 1)
        scatter_copy(g, s).wait_recv()
        keep = pl.ds(starts[g][s + 1], half)
        value = work[g, keep].astype(jnp.float32) + xland[g, pl.ds(nx - 2 * half, half)].astype(
            jnp.float32
        )
        if s < steps - 1:
            work[g, keep] = value.astype(work.dtype)
            scatter_copy(g, s + 1).start()
        else:
            sum_ref[g, keep] = value.astype(sum_ref.dtype)
            gather_copy(g, s, False).start()

    def gather(g, s):
        gather_copy(g, s, True).wait_recv()
        if s > 0:
            gather_copy(g, s - 1, False).start()

    events = []
    for g in range(groups):
        events.append((WAVES[g] * STAGGER, g, functools.partial(begin, g)))
        for s in range(steps):
            events.append((WAVES[g] * STAGGER + s + 1, g, functools.partial(scatter, g, s)))
            events.append(
                (WAVES[g] * STAGGER + 2 * steps - s, g, functools.partial(gather, g, s))
            )
    events.sort(key=lambda event: event[:2])
    first = [event[2] for event in events if event[0] < HALO_AT]
    rest = [event[2] for event in events if event[0] >= HALO_AT]
    for event in first:
        event()

    returned_ref[...] = jnp.zeros(returned_ref.shape, jnp.float32)
    for b in (0, 2):

        @pl.when(exists(me_y + 1 - b, ny))
        def _():
            side_copy(1, b).wait_recv()
            returned_ref[...] += side_land[1, b // 2].astype(jnp.float32)

    for a in (0, 2):

        @pl.when(exists(me_x + a - 1, nx))
        def _():
            for b in (0, 2):
                missing = jnp.logical_not(exists(me_y + 1 - b, ny))

                @pl.when(missing)
                def _():
                    side_land[a, b // 2] = jnp.zeros(side_land.shape[2:], side_land.dtype)

                @pl.when(jnp.logical_not(missing))
                def _():
                    side_copy(a, b).wait_recv()

            column[a // 2] = (
                borrowed_ref[3 * a + 1].astype(jnp.float32)
                + side_land[a, 0].astype(jnp.float32)
                + side_land[a, 1].astype(jnp.float32)
            ).astype(column.dtype)
            back_copy(a).start()

    for event in rest:
        event()

    for a in (0, 2):

        @pl.when(exists(me_x + 1 - a, nx))
        def _():
            back_copy(a).wait_recv()
            returned_ref[...] += x_land[a // 2].astype(jnp.float32)

    for g in range(groups):
        for step in range(1, ny):
            column_copy(step, g).wait_send()
        for s in range(steps):
            scatter_copy(g, s).wait_send()
            gather_copy(g, s, False).wait_send()
    sides(lambda a, b: side_copy(a, b).wait_send(), 1)
    for a in (0, 2):

        @pl.when(exists(me_x + a - 1, nx))
        def _():
            back_copy(a).wait_send()


def line_kernel(
    nx,
    ny,
    wpart_ref,
    borrowed_ref,
    sum_ref,
    returned_ref,
    work,
    yland,
    full_land,
    half_land,
    land,
    side_land,
    column,
    x_land,
    ysend,
    yrecv,
    csend,
    crecv,
    hsend,
    hrecv,
    bsend,
    brecv,
):
    me_x, me_y = lax.axis_index("gx"), lax.axis_index("gy")
    kvol = work.shape[0]
    f32 = jnp.float32
    bit_x, bit_y, z = lax.rem(me_x, 2), lax.rem(me_x // 2, 2), me_x // 4
    low, high = lax.rem(z, 2), z // 2
    beside = {"x": me_x + 1 - 2 * bit_x, "y": me_x + 2 - 4 * bit_y}
    across = beside["y"] + 1 - 2 * bit_x
    inner = exists(z - 1, 2)
    near = jnp.where(inner, me_x - 4 + 8 * high, me_x + 4 - 8 * high)
    middle = me_x + 4 - 8 * high
    peers = (3 - z, z + 2 - 4 * high, z + 1 - 2 * low)

    barrier = pltpu.get_barrier_semaphore()
    expected = greet_neighbours(barrier, me_x, me_y, nx, ny) + greet_column(
        barrier, me_x, me_y, ny
    )
    greeted = [beside["x"], beside["y"], across] + [me_x + 4 * (peer - z) for peer in peers]
    for device in greeted:
        pl.semaphore_signal(barrier, inc=1, device_id=(device, me_y), device_id_type=MESH)
    pl.semaphore_wait(barrier, expected + len(greeted))

    def side_copy(a, b):
        return pltpu.make_async_remote_copy(
            src_ref=borrowed_ref.at[3 * a + b],
            dst_ref=side_land.at[a, b // 2],
            send_sem=hsend.at[a, b // 2],
            recv_sem=hrecv.at[a, b // 2],
            device_id=(me_x, me_y + b - 1),
            device_id_type=MESH,
        )

    def back_copy(a):
        return pltpu.make_async_remote_copy(
            src_ref=column.at[a // 2],
            dst_ref=x_land.at[a // 2],
            send_sem=bsend.at[a // 2],
            recv_sem=brecv.at[a // 2],
            device_id=(me_x + a - 1, me_y),
            device_id_type=MESH,
        )

    def sides(act, sign):
        for a in range(3):
            for b in (0, 2):

                @pl.when(exists(me_x + a - 1, nx) & exists(me_y + sign * (b - 1), ny))
                def _():
                    act(a, b)

    def column_copy(step, g):
        other = lax.rem(me_y + step, ny)
        return pltpu.make_async_remote_copy(
            src_ref=wpart_ref.at[other, g],
            dst_ref=yland.at[step - 1, g],
            send_sem=ysend.at[step - 1, g],
            recv_sem=yrecv.at[step - 1, g],
            device_id=(me_x, other),
            device_id_type=MESH,
        )

    for g in range(kvol):
        for step in range(1, ny):
            column_copy(step, g).start()
    sides(lambda a, b: side_copy(a, b).start(), 1)

    def give_back():
        returned_ref[...] = jnp.zeros(returned_ref.shape, f32)
        for b in (0, 2):

            @pl.when(exists(me_y + 1 - b, ny))
            def _():
                side_copy(1, b).wait_recv()
                returned_ref[...] += side_land[1, b // 2].astype(f32)

        for a in (0, 2):

            @pl.when(exists(me_x + a - 1, nx))
            def _():
                for b in (0, 2):
                    missing = jnp.logical_not(exists(me_y + 1 - b, ny))

                    @pl.when(missing)
                    def _():
                        side_land[a, b // 2] = jnp.zeros(side_land.shape[2:], side_land.dtype)

                    @pl.when(jnp.logical_not(missing))
                    def _():
                        side_copy(a, b).wait_recv()

                column[a // 2] = (
                    borrowed_ref[3 * a + 1].astype(f32)
                    + side_land[a, 0].astype(f32)
                    + side_land[a, 1].astype(f32)
                ).astype(column.dtype)
                back_copy(a).start()

    def take_back():
        for a in (0, 2):

            @pl.when(exists(me_x + 1 - a, nx))
            def _():
                back_copy(a).wait_recv()
                returned_ref[...] += x_land[a // 2].astype(f32)

    def own_sum(g):
        value = wpart_ref[me_y, g].astype(f32)
        for step in range(1, ny):
            column_copy(step, g).wait_recv()
            value = value + yland[step - 1, g].astype(f32)
        return value

    def program(order, inside):
        sent = []

        def copy(g, src, dst, leave, arrive, device):
            return pltpu.make_async_remote_copy(
                src_ref=src,
                dst_ref=dst,
                send_sem=csend.at[leave, g],
                recv_sem=crecv.at[arrive, g],
                device_id=(device, me_y),
                device_id_type=MESH,
            )

        def send(g, src, dst, leave, arrive, device):
            made = copy(g, src, dst, leave, arrive, device)
            made.start()
            sent.append(made)

        def recv(g, dst, arrive):
            copy(g, dst, dst, 0, arrive, beside["x"]).wait_recv()

        def along(g, k):
            first, spread, gather, cross = LINE_KINDS[g][1:]
            second = "y" if first == "x" else "x"
            bits = {"x": bit_x, "y": bit_y}
            hb, qb = bits[first], bits[second]
            mine = 2 * hb + qb
            beside_mine, over, corner = 2 * hb + 1 - qb, 2 - 2 * hb + qb, 3 - mine
            kept, gone = pl.ds(2 * hb, 2), pl.ds(2 - 2 * hb, 2)
            total, ours = sum_ref.at[g], work.at[g]

            def spread_quarters():
                send(g, total.at[mine], total.at[mine], 9, 9, across)
                send(g, total.at[mine], total.at[mine], 8, 8, beside[first])
                send(g, total.at[mine], total.at[mine], 7, 7, beside[second])

            def gather_start():
                if gather == "d":
                    spread_quarters()
                else:
                    send(g, total.at[mine], total.at[mine], 7, 7, beside[second])

            if k == 0:
                work[g] = own_sum(g).astype(work.dtype)
                if spread == "d":
                    send(g, ours.at[corner], land.at[2, g], 2, 2, across)
                    send(g, ours.at[over], land.at[1, g], 1, 1, beside[first])
                    send(g, ours.at[beside_mine], land.at[0, g], 0, 0, beside[second])
                else:
                    send(g, ours.at[gone], half_land.at[g], 1, 1, beside[first])
            elif k == 1:
                if spread == "r":
                    recv(g, half_land.at[g], 1)
                    work[g, kept] = (
                        work[g, kept].astype(f32) + half_land[g].astype(f32)
                    ).astype(work.dtype)
                    send(g, ours.at[beside_mine], land.at[0, g], 0, 0, beside[second])
            elif k == 2:
                value = work[g, mine].astype(f32)
                for slot in range(3 if spread == "d" else 1):
                    recv(g, land.at[slot, g], slot)
                    value = value + land[slot, g].astype(f32)
                work[g, mine] = value.astype(work.dtype)
                if cross == "x":
                    land[3 + z, g] = value.astype(work.dtype)
                    for at, peer in enumerate(peers):
                        send(g, ours.at[mine], land.at[3 + z, g], 3 + at, 3 + z, me_x + 4 * (peer - z))
                elif not inside:
                    send(g, ours.at[mine], land.at[3, g], 3, 3, near)
            elif k == 3:
                if cross == "i" and inside:
                    recv(g, land.at[3, g], 3)
                    work[g, mine] = (
                        work[g, mine].astype(f32) + land[3, g].astype(f32)
                    ).astype(work.dtype)
                    send(g, ours.at[mine], land.at[4, g], 4, 4, middle)
            elif k == 4:
                if cross == "i" and inside:
                    recv(g, land.at[4, g], 4)
                    sum_ref[g, mine] = (
                        work[g, mine].astype(f32) + land[4, g].astype(f32)
                    ).astype(sum_ref.dtype)
                    send(g, total.at[mine], total.at[mine], 5, 5, near)
                    gather_start()
            elif k == 5:
                if cross == "x":
                    for peer in peers:
                        recv(g, land.at[3 + peer, g], 3 + peer)
                    sum_ref[g, mine] = (
                        (land[3, g].astype(f32) + land[4, g].astype(f32))
                        + (land[5, g].astype(f32) + land[6, g].astype(f32))
                    ).astype(sum_ref.dtype)
                    gather_start()
                elif not inside:
                    recv(g, total.at[mine], 5)
                    gather_start()
            elif k == 6:
                if gather == "r":
                    recv(g, total.at[beside_mine], 7)
                    send(g, total.at[kept], total.at[kept], 8, 8, beside[first])
            elif k == 7:
                if gather == "r":
                    recv(g, total.at[gone], 8)
                else:
                    recv(g, total.at[beside_mine], 7)
                    recv(g, total.at[over], 8)
                    recv(g, total.at[corner], 9)

        def fold(g, k):
            first = LINE_KINDS[g][1]
            second = "y" if first == "x" else "x"
            bits = {"x": bit_x, "y": bit_y}
            hb, qb = high, bits[first]
            mine, other = 2 * hb + qb, 2 * hb + 1 - qb
            kept, gone = pl.ds(2 * hb, 2), pl.ds(2 - 2 * hb, 2)
            total, ours = sum_ref.at[g], work.at[g]
            if not inside:
                if k == 0:
                    work[g] = own_sum(g).astype(work.dtype)
                    send(g, ours, full_land.at[g], 3, 3, near)
                elif k == 6:
                    recv(g, total.at[kept], 6)
                elif k == 7:
                    recv(g, total.at[gone], 8)
            elif k == 1:
                value = own_sum(g)
                recv(g, full_land.at[g], 3)
                work[g] = (value + full_land[g].astype(f32)).astype(work.dtype)
                send(g, ours.at[gone], half_land.at[g], 4, 4, middle)
            elif k == 2:
                recv(g, half_land.at[g], 4)
                work[g, kept] = (
                    work[g, kept].astype(f32) + half_land[g].astype(f32)
                ).astype(work.dtype)
                send(g, ours.at[other], land.at[0, g], 0, 0, beside[first])
            elif k == 3:
                recv(g, land.at[0, g], 0)
                work[g, mine] = (
                    work[g, mine].astype(f32) + land[0, g].astype(f32)
                ).astype(work.dtype)
                send(g, ours.at[mine], land.at[1, g], 1, 1, beside[second])
            elif k == 4:
                recv(g, land.at[1, g], 1)
                sum_ref[g, mine] = (
                    work[g, mine].astype(f32) + land[1, g].astype(f32)
                ).astype(sum_ref.dtype)
                send(g, total.at[mine], total.at[mine], 7, 7, beside[first])
            elif k == 5:
                recv(g, total.at[other], 7)
                send(g, total.at[kept], total.at[kept], 5, 5, middle)
                send(g, total.at[kept], total.at[kept], 6, 6, near)
            elif k == 6:
                recv(g, total.at[gone], 5)
                send(g, total.at[gone], total.at[gone], 8, 8, near)

        for event in order:
            g, k = divmod(event, 10)
            if g == kvol:
                (give_back, take_back)[k]()
            elif LINE_KINDS[g][0] == "B":
                fold(g, k)
            else:
                along(g, k)
        for made in sent:
            made.wait_send()

    @pl.when(inner)
    def _():
        program(LINE_ORDERS[0], True)

    @pl.when(jnp.logical_not(inner))
    def _():
        program(LINE_ORDERS[1], False)

    for g in range(kvol):
        for step in range(1, ny):
            column_copy(step, g).wait_send()
    sides(lambda a, b: side_copy(a, b).wait_send(), 1)
    for a in (0, 2):

        @pl.when(exists(me_x + a - 1, nx))
        def _():
            back_copy(a).wait_send()


def finish_kernel(
    send_ref, total_ref, own_ref, returned_ref, weight_ref, feat_ref, wide, feats, wsem, fsem
):
    chunks = wsem.shape[0]
    kvol, share, width = wide.shape
    per = kvol // chunks
    blocks, rows = own_ref.shape[:2]
    copies = []
    for c in range(chunks):
        at = pl.ds(c * per, per)
        if len(total_ref.shape) == 3:
            wide[at] = total_ref[at].astype(jnp.float32) * (1.0 / rows)
        else:
            for h in range(width // LANES):
                wide[at, :, h * LANES : (h + 1) * LANES] = total_ref[h, at].reshape(
                    per, share, LANES
                ).astype(jnp.float32) * (1.0 / rows)
        copy = pltpu.make_async_copy(wide.at[at], weight_ref.at[at], wsem.at[c])
        copy.start()
        copies.append(copy)
    for b in range(blocks):
        value = own_ref[b]
        for s in range(returned_ref.shape[0]):
            value = value + jnp.where(send_ref[s] == b, returned_ref[s], 0.0)
        feats[b] = value.astype(feats.dtype)
        copy = pltpu.make_async_copy(feats.at[b], feat_ref.at[b], fsem.at[b])
        copy.start()
        copies.append(copy)
    for copy in copies:
        copy.wait()


def on_device(
    nx,
    ny,
    features,
    kernel_weight,
    channel_bias,
    send_list,
    rule_source,
    rule_target,
    live_counts,
    out_grad,
):
    feats = features[0, 0]
    blocks, rows, width = feats.shape
    shared = send_list[0, 0]
    shared_count = shared.shape[0]
    kvol, slots = rule_source.shape[2:]
    share = kernel_weight.shape[1]
    bf16, f32 = jnp.bfloat16, jnp.float32
    shape = jax.ShapeDtypeStruct
    vmem = pl.BlockSpec(memory_space=VMEM)
    smem = pl.BlockSpec(memory_space=SMEM)
    hbm = pl.BlockSpec(memory_space=pltpu.HBM)
    dma = pltpu.SemaphoreType.DMA
    squares = 9

    halo, full = pl.pallas_call(
        functools.partial(exchange_kernel, nx, ny),
        out_shape=(
            shape((squares, shared_count, rows, width), bf16),
            shape((kvol, ny, share, width), bf16),
        ),
        in_specs=[smem, hbm, hbm],
        out_specs=(vmem, vmem),
        scratch_shapes=[
            VMEM((blocks, rows, width), bf16),
            dma((2,)),
            dma((2,)),
            dma((2,)),
            dma((3, 2)),
            dma((3, 2)),
            dma((ny,)),
            dma((ny,)),
        ],
        compiler_params=pltpu.CompilerParams(
            collective_id=0, has_side_effects=True, vmem_limit_bytes=EXCHANGE_BYTES
        ),
    )(shared, feats, kernel_weight)

    total_blocks = blocks + (squares - 1) * shared_count
    used = (width // LANES) * kvol * (share // TILE)
    groups = len(KINDS)
    unit = groups * nx
    tiles = -(-used // unit) * unit
    depth = tiles // unit
    line = nx == 16 and kvol == len(LINE_KINDS)
    quarters = (4, share // 4, width)
    outputs, own, borrowed, wpart = pl.pallas_call(
        compute_kernel,
        out_shape=(
            shape((blocks, rows, width), bf16),
            shape((blocks, rows, width), f32),
            shape((squares, shared_count, rows, width), bf16),
            shape((ny, kvol) + quarters if line else (ny, tiles, TILE, LANES), bf16),
        ),
        in_specs=[smem, smem, smem, vmem, vmem, vmem, vmem, vmem],
        out_specs=(vmem, vmem, vmem, vmem),
        scratch_shapes=[
            VMEM((total_blocks, rows, width), bf16),
            VMEM((total_blocks, width, rows), bf16),
            VMEM((blocks + 1, rows, width), f32),
            VMEM((blocks + 1, rows, width), bf16),
            VMEM((total_blocks + 1, rows, width), f32),
        ],
        compiler_params=pltpu.CompilerParams(vmem_limit_bytes=VMEM_BYTES),
    )(
        rule_source[0, 0].T,
        rule_target[0, 0].T,
        live_counts.reshape(-1),
        feats,
        halo,
        full.reshape(kvol, width, width),
        channel_bias.reshape(1, width),
        out_grad[0, 0],
    )

    steps = nx.bit_length() - 1
    block = (depth, TILE, LANES)
    boundary = (shared_count, rows, width)
    if line:
        total, returned = pl.pallas_call(
            functools.partial(line_kernel, nx, ny),
            out_shape=(shape((kvol,) + quarters, bf16), shape(boundary, f32)),
            in_specs=[vmem, vmem],
            out_specs=(vmem, vmem),
            scratch_shapes=[
                VMEM((kvol,) + quarters, bf16),
                VMEM((max(ny - 1, 1), kvol) + quarters, bf16),
                VMEM((kvol,) + quarters, bf16),
                VMEM((kvol, 2) + quarters[1:], bf16),
                VMEM((7, kvol) + quarters[1:], bf16),
                VMEM((3, 2) + boundary, bf16),
                VMEM((2,) + boundary, bf16),
                VMEM((2,) + boundary, bf16),
                dma((max(ny - 1, 1), kvol)),
                dma((max(ny - 1, 1), kvol)),
                dma((10, kvol)),
                dma((10, kvol)),
                dma((3, 2)),
                dma((3, 2)),
                dma((2,)),
                dma((2,)),
            ],
            compiler_params=pltpu.CompilerParams(
                collective_id=1, has_side_effects=True, vmem_limit_bytes=VMEM_BYTES
            ),
        )(wpart, borrowed)
        total = total.reshape(kvol, share, width)
    else:
        total, returned = pl.pallas_call(
            functools.partial(reduce_kernel, nx, ny),
            out_shape=(
                shape((groups, nx) + block, bf16),
                shape(boundary, f32),
            ),
            in_specs=[vmem, vmem],
            out_specs=(vmem, vmem),
            scratch_shapes=[
                VMEM((groups, nx) + block, bf16),
                VMEM((max(ny - 1, 1), groups, nx) + block, bf16),
                VMEM((groups, nx) + block, bf16),
                VMEM((3, 2) + boundary, bf16),
                VMEM((2,) + boundary, bf16),
                VMEM((2,) + boundary, bf16),
                dma((max(ny - 1, 1), groups)),
                dma((max(ny - 1, 1), groups)),
                dma((steps, groups)),
                dma((steps, groups)),
                dma((steps, groups)),
                dma((steps, groups)),
                dma((3, 2)),
                dma((3, 2)),
                dma((2,)),
                dma((2,)),
            ],
            compiler_params=pltpu.CompilerParams(
                collective_id=1, has_side_effects=True, vmem_limit_bytes=VMEM_BYTES
            ),
        )(wpart.reshape((ny, groups, nx) + block), borrowed)
        total = total.reshape(tiles, TILE, LANES)[:used].reshape(
            width // LANES, kvol, share // TILE, TILE, LANES
        )

    chunks = max(c for c in range(1, 10) if kvol % c == 0)
    weight_grad, feat_grad = pl.pallas_call(
        finish_kernel,
        out_shape=(shape((kvol, share, width), f32), shape((blocks, rows, width), bf16)),
        in_specs=[smem, vmem, vmem, vmem],
        out_specs=(hbm, hbm),
        scratch_shapes=[
            VMEM((kvol, share, width), f32),
            VMEM((blocks, rows, width), bf16),
            dma((chunks,)),
            dma((blocks,)),
        ],
        compiler_params=pltpu.CompilerParams(vmem_limit_bytes=VMEM_BYTES),
    )(
        shared,
        total,
        own,
        returned,
    )
    return (outputs[None, None], feat_grad[None, None], weight_grad)


def solution(mesh):
    return jax.shard_map(
        functools.partial(on_device, mesh.shape["gx"], mesh.shape["gy"]),
        mesh=mesh,
        in_specs=(
            P("gx", "gy", None, None, None),
            P(None, "gy", None),
            P(),
            P("gx", "gy", None),
            P("gx", "gy", None, None),
            P("gx", "gy", None, None),
            P("gx", "gy", None),
            P("gx", "gy", None, None, None),
        ),
        out_specs=(
            P("gx", "gy", None, None, None),
            P("gx", "gy", None, None, None),
            P(None, "gy", None),
        ),
        check_vma=False,
    )
```

```python
import functools
import math

import jax
import jax.numpy as jnp
from jax import lax
from jax.experimental import pallas as pl
from jax.experimental.pallas import tpu as pltpu
from jax.sharding import PartitionSpec as P

MESH = pl.DeviceIdType.MESH
VMEM = pltpu.VMEM
SMEM = pltpu.SMEM
LANES = 128
TILE = 16
KINDS = (2, 0, 1, 3, 0, 1, 0, 1, 0)
WAVES = (0,) * 9
STAGGER = 1
HALO_AT = 4
UNROLL = 9
VMEM_BYTES = 28 * 1024 * 1024
EXCHANGE_BYTES = 28 * 1024 * 1024

LINE_KINDS = (
    'Axrri', 'Ayrri', 'Axrri', 'Axrri', 'Byr', 'Axrri', 'Ayrri', 'Axrri',
    'Byr', 'Axrri', 'Axrri', 'Axrri', 'Byr', 'Ayrri', 'Ayrri', 'Axrri',
    'Axrri', 'Ayrri', 'Bxr', 'Byr', 'Axrri', 'Ayrri', 'Ayrri', 'Ayrri',
    'Ayrri', 'Byr', 'Ayrri',
)
LINE_ORDERS = (
(
    0, 10, 20, 60, 30, 130, 50, 140, 70, 170, 90, 210, 100, 1, 41, 220,
    110, 230, 150, 81, 21, 160, 240, 200, 31, 2, 121, 260, 11, 61, 51, 131,
    71, 181, 141, 91, 22, 171, 101, 211, 111, 221, 151, 32, 191, 231, 161, 241,
    201, 12, 261, 42, 62, 52, 270, 82, 132, 72, 251, 122, 142, 92, 172, 102,
    3, 212, 112, 23, 222, 152, 232, 33, 162, 242, 202, 13, 262, 63, 53, 73,
    192, 93, 252, 4, 103, 24, 113, 34, 133, 143, 14, 43, 153, 64, 83, 163,
    54, 123, 173, 74, 182, 203, 94, 193, 213, 104, 253, 223, 114, 233, 134, 243,
    271, 144, 263, 44, 154, 84, 164, 6, 124, 174, 183, 204, 194, 214, 254, 224,
    234, 244, 264, 45, 16, 26, 85, 7, 66, 36, 125, 136, 184, 56, 195, 146,
    76, 255, 176, 17, 96, 27, 216, 46, 67, 106, 37, 226, 86, 185, 137, 116,
    236, 126, 57, 147, 156, 246, 77, 177, 166, 266, 196, 97, 217, 206, 256, 107,
    227, 186, 117, 237, 157, 247, 167, 267, 207,
),
(
    0, 10, 40, 20, 60, 30, 130, 80, 50, 140, 70, 170, 120, 90, 210, 100,
    1, 180, 220, 110, 230, 150, 190, 21, 160, 240, 200, 31, 250, 260, 11, 61,
    51, 131, 71, 141, 2, 91, 171, 22, 101, 211, 111, 221, 151, 32, 231, 161,
    241, 201, 12, 261, 270, 62, 52, 72, 92, 102, 112, 132, 142, 152, 162, 172,
    202, 212, 222, 232, 242, 262, 5, 25, 35, 271, 15, 65, 55, 75, 95, 6,
    105, 115, 26, 135, 16, 145, 36, 155, 165, 175, 205, 215, 66, 7, 225, 235,
    27, 245, 136, 265, 17, 56, 146, 46, 37, 76, 176, 86, 96, 216, 126, 67,
    106, 226, 196, 137, 116, 236, 256, 57, 147, 156, 246, 47, 77, 177, 166, 266,
    87, 97, 217, 206, 127, 107, 227, 186, 117, 237, 197, 157, 247, 257, 167, 267,
    187, 207,
),
)


def greet_neighbours(barrier, me_x, me_y, nx, ny):
    total = 0
    for sx, sy in ((-1, 0), (1, 0), (0, -1), (0, 1)):
        x, y = me_x + sx, me_y + sy
        there = (x >= 0) & (x < nx) & (y >= 0) & (y < ny)

        @pl.when(there)
        def _():
            pl.semaphore_signal(barrier, inc=1, device_id=(x, y), device_id_type=MESH)

        total = total + there.astype(jnp.int32)
    return total


def greet_column(barrier, me_x, me_y, ny):
    for step in range(1, ny):
        pl.semaphore_signal(
            barrier, inc=1, device_id=(me_x, lax.rem(me_y + step, ny)), device_id_type=MESH
        )
    return ny - 1


def exists(index, count):
    return (index >= 0) & (index < count)


def exchange_kernel(
    nx, ny, send_ref, feats_ref, weight_ref, halo_ref, full_ref, feats, lsem, xsend, xrecv, hsend, hrecv, wsend, wrecv
):
    me_x, me_y = lax.axis_index("gx"), lax.axis_index("gy")
    barrier = pltpu.get_barrier_semaphore()
    expected = greet_neighbours(barrier, me_x, me_y, nx, ny) + greet_column(
        barrier, me_x, me_y, ny
    )
    load = pltpu.make_async_copy(feats_ref, feats, lsem.at[0])
    load.start()
    keep = pltpu.make_async_copy(weight_ref, full_ref.at[:, me_y], lsem.at[1])
    keep.start()
    load.wait()
    for s in range(halo_ref.shape[1]):
        halo_ref[4, s] = feats[send_ref[s]]
    pl.semaphore_wait(barrier, expected)

    def x_copy(a, device_x):
        return pltpu.make_async_remote_copy(
            src_ref=halo_ref.at[4],
            dst_ref=halo_ref.at[3 * a + 1],
            send_sem=xsend.at[a // 2],
            recv_sem=xrecv.at[a // 2],
            device_id=(device_x, me_y),
            device_id_type=MESH,
        )

    def y_copy(a, b, device_y):
        return pltpu.make_async_remote_copy(
            src_ref=halo_ref.at[3 * a + 1],
            dst_ref=halo_ref.at[3 * a + b],
            send_sem=hsend.at[a, b // 2],
            recv_sem=hrecv.at[a, b // 2],
            device_id=(me_x, device_y),
            device_id_type=MESH,
        )

    def weight_copy(step, owner):
        return pltpu.make_async_remote_copy(
            src_ref=weight_ref,
            dst_ref=full_ref.at[:, owner],
            send_sem=wsend.at[step],
            recv_sem=wrecv.at[step],
            device_id=(me_x, lax.rem(me_y + step, ny)),
            device_id_type=MESH,
        )

    def to_column(a, act):
        for b in (0, 2):
            target = me_y + 1 - b

            @pl.when(exists(target, ny))
            def _():
                act(y_copy(a, b, target))

    for a in (0, 2):
        target = me_x + 1 - a

        @pl.when(exists(target, nx))
        def _():
            x_copy(a, target).start()

    to_column(1, lambda copy: copy.start())
    for step in range(1, ny):
        weight_copy(step, me_y).start()
    blank = jnp.zeros(halo_ref.shape[1:], halo_ref.dtype)
    for a in (0, 2):
        here = exists(me_x + a - 1, nx)

        @pl.when(jnp.logical_not(here))
        def _():
            halo_ref[3 * a + 1] = blank

        @pl.when(here)
        def _():
            x_copy(a, me_x + a - 1).wait_recv()
            to_column(a, lambda copy: copy.start())

    for a in range(3):
        for b in (0, 2):
            there = exists(me_x + a - 1, nx) & exists(me_y + b - 1, ny)

            @pl.when(jnp.logical_not(there))
            def _():
                halo_ref[3 * a + b] = blank

            @pl.when(there)
            def _():
                y_copy(a, b, me_y + b - 1).wait_recv()

        @pl.when(exists(me_x + a - 1, nx))
        def _():
            to_column(a, lambda copy: copy.wait_send())

    for a in (0, 2):
        target = me_x + 1 - a

        @pl.when(exists(target, nx))
        def _():
            x_copy(a, target).wait_send()

    for step in range(1, ny):
        weight_copy(step, lax.rem(me_y - step + ny, ny)).wait_recv()
        weight_copy(step, me_y).wait_send()
    keep.wait()


def compute_kernel(
    source_ref,
    target_ref,
    count_ref,
    feats_ref,
    halo_ref,
    weight_ref,
    bias_ref,
    cot_ref,
    out_ref,
    own_ref,
    borrowed_ref,
    wpart_ref,
    table,
    turned,
    pre,
    dpre,
    grad,
):
    blocks, rows, width = feats_ref.shape
    slots = source_ref.shape[0]
    kvol = weight_ref.shape[0]
    total_blocks = grad.shape[0] - 1
    shared_count = halo_ref.shape[1]
    ny, tiles = wpart_ref.shape[:2]
    share = width // ny
    share_tiles = share // TILE
    places = [(b, feats_ref.at[b]) for b in range(blocks)]
    at = blocks
    for d in range(9):
        if d != 4:
            for s in range(shared_count):
                places.append((at, halo_ref.at[d, s]))
                at += 1
    for t, ref in places:
        value = ref[...]
        table[t] = value
        turned[t] = value.T
    for b in range(blocks):
        pre[b] = jnp.broadcast_to(bias_ref[...], (rows, width))
    for t in range(total_blocks):
        grad[t] = jnp.zeros((rows, width), jnp.float32)
    pre[blocks] = jnp.zeros((rows, width), jnp.float32)
    grad[total_blocks] = jnp.zeros((rows, width), jnp.float32)
    dpre[blocks] = jnp.zeros((rows, width), dpre.dtype)

    def rules(k):
        live = count_ref[k]
        sources = [source_ref[q, k] for q in range(slots)]
        targets = [target_ref[q, k] for q in range(slots)]
        reads = [jnp.where(q < live, v, 0) for q, v in enumerate(sources)]
        spread = [jnp.where(q < live, v, total_blocks) for q, v in enumerate(sources)]
        targets = [jnp.where(q < live, v, blocks) for q, v in enumerate(targets)]
        return reads, spread, targets

    def forward(k, carry):
        reads, _, targets = rules(k)
        taken = jnp.concatenate([table[s] for s in reads], axis=0)
        made = jnp.dot(taken, weight_ref[k], preferred_element_type=jnp.float32)
        for q, target in enumerate(targets):
            pre[target] += made[q * rows : (q + 1) * rows]
        return carry

    lax.fori_loop(0, kvol, forward, 0, unroll=UNROLL)

    def activate(b, carry):
        value = pre[b]
        sig = jax.nn.sigmoid(value)
        out_ref[b] = (value * sig).astype(out_ref.dtype)
        dpre[b] = (cot_ref[b].astype(jnp.float32) * sig * (1.0 + value * (1.0 - sig))).astype(
            dpre.dtype
        )
        return carry

    lax.fori_loop(0, blocks, activate, 0)

    line = len(wpart_ref.shape) == 5
    filled = 2 * kvol * share_tiles
    if not line and filled < tiles:
        for y in range(ny):
            wpart_ref[y, filled:] = jnp.zeros((tiles - filled, TILE, LANES), wpart_ref.dtype)

    def backward(k, carry):
        reads, spread, targets = rules(k)
        pulled = jnp.concatenate([dpre[t] for t in targets], axis=0)
        taken = jnp.concatenate([turned[s] for s in reads], axis=1)
        part = jnp.dot(taken, pulled, preferred_element_type=jnp.float32).astype(wpart_ref.dtype)
        if line:
            for y in range(ny):
                wpart_ref[y, k] = part[y * share : (y + 1) * share].reshape(wpart_ref.shape[2:])
        else:
            for y in range(ny):
                for h in range(width // LANES):
                    piece = part[y * share : (y + 1) * share, h * LANES : (h + 1) * LANES]
                    wpart_ref[y, pl.ds((h * kvol + k) * share_tiles, share_tiles)] = piece.reshape(
                        share_tiles, TILE, LANES
                    )
        back = lax.dot_general(
            pulled, weight_ref[k], (((1,), (1,)), ((), ())), preferred_element_type=jnp.float32
        )
        for q, source in enumerate(spread):
            grad[source] += back[q * rows : (q + 1) * rows]
        return carry

    lax.fori_loop(0, kvol, backward, 0, unroll=UNROLL)
    for b in range(blocks):
        own_ref[b] = grad[b]
    at = blocks
    for d in range(9):
        for s in range(shared_count):
            if d == 4:
                borrowed_ref[d, s] = jnp.zeros((rows, width), borrowed_ref.dtype)
            else:
                borrowed_ref[d, s] = grad[at].astype(borrowed_ref.dtype)
                at += 1


def reduce_kernel(
    nx,
    ny,
    wpart_ref,
    borrowed_ref,
    sum_ref,
    returned_ref,
    work,
    yland,
    xland,
    side_land,
    column,
    x_land,
    ysend,
    yrecv,
    rsend,
    rrecv,
    gsend,
    grecv,
    hsend,
    hrecv,
    bsend,
    brecv,
):
    me_x, me_y = lax.axis_index("gx"), lax.axis_index("gy")
    groups = work.shape[0]
    steps = nx.bit_length() - 1
    bits = [lax.rem(me_x // (1 << b), 2) for b in range(steps)]
    partners = [me_x + (1 - 2 * bits[b]) * (1 << b) for b in range(steps)]

    barrier = pltpu.get_barrier_semaphore()
    expected = greet_neighbours(barrier, me_x, me_y, nx, ny) + greet_column(
        barrier, me_x, me_y, ny
    )
    for b in range(steps):
        pl.semaphore_signal(barrier, inc=1, device_id=(partners[b], me_y), device_id_type=MESH)
    pl.semaphore_wait(barrier, expected + steps)

    def side_copy(a, b):
        return pltpu.make_async_remote_copy(
            src_ref=borrowed_ref.at[3 * a + b],
            dst_ref=side_land.at[a, b // 2],
            send_sem=hsend.at[a, b // 2],
            recv_sem=hrecv.at[a, b // 2],
            device_id=(me_x, me_y + b - 1),
            device_id_type=MESH,
        )

    def back_copy(a):
        return pltpu.make_async_remote_copy(
            src_ref=column.at[a // 2],
            dst_ref=x_land.at[a // 2],
            send_sem=bsend.at[a // 2],
            recv_sem=brecv.at[a // 2],
            device_id=(me_x + a - 1, me_y),
            device_id_type=MESH,
        )

    def sides(act, sign):
        for a in range(3):
            for b in (0, 2):

                @pl.when(exists(me_x + a - 1, nx) & exists(me_y + sign * (b - 1), ny))
                def _():
                    act(a, b)

    def column_copy(step, g):
        other = lax.rem(me_y + step, ny)
        return pltpu.make_async_remote_copy(
            src_ref=wpart_ref.at[other, g],
            dst_ref=yland.at[step - 1, g],
            send_sem=ysend.at[step - 1, g],
            recv_sem=yrecv.at[step - 1, g],
            device_id=(me_x, other),
            device_id_type=MESH,
        )

    late = list(range(2, steps))
    kinds = [[0, 1] + late, [1, 0] + late, late + [0, 1], late + [1, 0]]
    orders = [kinds[kind] for kind in KINDS]
    starts = []
    for g in range(groups):
        at = [0]
        for s in range(steps):
            at.append(at[-1] + bits[orders[g][s]] * (nx >> (s + 1)))
        starts.append(at)

    def scatter_copy(g, s):
        half = nx >> (s + 1)
        bit = bits[orders[g][s]]
        away = starts[g][s] + (1 - bit) * half
        return pltpu.make_async_remote_copy(
            src_ref=work.at[g, pl.ds(away, half)],
            dst_ref=xland.at[g, pl.ds(nx - 2 * half, half)],
            send_sem=rsend.at[s, g],
            recv_sem=rrecv.at[s, g],
            device_id=(partners[orders[g][s]], me_y),
            device_id_type=MESH,
        )

    def gather_copy(g, s, landing):
        half = nx >> (s + 1)
        bit = bits[orders[g][s]]
        mine = starts[g][s + 1]
        place = starts[g][s] + (1 - bit) * half if landing else mine
        return pltpu.make_async_remote_copy(
            src_ref=sum_ref.at[g, pl.ds(mine, half)],
            dst_ref=sum_ref.at[g, pl.ds(place, half)],
            send_sem=gsend.at[s, g],
            recv_sem=grecv.at[s, g],
            device_id=(partners[orders[g][s]], me_y),
            device_id_type=MESH,
        )

    for g in range(groups):
        for step in range(1, ny):
            column_copy(step, g).start()
    sides(lambda a, b: side_copy(a, b).start(), 1)

    def begin(g):
        value = wpart_ref[me_y, g].astype(jnp.float32)
        for step in range(1, ny):
            column_copy(step, g).wait_recv()
            value = value + yland[step - 1, g].astype(jnp.float32)
        work[g] = value.astype(work.dtype)
        scatter_copy(g, 0).start()

    def scatter(g, s):
        half = nx >> (s + 1)
        scatter_copy(g, s).wait_recv()
        keep = pl.ds(starts[g][s + 1], half)
        value = work[g, keep].astype(jnp.float32) + xland[g, pl.ds(nx - 2 * half, half)].astype(
            jnp.float32
        )
        if s < steps - 1:
            work[g, keep] = value.astype(work.dtype)
            scatter_copy(g, s + 1).start()
        else:
            sum_ref[g, keep] = value.astype(sum_ref.dtype)
            gather_copy(g, s, False).start()

    def gather(g, s):
        gather_copy(g, s, True).wait_recv()
        if s > 0:
            gather_copy(g, s - 1, False).start()

    events = []
    for g in range(groups):
        events.append((WAVES[g] * STAGGER, g, functools.partial(begin, g)))
        for s in range(steps):
            events.append((WAVES[g] * STAGGER + s + 1, g, functools.partial(scatter, g, s)))
            events.append(
                (WAVES[g] * STAGGER + 2 * steps - s, g, functools.partial(gather, g, s))
            )
    events.sort(key=lambda event: event[:2])
    first = [event[2] for event in events if event[0] < HALO_AT]
    rest = [event[2] for event in events if event[0] >= HALO_AT]
    for event in first:
        event()

    returned_ref[...] = jnp.zeros(returned_ref.shape, jnp.float32)
    for b in (0, 2):

        @pl.when(exists(me_y + 1 - b, ny))
        def _():
            side_copy(1, b).wait_recv()
            returned_ref[...] += side_land[1, b // 2].astype(jnp.float32)

    for a in (0, 2):

        @pl.when(exists(me_x + a - 1, nx))
        def _():
            for b in (0, 2):
                missing = jnp.logical_not(exists(me_y + 1 - b, ny))

                @pl.when(missing)
                def _():
                    side_land[a, b // 2] = jnp.zeros(side_land.shape[2:], side_land.dtype)

                @pl.when(jnp.logical_not(missing))
                def _():
                    side_copy(a, b).wait_recv()

            column[a // 2] = (
                borrowed_ref[3 * a + 1].astype(jnp.float32)
                + side_land[a, 0].astype(jnp.float32)
                + side_land[a, 1].astype(jnp.float32)
            ).astype(column.dtype)
            back_copy(a).start()

    for event in rest:
        event()

    for a in (0, 2):

        @pl.when(exists(me_x + 1 - a, nx))
        def _():
            back_copy(a).wait_recv()
            returned_ref[...] += x_land[a // 2].astype(jnp.float32)

    for g in range(groups):
        for step in range(1, ny):
            column_copy(step, g).wait_send()
        for s in range(steps):
            scatter_copy(g, s).wait_send()
            gather_copy(g, s, False).wait_send()
    sides(lambda a, b: side_copy(a, b).wait_send(), 1)
    for a in (0, 2):

        @pl.when(exists(me_x + a - 1, nx))
        def _():
            back_copy(a).wait_send()


def line_kernel(
    nx,
    ny,
    wpart_ref,
    borrowed_ref,
    sum_ref,
    returned_ref,
    work,
    yland,
    full_land,
    half_land,
    land,
    spare,
    side_land,
    column,
    x_land,
    ysend,
    yrecv,
    csend,
    crecv,
    hsend,
    hrecv,
    bsend,
    brecv,
):
    me_x, me_y = lax.axis_index("gx"), lax.axis_index("gy")
    kvol = work.shape[0]
    f32 = jnp.float32
    bit_x, bit_y, z = lax.rem(me_x, 2), lax.rem(me_x // 2, 2), me_x // 4
    high = z // 2
    beside = {"x": me_x + 1 - 2 * bit_x, "y": me_x + 2 - 4 * bit_y}
    inner = exists(z - 1, 2)
    near = jnp.where(inner, me_x - 4 + 8 * high, me_x + 4 - 8 * high)
    middle = me_x + 4 - 8 * high

    barrier = pltpu.get_barrier_semaphore()
    expected = greet_neighbours(barrier, me_x, me_y, nx, ny) + greet_column(
        barrier, me_x, me_y, ny
    )
    for device in (beside["x"], beside["y"], near):
        pl.semaphore_signal(barrier, inc=1, device_id=(device, me_y), device_id_type=MESH)

    @pl.when(inner)
    def _():
        pl.semaphore_signal(barrier, inc=1, device_id=(middle, me_y), device_id_type=MESH)

    pl.semaphore_wait(barrier, expected + 3 + inner.astype(jnp.int32))

    def side_copy(a, b):
        return pltpu.make_async_remote_copy(
            src_ref=borrowed_ref.at[3 * a + b],
            dst_ref=side_land.at[a, b // 2],
            send_sem=hsend.at[a, b // 2],
            recv_sem=hrecv.at[a, b // 2],
            device_id=(me_x, me_y + b - 1),
            device_id_type=MESH,
        )

    def back_copy(a):
        return pltpu.make_async_remote_copy(
            src_ref=column.at[a // 2],
            dst_ref=x_land.at[a // 2],
            send_sem=bsend.at[a // 2],
            recv_sem=brecv.at[a // 2],
            device_id=(me_x + a - 1, me_y),
            device_id_type=MESH,
        )

    def sides(act, sign):
        for a in range(3):
            for b in (0, 2):

                @pl.when(exists(me_x + a - 1, nx) & exists(me_y + sign * (b - 1), ny))
                def _():
                    act(a, b)

    def column_copy(step, g):
        other = lax.rem(me_y + step, ny)
        return pltpu.make_async_remote_copy(
            src_ref=wpart_ref.at[other, g],
            dst_ref=yland.at[step - 1, g],
            send_sem=ysend.at[step - 1],
            recv_sem=yrecv.at[step - 1, g],
            device_id=(me_x, other),
            device_id_type=MESH,
        )

    for g in range(kvol):
        for step in range(1, ny):
            column_copy(step, g).start()
    sides(lambda a, b: side_copy(a, b).start(), 1)

    def give_back():
        returned_ref[...] = jnp.zeros(returned_ref.shape, f32)
        for b in (0, 2):

            @pl.when(exists(me_y + 1 - b, ny))
            def _():
                side_copy(1, b).wait_recv()
                returned_ref[...] += side_land[1, b // 2].astype(f32)

        for a in (0, 2):

            @pl.when(exists(me_x + a - 1, nx))
            def _():
                for b in (0, 2):
                    missing = jnp.logical_not(exists(me_y + 1 - b, ny))

                    @pl.when(missing)
                    def _():
                        side_land[a, b // 2] = jnp.zeros(side_land.shape[2:], side_land.dtype)

                    @pl.when(jnp.logical_not(missing))
                    def _():
                        side_copy(a, b).wait_recv()

                column[a // 2] = (
                    borrowed_ref[3 * a + 1].astype(f32)
                    + side_land[a, 0].astype(f32)
                    + side_land[a, 1].astype(f32)
                ).astype(column.dtype)
                back_copy(a).start()

    def take_back():
        for a in (0, 2):

            @pl.when(exists(me_x + 1 - a, nx))
            def _():
                back_copy(a).wait_recv()
                returned_ref[...] += x_land[a // 2].astype(f32)

    def own_sum(g):
        value = wpart_ref[me_y, g].astype(f32)
        for step in range(1, ny):
            column_copy(step, g).wait_recv()
            value = value + yland[step - 1, g].astype(f32)
        return value

    def program(order, inside):
        sent = {}

        def copy(g, src, dst, leave, arrive, device):
            return pltpu.make_async_remote_copy(
                src_ref=src,
                dst_ref=dst,
                send_sem=csend.at[leave],
                recv_sem=crecv.at[arrive, g],
                device_id=(device, me_y),
                device_id_type=MESH,
            )

        def send(g, src, dst, leave, arrive, device):
            copy(g, src, dst, leave, arrive, device).start()
            sent[leave] = sent.get(leave, 0) + math.prod(src.shape[:-2])

        def recv(g, dst, arrive):
            copy(g, dst, dst, 0, arrive, beside["x"]).wait_recv()

        def along(g, k):
            first = LINE_KINDS[g][1]
            second = "y" if first == "x" else "x"
            bits = {"x": bit_x, "y": bit_y}
            hb, qb = bits[first], bits[second]
            mine, other = 2 * hb + qb, 2 * hb + 1 - qb
            kept, gone = pl.ds(2 * hb, 2), pl.ds(2 - 2 * hb, 2)
            total, ours = sum_ref.at[g], work.at[g]
            if k == 0:
                work[g] = own_sum(g).astype(work.dtype)
                send(g, ours.at[gone], half_land.at[g], 0, 0, beside[first])
            elif k == 1:
                recv(g, half_land.at[g], 0)
                work[g, kept] = (
                    work[g, kept].astype(f32) + half_land[g].astype(f32)
                ).astype(work.dtype)
                send(g, ours.at[other], land.at[0, g], 1, 1, beside[second])
            elif k == 2:
                recv(g, land.at[0, g], 1)
                work[g, mine] = (
                    work[g, mine].astype(f32) + land[0, g].astype(f32)
                ).astype(work.dtype)
                if not inside:
                    send(g, ours.at[mine], land.at[1, g], 2, 2, near)
            elif k == 3:
                recv(g, land.at[1, g], 2)
                work[g, mine] = (
                    work[g, mine].astype(f32) + land[1, g].astype(f32)
                ).astype(work.dtype)
                send(g, ours.at[mine], land.at[2, g], 3, 3, middle)
            elif k == 4:
                recv(g, land.at[2, g], 3)
                sum_ref[g, mine] = (
                    work[g, mine].astype(f32) + land[2, g].astype(f32)
                ).astype(sum_ref.dtype)
                send(g, total.at[mine], total.at[mine], 2, 2, near)
                send(g, total.at[mine], total.at[mine], 4, 0, beside[second])
            elif k == 5:
                recv(g, total.at[mine], 2)
                send(g, total.at[mine], total.at[mine], 4, 0, beside[second])
            elif k == 6:
                recv(g, total.at[other], 0)
                send(g, total.at[kept], total.at[kept], 5, 4, beside[first])
            elif k == 7:
                recv(g, total.at[gone], 4)

        def fold(g, k):
            first = LINE_KINDS[g][1]
            second = "y" if first == "x" else "x"
            bits = {"x": bit_x, "y": bit_y}
            hb, qb = high, bits[first]
            mine, other = 2 * hb + qb, 2 * hb + 1 - qb
            kept, gone = pl.ds(2 * hb, 2), pl.ds(2 - 2 * hb, 2)
            total, ours = sum_ref.at[g], work.at[g]
            if not inside:
                if k == 0:
                    work[g] = own_sum(g).astype(work.dtype)
                    send(g, ours, full_land.at[g], 6, 2, near)
                elif k == 6:
                    recv(g, total.at[kept], 2)
                elif k == 7:
                    recv(g, total.at[gone], 3)
            elif k == 1:
                value = own_sum(g)
                recv(g, full_land.at[g], 2)
                work[g] = (value + full_land[g].astype(f32)).astype(work.dtype)
                send(g, ours.at[gone], half_land.at[g], 7, 3, middle)
            elif k == 2:
                recv(g, half_land.at[g], 3)
                work[g, kept] = (
                    work[g, kept].astype(f32) + half_land[g].astype(f32)
                ).astype(work.dtype)
                send(g, ours.at[other], land.at[0, g], 1, 0, beside[first])
            elif k == 3:
                recv(g, land.at[0, g], 0)
                work[g, mine] = (
                    work[g, mine].astype(f32) + land[0, g].astype(f32)
                ).astype(work.dtype)
                send(g, ours.at[mine], land.at[1, g], 1, 1, beside[second])
            elif k == 4:
                recv(g, land.at[1, g], 1)
                sum_ref[g, mine] = (
                    work[g, mine].astype(f32) + land[1, g].astype(f32)
                ).astype(sum_ref.dtype)
                send(g, total.at[mine], total.at[mine], 4, 4, beside[first])
            elif k == 5:
                recv(g, total.at[other], 4)
                send(g, total.at[kept], total.at[kept], 8, 2, middle)
                send(g, total.at[kept], total.at[kept], 8, 2, near)
            elif k == 6:
                recv(g, total.at[gone], 2)
                send(g, total.at[gone], total.at[gone], 8, 3, near)

        for event in order:
            g, k = divmod(event, 10)
            if g == kvol:
                (give_back, take_back)[k]()
            elif LINE_KINDS[g][0] == "B":
                fold(g, k)
            else:
                along(g, k)
        for leave, pieces in sent.items():
            gone = spare.at[pl.ds(0, pieces)]
            copy(0, gone, gone, leave, 0, beside["x"]).wait_send()

    @pl.when(inner)
    def _():
        program(LINE_ORDERS[0], True)

    @pl.when(jnp.logical_not(inner))
    def _():
        program(LINE_ORDERS[1], False)

    for step in range(1, ny):
        other = lax.rem(me_y + step, ny)
        pltpu.make_async_remote_copy(
            src_ref=wpart_ref.at[other],
            dst_ref=yland.at[step - 1],
            send_sem=ysend.at[step - 1],
            recv_sem=yrecv.at[step - 1, 0],
            device_id=(me_x, other),
            device_id_type=MESH,
        ).wait_send()
    sides(lambda a, b: side_copy(a, b).wait_send(), 1)
    for a in (0, 2):

        @pl.when(exists(me_x + a - 1, nx))
        def _():
            back_copy(a).wait_send()


def finish_kernel(
    send_ref, total_ref, own_ref, returned_ref, weight_ref, feat_ref, wide, feats, wsem, fsem
):
    chunks = wsem.shape[0]
    kvol, share, width = wide.shape
    per = kvol // chunks
    blocks, rows = own_ref.shape[:2]
    copies = []
    for c in range(chunks):
        at = pl.ds(c * per, per)
        if len(total_ref.shape) == 3:
            wide[at] = total_ref[at].astype(jnp.float32) * (1.0 / rows)
        else:
            for h in range(width // LANES):
                wide[at, :, h * LANES : (h + 1) * LANES] = total_ref[h, at].reshape(
                    per, share, LANES
                ).astype(jnp.float32) * (1.0 / rows)
        copy = pltpu.make_async_copy(wide.at[at], weight_ref.at[at], wsem.at[c])
        copy.start()
        copies.append(copy)
    for b in range(blocks):
        value = own_ref[b]
        for s in range(returned_ref.shape[0]):
            value = value + jnp.where(send_ref[s] == b, returned_ref[s], 0.0)
        feats[b] = value.astype(feats.dtype)
        copy = pltpu.make_async_copy(feats.at[b], feat_ref.at[b], fsem.at[b])
        copy.start()
        copies.append(copy)
    for copy in copies:
        copy.wait()


def on_device(
    nx,
    ny,
    features,
    kernel_weight,
    channel_bias,
    send_list,
    rule_source,
    rule_target,
    live_counts,
    out_grad,
):
    feats = features[0, 0]
    blocks, rows, width = feats.shape
    shared = send_list[0, 0]
    shared_count = shared.shape[0]
    kvol, slots = rule_source.shape[2:]
    share = kernel_weight.shape[1]
    bf16, f32 = jnp.bfloat16, jnp.float32
    shape = jax.ShapeDtypeStruct
    vmem = pl.BlockSpec(memory_space=VMEM)
    smem = pl.BlockSpec(memory_space=SMEM)
    hbm = pl.BlockSpec(memory_space=pltpu.HBM)
    dma = pltpu.SemaphoreType.DMA
    squares = 9

    halo, full = pl.pallas_call(
        functools.partial(exchange_kernel, nx, ny),
        out_shape=(
            shape((squares, shared_count, rows, width), bf16),
            shape((kvol, ny, share, width), bf16),
        ),
        in_specs=[smem, hbm, hbm],
        out_specs=(vmem, vmem),
        scratch_shapes=[
            VMEM((blocks, rows, width), bf16),
            dma((2,)),
            dma((2,)),
            dma((2,)),
            dma((3, 2)),
            dma((3, 2)),
            dma((ny,)),
            dma((ny,)),
        ],
        compiler_params=pltpu.CompilerParams(
            collective_id=0, has_side_effects=True, vmem_limit_bytes=EXCHANGE_BYTES
        ),
    )(shared, feats, kernel_weight)

    total_blocks = blocks + (squares - 1) * shared_count
    used = (width // LANES) * kvol * (share // TILE)
    groups = len(KINDS)
    unit = groups * nx
    tiles = -(-used // unit) * unit
    depth = tiles // unit
    line = nx == 16 and kvol == len(LINE_KINDS)
    quarters = (4, share // 4, width)
    outputs, own, borrowed, wpart = pl.pallas_call(
        compute_kernel,
        out_shape=(
            shape((blocks, rows, width), bf16),
            shape((blocks, rows, width), f32),
            shape((squares, shared_count, rows, width), bf16),
            shape((ny, kvol) + quarters if line else (ny, tiles, TILE, LANES), bf16),
        ),
        in_specs=[smem, smem, smem, vmem, vmem, vmem, vmem, vmem],
        out_specs=(vmem, vmem, vmem, vmem),
        scratch_shapes=[
            VMEM((total_blocks, rows, width), bf16),
            VMEM((total_blocks, width, rows), bf16),
            VMEM((blocks + 1, rows, width), f32),
            VMEM((blocks + 1, rows, width), bf16),
            VMEM((total_blocks + 1, rows, width), f32),
        ],
        compiler_params=pltpu.CompilerParams(vmem_limit_bytes=VMEM_BYTES),
    )(
        rule_source[0, 0].T,
        rule_target[0, 0].T,
        live_counts.reshape(-1),
        feats,
        halo,
        full.reshape(kvol, width, width),
        channel_bias.reshape(1, width),
        out_grad[0, 0],
    )

    steps = nx.bit_length() - 1
    block = (depth, TILE, LANES)
    boundary = (shared_count, rows, width)
    if line:
        total, returned = pl.pallas_call(
            functools.partial(line_kernel, nx, ny),
            out_shape=(shape((kvol,) + quarters, bf16), shape(boundary, f32)),
            in_specs=[vmem, vmem],
            out_specs=(vmem, vmem),
            scratch_shapes=[
                VMEM((kvol,) + quarters, bf16),
                VMEM((max(ny - 1, 1), kvol) + quarters, bf16),
                VMEM((kvol,) + quarters, bf16),
                VMEM((kvol, 2) + quarters[1:], bf16),
                VMEM((3, kvol) + quarters[1:], bf16),
                VMEM((8 * kvol,) + quarters[1:], bf16),
                VMEM((3, 2) + boundary, bf16),
                VMEM((2,) + boundary, bf16),
                VMEM((2,) + boundary, bf16),
                dma((max(ny - 1, 1),)),
                dma((max(ny - 1, 1), kvol)),
                dma((9,)),
                dma((5, kvol)),
                dma((3, 2)),
                dma((3, 2)),
                dma((2,)),
                dma((2,)),
            ],
            compiler_params=pltpu.CompilerParams(
                collective_id=1, has_side_effects=True, vmem_limit_bytes=VMEM_BYTES
            ),
        )(wpart, borrowed)
        total = total.reshape(kvol, share, width)
    else:
        total, returned = pl.pallas_call(
            functools.partial(reduce_kernel, nx, ny),
            out_shape=(
                shape((groups, nx) + block, bf16),
                shape(boundary, f32),
            ),
            in_specs=[vmem, vmem],
            out_specs=(vmem, vmem),
            scratch_shapes=[
                VMEM((groups, nx) + block, bf16),
                VMEM((max(ny - 1, 1), groups, nx) + block, bf16),
                VMEM((groups, nx) + block, bf16),
                VMEM((3, 2) + boundary, bf16),
                VMEM((2,) + boundary, bf16),
                VMEM((2,) + boundary, bf16),
                dma((max(ny - 1, 1), groups)),
                dma((max(ny - 1, 1), groups)),
                dma((steps, groups)),
                dma((steps, groups)),
                dma((steps, groups)),
                dma((steps, groups)),
                dma((3, 2)),
                dma((3, 2)),
                dma((2,)),
                dma((2,)),
            ],
            compiler_params=pltpu.CompilerParams(
                collective_id=1, has_side_effects=True, vmem_limit_bytes=VMEM_BYTES
            ),
        )(wpart.reshape((ny, groups, nx) + block), borrowed)
        total = total.reshape(tiles, TILE, LANES)[:used].reshape(
            width // LANES, kvol, share // TILE, TILE, LANES
        )

    chunks = max(c for c in range(1, 10) if kvol % c == 0)
    weight_grad, feat_grad = pl.pallas_call(
        finish_kernel,
        out_shape=(shape((kvol, share, width), f32), shape((blocks, rows, width), bf16)),
        in_specs=[smem, vmem, vmem, vmem],
        out_specs=(hbm, hbm),
        scratch_shapes=[
            VMEM((kvol, share, width), f32),
            VMEM((blocks, rows, width), bf16),
            dma((chunks,)),
            dma((blocks,)),
        ],
        compiler_params=pltpu.CompilerParams(vmem_limit_bytes=VMEM_BYTES),
    )(
        shared,
        total,
        own,
        returned,
    )
    return (outputs[None, None], feat_grad[None, None], weight_grad)


def solution(mesh):
    return jax.shard_map(
        functools.partial(on_device, mesh.shape["gx"], mesh.shape["gy"]),
        mesh=mesh,
        in_specs=(
            P("gx", "gy", None, None, None),
            P(None, "gy", None),
            P(),
            P("gx", "gy", None),
            P("gx", "gy", None, None),
            P("gx", "gy", None, None),
            P("gx", "gy", None),
            P("gx", "gy", None, None, None),
        ),
        out_specs=(
            P("gx", "gy", None, None, None),
            P("gx", "gy", None, None, None),
            P(None, "gy", None),
        ),
        check_vma=False,
    )
```

```python
import functools
import math

import jax
import jax.numpy as jnp
from jax import lax
from jax.experimental import pallas as pl
from jax.experimental.pallas import tpu as pltpu
from jax.sharding import PartitionSpec as P

MESH = pl.DeviceIdType.MESH
VMEM = pltpu.VMEM
SMEM = pltpu.SMEM
LANES = 128
TILE = 16
KINDS = (2, 0, 1, 3, 0, 1, 0, 1, 0)
WAVES = (0,) * 9
STAGGER = 1
HALO_AT = 4
UNROLL = 9
VMEM_BYTES = 28 * 1024 * 1024
EXCHANGE_BYTES = 28 * 1024 * 1024
LINE_BYTES = 28 * 1024 * 1024
LINE_LENGTH = 4
MAKE_AT = (4, 12, 27)
MAKE_LEAD = 2

LINE_KINDS = (
    'Ax', 'Ay', 'Ax', 'By', 'Ay', 'Ax', 'Ay', 'Ax', 'By',
    'Ay', 'Ax', 'Ay', 'Ax', 'Ay', 'Ax', 'By', 'Ay', 'Ax',
    'Bx', 'Ay', 'Ax', 'Ax', 'By', 'Ay', 'Ax', 'Ay', 'By',
)
LINE_ORDERS = (
(
    1, 31, 81, 21, 51, 2, 151, 11, 41, 71, 61, 101, 181, 91, 121, 22,
    111, 141, 131, 171, 161, 201, 52, 221, 191, 211, 231, 241, 12, 251, 32, 42,
    72, 270, 82, 62, 102, 261, 152, 92, 122, 112, 142, 3, 132, 172, 23, 162,
    202, 192, 53, 212, 232, 242, 13, 252, 43, 73, 103, 222, 123, 262, 4, 143,
    24, 173, 54, 63, 93, 14, 33, 203, 44, 83, 213, 74, 153, 113, 104, 182,
    243, 124, 223, 133, 144, 263, 163, 174, 193, 64, 233, 271, 94, 253, 34, 204,
    84, 214, 6, 154, 114, 183, 244, 224, 134, 264, 164, 194, 234, 254, 35, 16,
    26, 85, 7, 46, 56, 155, 66, 184, 76, 225, 96, 106, 265, 116, 17, 126,
    27, 136, 36, 47, 146, 57, 166, 86, 185, 67, 176, 196, 156, 77, 97, 206,
    236, 107, 117, 216, 256, 226, 127, 137, 246, 266, 147, 167, 186, 177, 197, 207,
    237, 217, 257, 247,
),
(
    1, 21, 51, 11, 41, 71, 61, 101, 91, 2, 121, 111, 22, 141, 131, 171,
    161, 201, 52, 191, 211, 231, 241, 12, 251, 270, 42, 72, 102, 122, 142, 172,
    62, 92, 202, 212, 112, 242, 132, 162, 192, 232, 252, 5, 25, 55, 271, 15,
    45, 75, 105, 125, 6, 145, 175, 26, 65, 16, 95, 56, 205, 215, 115, 245,
    135, 46, 7, 165, 195, 27, 235, 66, 255, 17, 76, 96, 36, 57, 106, 116,
    86, 126, 136, 156, 47, 146, 166, 226, 67, 176, 196, 266, 77, 97, 206, 236,
    37, 107, 117, 216, 256, 87, 127, 137, 246, 157, 147, 167, 186, 177, 197, 227,
    207, 237, 267, 217, 257, 187, 247,
),
)


def greet_neighbours(barrier, me_x, me_y, nx, ny):
    total = 0
    for sx, sy in ((-1, 0), (1, 0), (0, -1), (0, 1)):
        x, y = me_x + sx, me_y + sy
        there = (x >= 0) & (x < nx) & (y >= 0) & (y < ny)

        @pl.when(there)
        def _():
            pl.semaphore_signal(barrier, inc=1, device_id=(x, y), device_id_type=MESH)

        total = total + there.astype(jnp.int32)
    return total


def greet_column(barrier, me_x, me_y, ny):
    for step in range(1, ny):
        pl.semaphore_signal(
            barrier, inc=1, device_id=(me_x, lax.rem(me_y + step, ny)), device_id_type=MESH
        )
    return ny - 1


def exists(index, count):
    return (index >= 0) & (index < count)


def exchange_kernel(
    nx, ny, send_ref, feats_ref, weight_ref, halo_ref, full_ref, feats, lsem, xsend, xrecv, hsend, hrecv, wsend, wrecv
):
    me_x, me_y = lax.axis_index("gx"), lax.axis_index("gy")
    barrier = pltpu.get_barrier_semaphore()
    expected = greet_neighbours(barrier, me_x, me_y, nx, ny) + greet_column(
        barrier, me_x, me_y, ny
    )
    load = pltpu.make_async_copy(feats_ref, feats, lsem.at[0])
    load.start()
    keep = pltpu.make_async_copy(weight_ref, full_ref.at[:, me_y], lsem.at[1])
    keep.start()
    load.wait()
    for s in range(halo_ref.shape[1]):
        halo_ref[4, s] = feats[send_ref[s]]
    pl.semaphore_wait(barrier, expected)

    def x_copy(a, device_x):
        return pltpu.make_async_remote_copy(
            src_ref=halo_ref.at[4],
            dst_ref=halo_ref.at[3 * a + 1],
            send_sem=xsend.at[a // 2],
            recv_sem=xrecv.at[a // 2],
            device_id=(device_x, me_y),
            device_id_type=MESH,
        )

    def y_copy(a, b, device_y):
        return pltpu.make_async_remote_copy(
            src_ref=halo_ref.at[3 * a + 1],
            dst_ref=halo_ref.at[3 * a + b],
            send_sem=hsend.at[a, b // 2],
            recv_sem=hrecv.at[a, b // 2],
            device_id=(me_x, device_y),
            device_id_type=MESH,
        )

    def weight_copy(step, owner):
        return pltpu.make_async_remote_copy(
            src_ref=weight_ref,
            dst_ref=full_ref.at[:, owner],
            send_sem=wsend.at[step],
            recv_sem=wrecv.at[step],
            device_id=(me_x, lax.rem(me_y + step, ny)),
            device_id_type=MESH,
        )

    def to_column(a, act):
        for b in (0, 2):
            target = me_y + 1 - b

            @pl.when(exists(target, ny))
            def _():
                act(y_copy(a, b, target))

    for a in (0, 2):
        target = me_x + 1 - a

        @pl.when(exists(target, nx))
        def _():
            x_copy(a, target).start()

    to_column(1, lambda copy: copy.start())
    for step in range(1, ny):
        weight_copy(step, me_y).start()
    blank = jnp.zeros(halo_ref.shape[1:], halo_ref.dtype)
    for a in (0, 2):
        here = exists(me_x + a - 1, nx)

        @pl.when(jnp.logical_not(here))
        def _():
            halo_ref[3 * a + 1] = blank

        @pl.when(here)
        def _():
            x_copy(a, me_x + a - 1).wait_recv()
            to_column(a, lambda copy: copy.start())

    for a in range(3):
        for b in (0, 2):
            there = exists(me_x + a - 1, nx) & exists(me_y + b - 1, ny)

            @pl.when(jnp.logical_not(there))
            def _():
                halo_ref[3 * a + b] = blank

            @pl.when(there)
            def _():
                y_copy(a, b, me_y + b - 1).wait_recv()

        @pl.when(exists(me_x + a - 1, nx))
        def _():
            to_column(a, lambda copy: copy.wait_send())

    for a in (0, 2):
        target = me_x + 1 - a

        @pl.when(exists(target, nx))
        def _():
            x_copy(a, target).wait_send()

    for step in range(1, ny):
        weight_copy(step, lax.rem(me_y - step + ny, ny)).wait_recv()
        weight_copy(step, me_y).wait_send()
    keep.wait()


def compute_kernel(
    source_ref,
    target_ref,
    count_ref,
    feats_ref,
    halo_ref,
    weight_ref,
    bias_ref,
    cot_ref,
    out_ref,
    own_ref,
    borrowed_ref,
    wpart_ref,
    table,
    turned,
    pre,
    dpre,
    grad,
):
    blocks, rows, width = feats_ref.shape
    slots = source_ref.shape[0]
    kvol = weight_ref.shape[0]
    total_blocks = grad.shape[0] - 1
    shared_count = halo_ref.shape[1]
    ny, tiles = wpart_ref.shape[:2]
    share = width // ny
    share_tiles = share // TILE
    places = [(b, feats_ref.at[b]) for b in range(blocks)]
    at = blocks
    for d in range(9):
        if d != 4:
            for s in range(shared_count):
                places.append((at, halo_ref.at[d, s]))
                at += 1
    for t, ref in places:
        value = ref[...]
        table[t] = value
        turned[t] = value.T
    for b in range(blocks):
        pre[b] = jnp.broadcast_to(bias_ref[...], (rows, width))
    for t in range(total_blocks):
        grad[t] = jnp.zeros((rows, width), jnp.float32)
    pre[blocks] = jnp.zeros((rows, width), jnp.float32)
    grad[total_blocks] = jnp.zeros((rows, width), jnp.float32)
    dpre[blocks] = jnp.zeros((rows, width), dpre.dtype)

    def rules(k):
        live = count_ref[k]
        sources = [source_ref[q, k] for q in range(slots)]
        targets = [target_ref[q, k] for q in range(slots)]
        reads = [jnp.where(q < live, v, 0) for q, v in enumerate(sources)]
        spread = [jnp.where(q < live, v, total_blocks) for q, v in enumerate(sources)]
        targets = [jnp.where(q < live, v, blocks) for q, v in enumerate(targets)]
        return reads, spread, targets

    def forward(k, carry):
        reads, _, targets = rules(k)
        taken = jnp.concatenate([table[s] for s in reads], axis=0)
        made = jnp.dot(taken, weight_ref[k], preferred_element_type=jnp.float32)
        for q, target in enumerate(targets):
            pre[target] += made[q * rows : (q + 1) * rows]
        return carry

    lax.fori_loop(0, kvol, forward, 0, unroll=UNROLL)

    def activate(b, carry):
        value = pre[b]
        sig = jax.nn.sigmoid(value)
        out_ref[b] = (value * sig).astype(out_ref.dtype)
        dpre[b] = (cot_ref[b].astype(jnp.float32) * sig * (1.0 + value * (1.0 - sig))).astype(
            dpre.dtype
        )
        return carry

    lax.fori_loop(0, blocks, activate, 0)

    filled = 2 * kvol * share_tiles
    if filled < tiles:
        for y in range(ny):
            wpart_ref[y, filled:] = jnp.zeros((tiles - filled, TILE, LANES), wpart_ref.dtype)

    def backward(k, carry):
        reads, spread, targets = rules(k)
        pulled = jnp.concatenate([dpre[t] for t in targets], axis=0)
        taken = jnp.concatenate([turned[s] for s in reads], axis=1)
        part = jnp.dot(taken, pulled, preferred_element_type=jnp.float32).astype(wpart_ref.dtype)
        for y in range(ny):
            for h in range(width // LANES):
                piece = part[y * share : (y + 1) * share, h * LANES : (h + 1) * LANES]
                wpart_ref[y, pl.ds((h * kvol + k) * share_tiles, share_tiles)] = piece.reshape(
                    share_tiles, TILE, LANES
                )
        back = lax.dot_general(
            pulled, weight_ref[k], (((1,), (1,)), ((), ())), preferred_element_type=jnp.float32
        )
        for q, source in enumerate(spread):
            grad[source] += back[q * rows : (q + 1) * rows]
        return carry

    lax.fori_loop(0, kvol, backward, 0, unroll=UNROLL)
    for b in range(blocks):
        own_ref[b] = grad[b]
    at = blocks
    for d in range(9):
        for s in range(shared_count):
            if d == 4:
                borrowed_ref[d, s] = jnp.zeros((rows, width), borrowed_ref.dtype)
            else:
                borrowed_ref[d, s] = grad[at].astype(borrowed_ref.dtype)
                at += 1


def reduce_kernel(
    nx,
    ny,
    wpart_ref,
    borrowed_ref,
    sum_ref,
    returned_ref,
    work,
    yland,
    xland,
    side_land,
    column,
    x_land,
    ysend,
    yrecv,
    rsend,
    rrecv,
    gsend,
    grecv,
    hsend,
    hrecv,
    bsend,
    brecv,
):
    me_x, me_y = lax.axis_index("gx"), lax.axis_index("gy")
    groups = work.shape[0]
    steps = nx.bit_length() - 1
    bits = [lax.rem(me_x // (1 << b), 2) for b in range(steps)]
    partners = [me_x + (1 - 2 * bits[b]) * (1 << b) for b in range(steps)]

    barrier = pltpu.get_barrier_semaphore()
    expected = greet_neighbours(barrier, me_x, me_y, nx, ny) + greet_column(
        barrier, me_x, me_y, ny
    )
    for b in range(steps):
        pl.semaphore_signal(barrier, inc=1, device_id=(partners[b], me_y), device_id_type=MESH)
    pl.semaphore_wait(barrier, expected + steps)

    def side_copy(a, b):
        return pltpu.make_async_remote_copy(
            src_ref=borrowed_ref.at[3 * a + b],
            dst_ref=side_land.at[a, b // 2],
            send_sem=hsend.at[a, b // 2],
            recv_sem=hrecv.at[a, b // 2],
            device_id=(me_x, me_y + b - 1),
            device_id_type=MESH,
        )

    def back_copy(a):
        return pltpu.make_async_remote_copy(
            src_ref=column.at[a // 2],
            dst_ref=x_land.at[a // 2],
            send_sem=bsend.at[a // 2],
            recv_sem=brecv.at[a // 2],
            device_id=(me_x + a - 1, me_y),
            device_id_type=MESH,
        )

    def sides(act, sign):
        for a in range(3):
            for b in (0, 2):

                @pl.when(exists(me_x + a - 1, nx) & exists(me_y + sign * (b - 1), ny))
                def _():
                    act(a, b)

    def column_copy(step, g):
        other = lax.rem(me_y + step, ny)
        return pltpu.make_async_remote_copy(
            src_ref=wpart_ref.at[other, g],
            dst_ref=yland.at[step - 1, g],
            send_sem=ysend.at[step - 1, g],
            recv_sem=yrecv.at[step - 1, g],
            device_id=(me_x, other),
            device_id_type=MESH,
        )

    late = list(range(2, steps))
    kinds = [[0, 1] + late, [1, 0] + late, late + [0, 1], late + [1, 0]]
    orders = [kinds[kind] for kind in KINDS]
    starts = []
    for g in range(groups):
        at = [0]
        for s in range(steps):
            at.append(at[-1] + bits[orders[g][s]] * (nx >> (s + 1)))
        starts.append(at)

    def scatter_copy(g, s):
        half = nx >> (s + 1)
        bit = bits[orders[g][s]]
        away = starts[g][s] + (1 - bit) * half
        return pltpu.make_async_remote_copy(
            src_ref=work.at[g, pl.ds(away, half)],
            dst_ref=xland.at[g, pl.ds(nx - 2 * half, half)],
            send_sem=rsend.at[s, g],
            recv_sem=rrecv.at[s, g],
            device_id=(partners[orders[g][s]], me_y),
            device_id_type=MESH,
        )

    def gather_copy(g, s, landing):
        half = nx >> (s + 1)
        bit = bits[orders[g][s]]
        mine = starts[g][s + 1]
        place = starts[g][s] + (1 - bit) * half if landing else mine
        return pltpu.make_async_remote_copy(
            src_ref=sum_ref.at[g, pl.ds(mine, half)],
            dst_ref=sum_ref.at[g, pl.ds(place, half)],
            send_sem=gsend.at[s, g],
            recv_sem=grecv.at[s, g],
            device_id=(partners[orders[g][s]], me_y),
            device_id_type=MESH,
        )

    for g in range(groups):
        for step in range(1, ny):
            column_copy(step, g).start()
    sides(lambda a, b: side_copy(a, b).start(), 1)

    def begin(g):
        value = wpart_ref[me_y, g].astype(jnp.float32)
        for step in range(1, ny):
            column_copy(step, g).wait_recv()
            value = value + yland[step - 1, g].astype(jnp.float32)
        work[g] = value.astype(work.dtype)
        scatter_copy(g, 0).start()

    def scatter(g, s):
        half = nx >> (s + 1)
        scatter_copy(g, s).wait_recv()
        keep = pl.ds(starts[g][s + 1], half)
        value = work[g, keep].astype(jnp.float32) + xland[g, pl.ds(nx - 2 * half, half)].astype(
            jnp.float32
        )
        if s < steps - 1:
            work[g, keep] = value.astype(work.dtype)
            scatter_copy(g, s + 1).start()
        else:
            sum_ref[g, keep] = value.astype(sum_ref.dtype)
            gather_copy(g, s, False).start()

    def gather(g, s):
        gather_copy(g, s, True).wait_recv()
        if s > 0:
            gather_copy(g, s - 1, False).start()

    events = []
    for g in range(groups):
        events.append((WAVES[g] * STAGGER, g, functools.partial(begin, g)))
        for s in range(steps):
            events.append((WAVES[g] * STAGGER + s + 1, g, functools.partial(scatter, g, s)))
            events.append(
                (WAVES[g] * STAGGER + 2 * steps - s, g, functools.partial(gather, g, s))
            )
    events.sort(key=lambda event: event[:2])
    first = [event[2] for event in events if event[0] < HALO_AT]
    rest = [event[2] for event in events if event[0] >= HALO_AT]
    for event in first:
        event()

    returned_ref[...] = jnp.zeros(returned_ref.shape, jnp.float32)
    for b in (0, 2):

        @pl.when(exists(me_y + 1 - b, ny))
        def _():
            side_copy(1, b).wait_recv()
            returned_ref[...] += side_land[1, b // 2].astype(jnp.float32)

    for a in (0, 2):

        @pl.when(exists(me_x + a - 1, nx))
        def _():
            for b in (0, 2):
                missing = jnp.logical_not(exists(me_y + 1 - b, ny))

                @pl.when(missing)
                def _():
                    side_land[a, b // 2] = jnp.zeros(side_land.shape[2:], side_land.dtype)

                @pl.when(jnp.logical_not(missing))
                def _():
                    side_copy(a, b).wait_recv()

            column[a // 2] = (
                borrowed_ref[3 * a + 1].astype(jnp.float32)
                + side_land[a, 0].astype(jnp.float32)
                + side_land[a, 1].astype(jnp.float32)
            ).astype(column.dtype)
            back_copy(a).start()

    for event in rest:
        event()

    for a in (0, 2):

        @pl.when(exists(me_x + 1 - a, nx))
        def _():
            back_copy(a).wait_recv()
            returned_ref[...] += x_land[a // 2].astype(jnp.float32)

    for g in range(groups):
        for step in range(1, ny):
            column_copy(step, g).wait_send()
        for s in range(steps):
            scatter_copy(g, s).wait_send()
            gather_copy(g, s, False).wait_send()
    sides(lambda a, b: side_copy(a, b).wait_send(), 1)
    for a in (0, 2):

        @pl.when(exists(me_x + a - 1, nx))
        def _():
            back_copy(a).wait_send()


def layer_kernel(
    source_ref,
    target_ref,
    count_ref,
    feats_ref,
    halo_ref,
    weight_ref,
    bias_ref,
    cot_ref,
    out_ref,
    own_ref,
    borrowed_ref,
    dpre_ref,
    turned_ref,
    table,
    pre,
    grad,
    out,
    osem,
):
    blocks, rows, width = feats_ref.shape
    slots = source_ref.shape[0]
    kvol = weight_ref.shape[0]
    total_blocks = table.shape[0]
    shared_count = halo_ref.shape[1]
    f32 = jnp.float32
    places = [(b, feats_ref.at[b]) for b in range(blocks)]
    at = blocks
    for d in range(9):
        if d != 4:
            for s in range(shared_count):
                places.append((at, halo_ref.at[d, s]))
                at += 1
    for t, ref in places:
        value = ref[...]
        table[t] = value
        turned_ref[t] = value.T
    for b in range(blocks):
        pre[b] = jnp.broadcast_to(bias_ref[...], (rows, width))
    for t in range(total_blocks):
        grad[t] = jnp.zeros((rows, width), f32)
    pre[blocks] = jnp.zeros((rows, width), f32)
    grad[total_blocks] = jnp.zeros((rows, width), f32)
    dpre_ref[blocks] = jnp.zeros((rows, width), dpre_ref.dtype)

    def forward(k, carry):
        live = count_ref[k]
        taken, targets = [], []
        for q in range(slots):
            taken.append(table[jnp.where(q < live, source_ref[q, k], 0)])
            targets.append(jnp.where(q < live, target_ref[q, k], blocks))
        made = jnp.dot(jnp.concatenate(taken, axis=0), weight_ref[k], preferred_element_type=f32)
        for q, target in enumerate(targets):
            pre[target] += made[q * rows : (q + 1) * rows]
        return carry

    lax.fori_loop(0, kvol, forward, 0, unroll=UNROLL)

    def activate(b, carry):
        value = pre[b]
        sig = jax.nn.sigmoid(value)
        out[b] = (value * sig).astype(out.dtype)
        dpre_ref[b] = (cot_ref[b].astype(f32) * sig * (1.0 + value * (1.0 - sig))).astype(
            dpre_ref.dtype
        )
        return carry

    lax.fori_loop(0, blocks, activate, 0)
    keep = pltpu.make_async_copy(out, out_ref, osem)
    keep.start()

    def backward(k, carry):
        live = count_ref[k]
        pulled, spread = [], []
        for q in range(slots):
            pulled.append(dpre_ref[jnp.where(q < live, target_ref[q, k], blocks)])
            spread.append(jnp.where(q < live, source_ref[q, k], total_blocks))
        back = lax.dot_general(
            jnp.concatenate(pulled, axis=0),
            weight_ref[k],
            (((1,), (1,)), ((), ())),
            preferred_element_type=f32,
        )
        for q, source in enumerate(spread):
            grad[source] += back[q * rows : (q + 1) * rows]
        return carry

    lax.fori_loop(0, kvol, backward, 0, unroll=UNROLL)
    for b in range(blocks):
        own_ref[b] = grad[b]
    at = blocks
    for d in range(9):
        for s in range(shared_count):
            if d != 4:
                borrowed_ref[d, s] = grad[at].astype(borrowed_ref.dtype)
                at += 1
    keep.wait()


def line_kernel(
    nx,
    ny,
    source_ref,
    target_ref,
    count_ref,
    send_ref,
    turned_ref,
    dpre_ref,
    own_ref,
    borrowed_ref,
    wide_ref,
    feat_ref,
    away,
    sums,
    back,
    work,
    yland,
    full_land,
    half_land,
    land,
    spare,
    side_land,
    column,
    x_land,
    ysend,
    yrecv,
    csend,
    crecv,
    hsend,
    hrecv,
    bsend,
    brecv,
):
    me_x, me_y = lax.axis_index("gx"), lax.axis_index("gy")
    kvol, parts, deep, width = work.shape
    slots = source_ref.shape[0]
    blocks, rows = own_ref.shape[:2]
    f32 = jnp.float32
    bit_x, bit_y, z = lax.rem(me_x, 2), lax.rem(me_x // 2, 2), me_x // 4
    high = z // 2
    beside = {"x": me_x + 1 - 2 * bit_x, "y": me_x + 2 - 4 * bit_y}
    inner = exists(z - 1, 2)
    near = jnp.where(inner, me_x - 4 + 8 * high, me_x + 4 - 8 * high)
    middle = me_x + 4 - 8 * high

    barrier = pltpu.get_barrier_semaphore()
    expected = greet_neighbours(barrier, me_x, me_y, nx, ny) + greet_column(
        barrier, me_x, me_y, ny
    )
    for device in (beside["x"], beside["y"], near):
        pl.semaphore_signal(barrier, inc=1, device_id=(device, me_y), device_id_type=MESH)

    @pl.when(inner)
    def _():
        pl.semaphore_signal(barrier, inc=1, device_id=(middle, me_y), device_id_type=MESH)

    pl.semaphore_wait(barrier, expected + 3 + inner.astype(jnp.int32))

    def side_copy(a, b):
        return pltpu.make_async_remote_copy(
            src_ref=borrowed_ref.at[3 * a + b],
            dst_ref=side_land.at[a, b // 2],
            send_sem=hsend.at[a, b // 2],
            recv_sem=hrecv.at[a, b // 2],
            device_id=(me_x, me_y + b - 1),
            device_id_type=MESH,
        )

    def back_copy(a):
        return pltpu.make_async_remote_copy(
            src_ref=column.at[a // 2],
            dst_ref=x_land.at[a // 2],
            send_sem=bsend.at[a // 2],
            recv_sem=brecv.at[a // 2],
            device_id=(me_x + a - 1, me_y),
            device_id_type=MESH,
        )

    def sides(act, sign):
        for a in range(3):
            for b in (0, 2):

                @pl.when(exists(me_x + a - 1, nx) & exists(me_y + sign * (b - 1), ny))
                def _():
                    act(a, b)

    def column_copy(step, g):
        other = lax.rem(me_y + step, ny)
        return pltpu.make_async_remote_copy(
            src_ref=away.at[step - 1, g],
            dst_ref=yland.at[step - 1, g],
            send_sem=ysend.at[step - 1],
            recv_sem=yrecv.at[step - 1, g],
            device_id=(me_x, other),
            device_id_type=MESH,
        )

    def make(g, carry):
        live = count_ref[g]
        taken, pulled = [], []
        for q in range(slots):
            taken.append(turned_ref[jnp.where(q < live, source_ref[q, g], 0)])
            pulled.append(dpre_ref[jnp.where(q < live, target_ref[q, g], blocks)])
        part = jnp.dot(
            jnp.concatenate(taken, axis=1),
            jnp.concatenate(pulled, axis=0),
            preferred_element_type=f32,
        ).astype(work.dtype).reshape(ny, parts, deep, width)
        for y in range(ny):
            step = lax.rem(y - me_y + ny, ny)
            for d in range(ny):

                @pl.when(step == d)
                def _():
                    if d == 0:
                        work[g] = part[y]
                    else:
                        away[d - 1, g] = part[y]

        for step in range(1, ny):
            column_copy(step, g).start()
        return carry

    sides(lambda a, b: side_copy(a, b).start(), 1)

    def give_back():
        back[...] = jnp.zeros(back.shape, f32)
        for b in (0, 2):

            @pl.when(exists(me_y + 1 - b, ny))
            def _():
                side_copy(1, b).wait_recv()
                back[...] += side_land[1, b // 2].astype(f32)

        for a in (0, 2):

            @pl.when(exists(me_x + a - 1, nx))
            def _():
                for b in (0, 2):
                    missing = jnp.logical_not(exists(me_y + 1 - b, ny))

                    @pl.when(missing)
                    def _():
                        side_land[a, b // 2] = jnp.zeros(side_land.shape[2:], side_land.dtype)

                    @pl.when(jnp.logical_not(missing))
                    def _():
                        side_copy(a, b).wait_recv()

                column[a // 2] = (
                    borrowed_ref[3 * a + 1].astype(f32)
                    + side_land[a, 0].astype(f32)
                    + side_land[a, 1].astype(f32)
                ).astype(column.dtype)
                back_copy(a).start()

    def take_back():
        for a in (0, 2):

            @pl.when(exists(me_x + 1 - a, nx))
            def _():
                back_copy(a).wait_recv()
                back[...] += x_land[a // 2].astype(f32)

        for b in range(blocks):
            value = own_ref[b]
            for s in range(back.shape[0]):
                value = value + jnp.where(send_ref[s] == b, back[s], 0.0)
            feat_ref[b] = value.astype(feat_ref.dtype)

    def own_sum(g):
        value = work[g].astype(f32)
        for step in range(1, ny):
            column_copy(step, g).wait_recv()
            value = value + yland[step - 1, g].astype(f32)
        return value

    def first_send(g):
        kind = LINE_KINDS[g]
        if kind[0] == "B":

            @pl.when(jnp.logical_not(inner))
            def _():
                work[g] = own_sum(g).astype(work.dtype)
                copy(g, work.at[g], full_land.at[g], 6, 2, near).start()

        else:
            gone = 2 - 2 * (bit_x if kind[1] == "x" else bit_y)
            work[g] = own_sum(g).astype(work.dtype)
            copy(
                g, work.at[g, pl.ds(gone, 2)], half_land.at[g], 0, 0, beside[kind[1]]
            ).start()

    def copy(g, src, dst, leave, arrive, device):
        return pltpu.make_async_remote_copy(
            src_ref=src,
            dst_ref=dst,
            send_sem=csend.at[leave],
            recv_sem=crecv.at[arrive, g],
            device_id=(device, me_y),
            device_id_type=MESH,
        )

    def program(order, inside):
        sent = {}
        for kind in LINE_KINDS:
            if kind[0] == "A":
                sent[0] = sent.get(0, 0) + parts // 2
            elif not inside:
                sent[6] = sent.get(6, 0) + parts

        def send(g, src, dst, leave, arrive, device):
            copy(g, src, dst, leave, arrive, device).start()
            sent[leave] = sent.get(leave, 0) + math.prod(src.shape[:-2])

        def recv(g, dst, arrive):
            copy(g, dst, dst, 0, arrive, beside["x"]).wait_recv()

        def finish(g):
            wide_ref[g] = sums[g].reshape(parts * deep, width).astype(f32) * (1.0 / rows)

        def along(g, k):
            first = LINE_KINDS[g][1]
            second = "y" if first == "x" else "x"
            bits = {"x": bit_x, "y": bit_y}
            hb, qb = bits[first], bits[second]
            mine, other = 2 * hb + qb, 2 * hb + 1 - qb
            kept, gone = pl.ds(2 * hb, 2), pl.ds(2 - 2 * hb, 2)
            total, ours = sums.at[g], work.at[g]
            if k == 1:
                recv(g, half_land.at[g], 0)
                work[g, kept] = (
                    work[g, kept].astype(f32) + half_land[g].astype(f32)
                ).astype(work.dtype)
                send(g, ours.at[other], land.at[0, g], 1, 1, beside[second])
            elif k == 2:
                recv(g, land.at[0, g], 1)
                work[g, mine] = (
                    work[g, mine].astype(f32) + land[0, g].astype(f32)
                ).astype(work.dtype)
                if not inside:
                    send(g, ours.at[mine], land.at[1, g], 2, 2, near)
            elif k == 3:
                recv(g, land.at[1, g], 2)
                work[g, mine] = (
                    work[g, mine].astype(f32) + land[1, g].astype(f32)
                ).astype(work.dtype)
                send(g, ours.at[mine], land.at[2, g], 3, 3, middle)
            elif k == 4:
                recv(g, land.at[2, g], 3)
                sums[g, mine] = (
                    work[g, mine].astype(f32) + land[2, g].astype(f32)
                ).astype(sums.dtype)
                send(g, total.at[mine], total.at[mine], 2, 2, near)
                send(g, total.at[mine], total.at[mine], 4, 0, beside[second])
            elif k == 5:
                recv(g, total.at[mine], 2)
                send(g, total.at[mine], total.at[mine], 4, 0, beside[second])
            elif k == 6:
                recv(g, total.at[other], 0)
                send(g, total.at[kept], total.at[kept], 5, 4, beside[first])
            elif k == 7:
                recv(g, total.at[gone], 4)
                finish(g)

        def fold(g, k):
            first = LINE_KINDS[g][1]
            second = "y" if first == "x" else "x"
            bits = {"x": bit_x, "y": bit_y}
            hb, qb = high, bits[first]
            mine, other = 2 * hb + qb, 2 * hb + 1 - qb
            kept, gone = pl.ds(2 * hb, 2), pl.ds(2 - 2 * hb, 2)
            total, ours = sums.at[g], work.at[g]
            if not inside:
                if k == 6:
                    recv(g, total.at[kept], 2)
                elif k == 7:
                    recv(g, total.at[gone], 3)
                    finish(g)
            elif k == 1:
                value = own_sum(g)
                recv(g, full_land.at[g], 2)
                work[g] = (value + full_land[g].astype(f32)).astype(work.dtype)
                send(g, ours.at[gone], half_land.at[g], 7, 3, middle)
            elif k == 2:
                recv(g, half_land.at[g], 3)
                work[g, kept] = (
                    work[g, kept].astype(f32) + half_land[g].astype(f32)
                ).astype(work.dtype)
                send(g, ours.at[other], land.at[0, g], 1, 0, beside[first])
            elif k == 3:
                recv(g, land.at[0, g], 0)
                work[g, mine] = (
                    work[g, mine].astype(f32) + land[0, g].astype(f32)
                ).astype(work.dtype)
                send(g, ours.at[mine], land.at[1, g], 1, 1, beside[second])
            elif k == 4:
                recv(g, land.at[1, g], 1)
                sums[g, mine] = (
                    work[g, mine].astype(f32) + land[1, g].astype(f32)
                ).astype(sums.dtype)
                send(g, total.at[mine], total.at[mine], 4, 4, beside[first])
            elif k == 5:
                recv(g, total.at[other], 4)
                send(g, total.at[kept], total.at[kept], 8, 2, middle)
                send(g, total.at[kept], total.at[kept], 8, 2, near)
            elif k == 6:
                recv(g, total.at[gone], 2)
                send(g, total.at[gone], total.at[gone], 8, 3, near)
                finish(g)

        for event in order:
            g, k = divmod(event, 10)
            if g == kvol:
                (give_back, take_back)[k]()
            elif LINE_KINDS[g][0] == "B":
                fold(g, k)
            else:
                along(g, k)
        for leave, pieces in sent.items():
            gone = spare.at[pl.ds(0, pieces)]
            copy(0, gone, gone, leave, 0, beside["x"]).wait_send()

    at = 0
    for upto in MAKE_AT:
        lax.fori_loop(at, upto, make, 0)
        for g in range(max(at - MAKE_LEAD, 0), upto - MAKE_LEAD if upto < kvol else kvol):
            first_send(g)
        at = upto

    @pl.when(inner)
    def _():
        program(LINE_ORDERS[0], True)

    @pl.when(jnp.logical_not(inner))
    def _():
        program(LINE_ORDERS[1], False)

    for step in range(1, ny):
        other = lax.rem(me_y + step, ny)
        pltpu.make_async_remote_copy(
            src_ref=away.at[step - 1],
            dst_ref=yland.at[step - 1],
            send_sem=ysend.at[step - 1],
            recv_sem=yrecv.at[step - 1, 0],
            device_id=(me_x, other),
            device_id_type=MESH,
        ).wait_send()
    sides(lambda a, b: side_copy(a, b).wait_send(), 1)
    for a in (0, 2):

        @pl.when(exists(me_x + a - 1, nx))
        def _():
            back_copy(a).wait_send()


def finish_kernel(
    send_ref, total_ref, own_ref, returned_ref, weight_ref, feat_ref, wide, feats, wsem, fsem
):
    chunks = wsem.shape[0]
    kvol, share, width = wide.shape
    per = kvol // chunks
    blocks, rows = own_ref.shape[:2]
    copies = []
    for c in range(chunks):
        at = pl.ds(c * per, per)
        for h in range(width // LANES):
            wide[at, :, h * LANES : (h + 1) * LANES] = total_ref[h, at].reshape(
                per, share, LANES
            ).astype(jnp.float32) * (1.0 / rows)
        copy = pltpu.make_async_copy(wide.at[at], weight_ref.at[at], wsem.at[c])
        copy.start()
        copies.append(copy)
    for b in range(blocks):
        value = own_ref[b]
        for s in range(returned_ref.shape[0]):
            value = value + jnp.where(send_ref[s] == b, returned_ref[s], 0.0)
        feats[b] = value.astype(feats.dtype)
        copy = pltpu.make_async_copy(feats.at[b], feat_ref.at[b], fsem.at[b])
        copy.start()
        copies.append(copy)
    for copy in copies:
        copy.wait()


def store_kernel(wide_ref, feat_ref, weight_out, feat_out, sem):
    chunks = sem.shape[0] - 1
    per = wide_ref.shape[0] // chunks
    copies = [pltpu.make_async_copy(feat_ref, feat_out, sem.at[chunks])]
    for c in range(chunks):
        at = pl.ds(c * per, per)
        copies.append(pltpu.make_async_copy(wide_ref.at[at], weight_out.at[at], sem.at[c]))
    for copy in copies:
        copy.start()
    for copy in copies:
        copy.wait()


def on_device(
    nx,
    ny,
    features,
    kernel_weight,
    channel_bias,
    send_list,
    rule_source,
    rule_target,
    live_counts,
    out_grad,
):
    feats = features[0, 0]
    blocks, rows, width = feats.shape
    shared = send_list[0, 0]
    shared_count = shared.shape[0]
    kvol, slots = rule_source.shape[2:]
    share = kernel_weight.shape[1]
    bf16, f32 = jnp.bfloat16, jnp.float32
    shape = jax.ShapeDtypeStruct
    vmem = pl.BlockSpec(memory_space=VMEM)
    smem = pl.BlockSpec(memory_space=SMEM)
    hbm = pl.BlockSpec(memory_space=pltpu.HBM)
    dma = pltpu.SemaphoreType.DMA
    squares = 9

    halo, full = pl.pallas_call(
        functools.partial(exchange_kernel, nx, ny),
        out_shape=(
            shape((squares, shared_count, rows, width), bf16),
            shape((kvol, ny, share, width), bf16),
        ),
        in_specs=[smem, hbm, hbm],
        out_specs=(vmem, vmem),
        scratch_shapes=[
            VMEM((blocks, rows, width), bf16),
            dma((2,)),
            dma((2,)),
            dma((2,)),
            dma((3, 2)),
            dma((3, 2)),
            dma((ny,)),
            dma((ny,)),
        ],
        compiler_params=pltpu.CompilerParams(
            collective_id=0, has_side_effects=True, vmem_limit_bytes=EXCHANGE_BYTES
        ),
    )(shared, feats, kernel_weight)

    total_blocks = blocks + (squares - 1) * shared_count
    if nx == 4 * LINE_LENGTH and kvol == len(LINE_KINDS):
        rules = (rule_source[0, 0].T, rule_target[0, 0].T, live_counts.reshape(-1))
        boundary = (shared_count, rows, width)
        quarters = (4, share // 4, width)
        outputs, own, borrowed, dpre, turned = pl.pallas_call(
            layer_kernel,
            out_shape=(
                shape((blocks, rows, width), bf16),
                shape((blocks, rows, width), f32),
                shape((squares,) + boundary, bf16),
                shape((blocks + 1, rows, width), bf16),
                shape((total_blocks, width, rows), bf16),
            ),
            in_specs=[smem, smem, smem, vmem, vmem, vmem, vmem, vmem],
            out_specs=(hbm, vmem, vmem, vmem, vmem),
            scratch_shapes=[
                VMEM((total_blocks, rows, width), bf16),
                VMEM((blocks + 1, rows, width), f32),
                VMEM((total_blocks + 1, rows, width), f32),
                VMEM((blocks, rows, width), bf16),
                dma(()),
            ],
            compiler_params=pltpu.CompilerParams(vmem_limit_bytes=VMEM_BYTES),
        )(
            *rules,
            feats,
            halo,
            full.reshape(kvol, width, width),
            channel_bias.reshape(1, width),
            out_grad[0, 0],
        )
        wide, feat = pl.pallas_call(
            functools.partial(line_kernel, nx, ny),
            out_shape=(shape((kvol, share, width), f32), shape((blocks, rows, width), bf16)),
            in_specs=[smem, smem, smem, smem, vmem, vmem, vmem, vmem],
            out_specs=(vmem, vmem),
            scratch_shapes=[
                VMEM((max(ny - 1, 1), kvol) + quarters, bf16),
                VMEM((kvol,) + quarters, bf16),
                VMEM(boundary, f32),
                VMEM((kvol,) + quarters, bf16),
                VMEM((max(ny - 1, 1), kvol) + quarters, bf16),
                VMEM((kvol,) + quarters, bf16),
                VMEM((kvol, 2) + quarters[1:], bf16),
                VMEM((3, kvol) + quarters[1:], bf16),
                VMEM((8 * kvol,) + quarters[1:], bf16),
                VMEM((3, 2) + boundary, bf16),
                VMEM((2,) + boundary, bf16),
                VMEM((2,) + boundary, bf16),
                dma((max(ny - 1, 1),)),
                dma((max(ny - 1, 1), kvol)),
                dma((9,)),
                dma((5, kvol)),
                dma((3, 2)),
                dma((3, 2)),
                dma((2,)),
                dma((2,)),
            ],
            compiler_params=pltpu.CompilerParams(
                collective_id=2, has_side_effects=True, vmem_limit_bytes=LINE_BYTES
            ),
        )(*rules, shared, turned, dpre, own, borrowed)
        chunks = max(c for c in range(1, 10) if kvol % c == 0)
        weight_grad, feat_grad = pl.pallas_call(
            store_kernel,
            out_shape=(shape((kvol, share, width), f32), shape((blocks, rows, width), bf16)),
            in_specs=[vmem, vmem],
            out_specs=(hbm, hbm),
            scratch_shapes=[dma((chunks + 1,))],
            compiler_params=pltpu.CompilerParams(vmem_limit_bytes=VMEM_BYTES),
        )(wide, feat)
        return (outputs[None, None], feat_grad[None, None], weight_grad)

    used = (width // LANES) * kvol * (share // TILE)
    groups = len(KINDS)
    unit = groups * nx
    tiles = -(-used // unit) * unit
    depth = tiles // unit
    outputs, own, borrowed, wpart = pl.pallas_call(
        compute_kernel,
        out_shape=(
            shape((blocks, rows, width), bf16),
            shape((blocks, rows, width), f32),
            shape((squares, shared_count, rows, width), bf16),
            shape((ny, tiles, TILE, LANES), bf16),
        ),
        in_specs=[smem, smem, smem, vmem, vmem, vmem, vmem, vmem],
        out_specs=(vmem, vmem, vmem, vmem),
        scratch_shapes=[
            VMEM((total_blocks, rows, width), bf16),
            VMEM((total_blocks, width, rows), bf16),
            VMEM((blocks + 1, rows, width), f32),
            VMEM((blocks + 1, rows, width), bf16),
            VMEM((total_blocks + 1, rows, width), f32),
        ],
        compiler_params=pltpu.CompilerParams(vmem_limit_bytes=VMEM_BYTES),
    )(
        rule_source[0, 0].T,
        rule_target[0, 0].T,
        live_counts.reshape(-1),
        feats,
        halo,
        full.reshape(kvol, width, width),
        channel_bias.reshape(1, width),
        out_grad[0, 0],
    )

    steps = nx.bit_length() - 1
    block = (depth, TILE, LANES)
    boundary = (shared_count, rows, width)
    total, returned = pl.pallas_call(
        functools.partial(reduce_kernel, nx, ny),
        out_shape=(
            shape((groups, nx) + block, bf16),
            shape(boundary, f32),
        ),
        in_specs=[vmem, vmem],
        out_specs=(vmem, vmem),
        scratch_shapes=[
            VMEM((groups, nx) + block, bf16),
            VMEM((max(ny - 1, 1), groups, nx) + block, bf16),
            VMEM((groups, nx) + block, bf16),
            VMEM((3, 2) + boundary, bf16),
            VMEM((2,) + boundary, bf16),
            VMEM((2,) + boundary, bf16),
            dma((max(ny - 1, 1), groups)),
            dma((max(ny - 1, 1), groups)),
            dma((steps, groups)),
            dma((steps, groups)),
            dma((steps, groups)),
            dma((steps, groups)),
            dma((3, 2)),
            dma((3, 2)),
            dma((2,)),
            dma((2,)),
        ],
        compiler_params=pltpu.CompilerParams(
            collective_id=1, has_side_effects=True, vmem_limit_bytes=VMEM_BYTES
        ),
    )(wpart.reshape((ny, groups, nx) + block), borrowed)

    halves, share_tiles = width // LANES, share // TILE
    chunks = max(c for c in range(1, 10) if kvol % c == 0)
    weight_grad, feat_grad = pl.pallas_call(
        finish_kernel,
        out_shape=(shape((kvol, share, width), f32), shape((blocks, rows, width), bf16)),
        in_specs=[smem, vmem, vmem, vmem],
        out_specs=(hbm, hbm),
        scratch_shapes=[
            VMEM((kvol, share, width), f32),
            VMEM((blocks, rows, width), bf16),
            dma((chunks,)),
            dma((blocks,)),
        ],
        compiler_params=pltpu.CompilerParams(vmem_limit_bytes=VMEM_BYTES),
    )(
        shared,
        total.reshape(tiles, TILE, LANES)[:used].reshape(halves, kvol, share_tiles, TILE, LANES),
        own,
        returned,
    )
    return (outputs[None, None], feat_grad[None, None], weight_grad)


def solution(mesh):
    return jax.shard_map(
        functools.partial(on_device, mesh.shape["gx"], mesh.shape["gy"]),
        mesh=mesh,
        in_specs=(
            P("gx", "gy", None, None, None),
            P(None, "gy", None),
            P(),
            P("gx", "gy", None),
            P("gx", "gy", None, None),
            P("gx", "gy", None, None),
            P("gx", "gy", None),
            P("gx", "gy", None, None, None),
        ),
        out_specs=(
            P("gx", "gy", None, None, None),
            P("gx", "gy", None, None, None),
            P(None, "gy", None),
        ),
        check_vma=False,
    )
```

```python
import functools
import math

import jax
import jax.numpy as jnp
from jax import lax
from jax.experimental import pallas as pl
from jax.experimental.pallas import tpu as pltpu
from jax.sharding import PartitionSpec as P

MESH = pl.DeviceIdType.MESH
VMEM = pltpu.VMEM
SMEM = pltpu.SMEM
LANES = 128
TILE = 16
KINDS = (2, 0, 1, 3, 0, 1, 0, 1, 0)
WAVES = (0,) * 9
STAGGER = 1
HALO_AT = 4
UNROLL = 9
VMEM_BYTES = 28 * 1024 * 1024
EXCHANGE_BYTES = 28 * 1024 * 1024
LINE_BYTES = 28 * 1024 * 1024
GATHER_BYTES = 40 * 1024 * 1024
LAYER_BYTES = 28 * 1024 * 1024
LINE_LENGTH = 4
MAKE_STEP = 4
MAKE_LEAD = 3

LINE_KINDS = (
    'Ax', 'Ay', 'Ax', 'By', 'Ay', 'Ax', 'Ay', 'Ax', 'By',
    'Ay', 'Ax', 'Ay', 'Ax', 'Ay', 'Ax', 'By', 'Ay', 'Ax',
    'Bx', 'Ay', 'Ax', 'Ax', 'By', 'Ay', 'Ax', 'Ay', 'By',
)
LINE_ORDERS = (
(
    0, 10, 20, 40, 50, 60, 70, 90, 100, 110, 120, 130, 140, 1, 31, 160,
    170, 190, 200, 81, 21, 210, 230, 240, 51, 2, 151, 250, 11, 41, 71, 61,
    101, 181, 91, 121, 22, 111, 141, 131, 171, 161, 201, 52, 221, 191, 211, 231,
    241, 12, 251, 32, 42, 72, 270, 82, 62, 102, 261, 152, 92, 122, 112, 142,
    3, 132, 172, 23, 162, 202, 192, 53, 212, 232, 242, 13, 252, 43, 73, 103,
    222, 123, 262, 4, 143, 24, 173, 54, 63, 93, 14, 33, 203, 44, 83, 213,
    74, 153, 113, 104, 182, 243, 124, 223, 133, 144, 263, 163, 174, 193, 64, 233,
    271, 94, 253, 34, 204, 84, 214, 6, 154, 114, 183, 244, 224, 134, 264, 164,
    194, 234, 254, 35, 16, 26, 85, 7, 46, 56, 155, 66, 184, 76, 225, 96,
    106, 265, 116, 17, 126, 27, 136, 36, 47, 146, 57, 166, 86, 185, 67, 176,
    196, 156, 77, 97, 206, 236, 107, 117, 216, 256, 226, 127, 137, 246, 266, 147,
    167, 186, 177, 197, 207, 237, 217, 257, 247,
),
(
    0, 10, 30, 20, 40, 50, 60, 80, 70, 90, 100, 110, 150, 120, 130, 140,
    1, 180, 160, 170, 190, 200, 220, 21, 210, 230, 240, 51, 260, 250, 11, 41,
    71, 61, 101, 91, 2, 121, 111, 22, 141, 131, 171, 161, 201, 52, 191, 211,
    231, 241, 12, 251, 270, 42, 72, 102, 122, 142, 172, 62, 92, 202, 212, 112,
    242, 132, 162, 192, 232, 252, 5, 25, 55, 271, 15, 45, 75, 105, 125, 6,
    145, 175, 26, 65, 16, 95, 56, 205, 215, 115, 245, 135, 46, 7, 165, 195,
    27, 235, 66, 255, 17, 76, 96, 36, 57, 106, 116, 86, 126, 136, 156, 47,
    146, 166, 226, 67, 176, 196, 266, 77, 97, 206, 236, 37, 107, 117, 216, 256,
    87, 127, 137, 246, 157, 147, 167, 186, 177, 197, 227, 207, 237, 267, 217, 257,
    187, 247,
),
)


def greet_neighbours(barrier, me_x, me_y, nx, ny):
    total = 0
    for sx, sy in ((-1, 0), (1, 0), (0, -1), (0, 1)):
        x, y = me_x + sx, me_y + sy
        there = (x >= 0) & (x < nx) & (y >= 0) & (y < ny)

        @pl.when(there)
        def _():
            pl.semaphore_signal(barrier, inc=1, device_id=(x, y), device_id_type=MESH)

        total = total + there.astype(jnp.int32)
    return total


def greet_column(barrier, me_x, me_y, ny):
    for step in range(1, ny):
        pl.semaphore_signal(
            barrier, inc=1, device_id=(me_x, lax.rem(me_y + step, ny)), device_id_type=MESH
        )
    return ny - 1


def exists(index, count):
    return (index >= 0) & (index < count)


def exchange_kernel(
    nx, ny, send_ref, feats_ref, weight_ref, halo_ref, full_ref, feats, lsem, xsend, xrecv, hsend, hrecv, wsend, wrecv
):
    me_x, me_y = lax.axis_index("gx"), lax.axis_index("gy")
    barrier = pltpu.get_barrier_semaphore()
    expected = greet_neighbours(barrier, me_x, me_y, nx, ny) + greet_column(
        barrier, me_x, me_y, ny
    )
    load = pltpu.make_async_copy(feats_ref, feats, lsem.at[0])
    load.start()
    keep = pltpu.make_async_copy(weight_ref, full_ref.at[:, me_y], lsem.at[1])
    keep.start()
    load.wait()
    for s in range(halo_ref.shape[1]):
        halo_ref[4, s] = feats[send_ref[s]]
    pl.semaphore_wait(barrier, expected)

    def x_copy(a, device_x):
        return pltpu.make_async_remote_copy(
            src_ref=halo_ref.at[4],
            dst_ref=halo_ref.at[3 * a + 1],
            send_sem=xsend.at[a // 2],
            recv_sem=xrecv.at[a // 2],
            device_id=(device_x, me_y),
            device_id_type=MESH,
        )

    def y_copy(a, b, device_y):
        return pltpu.make_async_remote_copy(
            src_ref=halo_ref.at[3 * a + 1],
            dst_ref=halo_ref.at[3 * a + b],
            send_sem=hsend.at[a, b // 2],
            recv_sem=hrecv.at[a, b // 2],
            device_id=(me_x, device_y),
            device_id_type=MESH,
        )

    def weight_copy(step, owner):
        return pltpu.make_async_remote_copy(
            src_ref=weight_ref,
            dst_ref=full_ref.at[:, owner],
            send_sem=wsend.at[step],
            recv_sem=wrecv.at[step],
            device_id=(me_x, lax.rem(me_y + step, ny)),
            device_id_type=MESH,
        )

    def to_column(a, act):
        for b in (0, 2):
            target = me_y + 1 - b

            @pl.when(exists(target, ny))
            def _():
                act(y_copy(a, b, target))

    for a in (0, 2):
        target = me_x + 1 - a

        @pl.when(exists(target, nx))
        def _():
            x_copy(a, target).start()

    to_column(1, lambda copy: copy.start())
    for step in range(1, ny):
        weight_copy(step, me_y).start()
    blank = jnp.zeros(halo_ref.shape[1:], halo_ref.dtype)
    for a in (0, 2):
        here = exists(me_x + a - 1, nx)

        @pl.when(jnp.logical_not(here))
        def _():
            halo_ref[3 * a + 1] = blank

        @pl.when(here)
        def _():
            x_copy(a, me_x + a - 1).wait_recv()
            to_column(a, lambda copy: copy.start())

    for a in range(3):
        for b in (0, 2):
            there = exists(me_x + a - 1, nx) & exists(me_y + b - 1, ny)

            @pl.when(jnp.logical_not(there))
            def _():
                halo_ref[3 * a + b] = blank

            @pl.when(there)
            def _():
                y_copy(a, b, me_y + b - 1).wait_recv()

        @pl.when(exists(me_x + a - 1, nx))
        def _():
            to_column(a, lambda copy: copy.wait_send())

    for a in (0, 2):
        target = me_x + 1 - a

        @pl.when(exists(target, nx))
        def _():
            x_copy(a, target).wait_send()

    for step in range(1, ny):
        weight_copy(step, lax.rem(me_y - step + ny, ny)).wait_recv()
        weight_copy(step, me_y).wait_send()
    keep.wait()


def compute_kernel(
    source_ref,
    target_ref,
    count_ref,
    feats_ref,
    halo_ref,
    weight_ref,
    bias_ref,
    cot_ref,
    out_ref,
    own_ref,
    borrowed_ref,
    wpart_ref,
    table,
    turned,
    pre,
    dpre,
    grad,
):
    blocks, rows, width = feats_ref.shape
    slots = source_ref.shape[0]
    kvol = weight_ref.shape[0]
    total_blocks = grad.shape[0] - 1
    shared_count = halo_ref.shape[1]
    ny, tiles = wpart_ref.shape[:2]
    share = width // ny
    share_tiles = share // TILE
    places = [(b, feats_ref.at[b]) for b in range(blocks)]
    at = blocks
    for d in range(9):
        if d != 4:
            for s in range(shared_count):
                places.append((at, halo_ref.at[d, s]))
                at += 1
    for t, ref in places:
        value = ref[...]
        table[t] = value
        turned[t] = value.T
    for b in range(blocks):
        pre[b] = jnp.broadcast_to(bias_ref[...], (rows, width))
    for t in range(total_blocks):
        grad[t] = jnp.zeros((rows, width), jnp.float32)
    pre[blocks] = jnp.zeros((rows, width), jnp.float32)
    grad[total_blocks] = jnp.zeros((rows, width), jnp.float32)
    dpre[blocks] = jnp.zeros((rows, width), dpre.dtype)

    def rules(k):
        live = count_ref[k]
        sources = [source_ref[q, k] for q in range(slots)]
        targets = [target_ref[q, k] for q in range(slots)]
        reads = [jnp.where(q < live, v, 0) for q, v in enumerate(sources)]
        spread = [jnp.where(q < live, v, total_blocks) for q, v in enumerate(sources)]
        targets = [jnp.where(q < live, v, blocks) for q, v in enumerate(targets)]
        return reads, spread, targets

    def forward(k, carry):
        reads, _, targets = rules(k)
        taken = jnp.concatenate([table[s] for s in reads], axis=0)
        made = jnp.dot(taken, weight_ref[k], preferred_element_type=jnp.float32)
        for q, target in enumerate(targets):
            pre[target] += made[q * rows : (q + 1) * rows]
        return carry

    lax.fori_loop(0, kvol, forward, 0, unroll=UNROLL)

    def activate(b, carry):
        value = pre[b]
        sig = jax.nn.sigmoid(value)
        out_ref[b] = (value * sig).astype(out_ref.dtype)
        dpre[b] = (cot_ref[b].astype(jnp.float32) * sig * (1.0 + value * (1.0 - sig))).astype(
            dpre.dtype
        )
        return carry

    lax.fori_loop(0, blocks, activate, 0)

    filled = 2 * kvol * share_tiles
    if filled < tiles:
        for y in range(ny):
            wpart_ref[y, filled:] = jnp.zeros((tiles - filled, TILE, LANES), wpart_ref.dtype)

    def backward(k, carry):
        reads, spread, targets = rules(k)
        pulled = jnp.concatenate([dpre[t] for t in targets], axis=0)
        taken = jnp.concatenate([turned[s] for s in reads], axis=1)
        part = jnp.dot(taken, pulled, preferred_element_type=jnp.float32).astype(wpart_ref.dtype)
        for y in range(ny):
            for h in range(width // LANES):
                piece = part[y * share : (y + 1) * share, h * LANES : (h + 1) * LANES]
                wpart_ref[y, pl.ds((h * kvol + k) * share_tiles, share_tiles)] = piece.reshape(
                    share_tiles, TILE, LANES
                )
        back = lax.dot_general(
            pulled, weight_ref[k], (((1,), (1,)), ((), ())), preferred_element_type=jnp.float32
        )
        for q, source in enumerate(spread):
            grad[source] += back[q * rows : (q + 1) * rows]
        return carry

    lax.fori_loop(0, kvol, backward, 0, unroll=UNROLL)
    for b in range(blocks):
        own_ref[b] = grad[b]
    at = blocks
    for d in range(9):
        for s in range(shared_count):
            if d == 4:
                borrowed_ref[d, s] = jnp.zeros((rows, width), borrowed_ref.dtype)
            else:
                borrowed_ref[d, s] = grad[at].astype(borrowed_ref.dtype)
                at += 1


def reduce_kernel(
    nx,
    ny,
    wpart_ref,
    borrowed_ref,
    sum_ref,
    returned_ref,
    work,
    yland,
    xland,
    side_land,
    column,
    x_land,
    ysend,
    yrecv,
    rsend,
    rrecv,
    gsend,
    grecv,
    hsend,
    hrecv,
    bsend,
    brecv,
):
    me_x, me_y = lax.axis_index("gx"), lax.axis_index("gy")
    groups = work.shape[0]
    steps = nx.bit_length() - 1
    bits = [lax.rem(me_x // (1 << b), 2) for b in range(steps)]
    partners = [me_x + (1 - 2 * bits[b]) * (1 << b) for b in range(steps)]

    barrier = pltpu.get_barrier_semaphore()
    expected = greet_neighbours(barrier, me_x, me_y, nx, ny) + greet_column(
        barrier, me_x, me_y, ny
    )
    for b in range(steps):
        pl.semaphore_signal(barrier, inc=1, device_id=(partners[b], me_y), device_id_type=MESH)
    pl.semaphore_wait(barrier, expected + steps)

    def side_copy(a, b):
        return pltpu.make_async_remote_copy(
            src_ref=borrowed_ref.at[3 * a + b],
            dst_ref=side_land.at[a, b // 2],
            send_sem=hsend.at[a, b // 2],
            recv_sem=hrecv.at[a, b // 2],
            device_id=(me_x, me_y + b - 1),
            device_id_type=MESH,
        )

    def back_copy(a):
        return pltpu.make_async_remote_copy(
            src_ref=column.at[a // 2],
            dst_ref=x_land.at[a // 2],
            send_sem=bsend.at[a // 2],
            recv_sem=brecv.at[a // 2],
            device_id=(me_x + a - 1, me_y),
            device_id_type=MESH,
        )

    def sides(act, sign):
        for a in range(3):
            for b in (0, 2):

                @pl.when(exists(me_x + a - 1, nx) & exists(me_y + sign * (b - 1), ny))
                def _():
                    act(a, b)

    def column_copy(step, g):
        other = lax.rem(me_y + step, ny)
        return pltpu.make_async_remote_copy(
            src_ref=wpart_ref.at[other, g],
            dst_ref=yland.at[step - 1, g],
            send_sem=ysend.at[step - 1, g],
            recv_sem=yrecv.at[step - 1, g],
            device_id=(me_x, other),
            device_id_type=MESH,
        )

    late = list(range(2, steps))
    kinds = [[0, 1] + late, [1, 0] + late, late + [0, 1], late + [1, 0]]
    orders = [kinds[kind] for kind in KINDS]
    starts = []
    for g in range(groups):
        at = [0]
        for s in range(steps):
            at.append(at[-1] + bits[orders[g][s]] * (nx >> (s + 1)))
        starts.append(at)

    def scatter_copy(g, s):
        half = nx >> (s + 1)
        bit = bits[orders[g][s]]
        away = starts[g][s] + (1 - bit) * half
        return pltpu.make_async_remote_copy(
            src_ref=work.at[g, pl.ds(away, half)],
            dst_ref=xland.at[g, pl.ds(nx - 2 * half, half)],
            send_sem=rsend.at[s, g],
            recv_sem=rrecv.at[s, g],
            device_id=(partners[orders[g][s]], me_y),
            device_id_type=MESH,
        )

    def gather_copy(g, s, landing):
        half = nx >> (s + 1)
        bit = bits[orders[g][s]]
        mine = starts[g][s + 1]
        place = starts[g][s] + (1 - bit) * half if landing else mine
        return pltpu.make_async_remote_copy(
            src_ref=sum_ref.at[g, pl.ds(mine, half)],
            dst_ref=sum_ref.at[g, pl.ds(place, half)],
            send_sem=gsend.at[s, g],
            recv_sem=grecv.at[s, g],
            device_id=(partners[orders[g][s]], me_y),
            device_id_type=MESH,
        )

    for g in range(groups):
        for step in range(1, ny):
            column_copy(step, g).start()
    sides(lambda a, b: side_copy(a, b).start(), 1)

    def begin(g):
        value = wpart_ref[me_y, g].astype(jnp.float32)
        for step in range(1, ny):
            column_copy(step, g).wait_recv()
            value = value + yland[step - 1, g].astype(jnp.float32)
        work[g] = value.astype(work.dtype)
        scatter_copy(g, 0).start()

    def scatter(g, s):
        half = nx >> (s + 1)
        scatter_copy(g, s).wait_recv()
        keep = pl.ds(starts[g][s + 1], half)
        value = work[g, keep].astype(jnp.float32) + xland[g, pl.ds(nx - 2 * half, half)].astype(
            jnp.float32
        )
        if s < steps - 1:
            work[g, keep] = value.astype(work.dtype)
            scatter_copy(g, s + 1).start()
        else:
            sum_ref[g, keep] = value.astype(sum_ref.dtype)
            gather_copy(g, s, False).start()

    def gather(g, s):
        gather_copy(g, s, True).wait_recv()
        if s > 0:
            gather_copy(g, s - 1, False).start()

    events = []
    for g in range(groups):
        events.append((WAVES[g] * STAGGER, g, functools.partial(begin, g)))
        for s in range(steps):
            events.append((WAVES[g] * STAGGER + s + 1, g, functools.partial(scatter, g, s)))
            events.append(
                (WAVES[g] * STAGGER + 2 * steps - s, g, functools.partial(gather, g, s))
            )
    events.sort(key=lambda event: event[:2])
    first = [event[2] for event in events if event[0] < HALO_AT]
    rest = [event[2] for event in events if event[0] >= HALO_AT]
    for event in first:
        event()

    returned_ref[...] = jnp.zeros(returned_ref.shape, jnp.float32)
    for b in (0, 2):

        @pl.when(exists(me_y + 1 - b, ny))
        def _():
            side_copy(1, b).wait_recv()
            returned_ref[...] += side_land[1, b // 2].astype(jnp.float32)

    for a in (0, 2):

        @pl.when(exists(me_x + a - 1, nx))
        def _():
            for b in (0, 2):
                missing = jnp.logical_not(exists(me_y + 1 - b, ny))

                @pl.when(missing)
                def _():
                    side_land[a, b // 2] = jnp.zeros(side_land.shape[2:], side_land.dtype)

                @pl.when(jnp.logical_not(missing))
                def _():
                    side_copy(a, b).wait_recv()

            column[a // 2] = (
                borrowed_ref[3 * a + 1].astype(jnp.float32)
                + side_land[a, 0].astype(jnp.float32)
                + side_land[a, 1].astype(jnp.float32)
            ).astype(column.dtype)
            back_copy(a).start()

    for event in rest:
        event()

    for a in (0, 2):

        @pl.when(exists(me_x + 1 - a, nx))
        def _():
            back_copy(a).wait_recv()
            returned_ref[...] += x_land[a // 2].astype(jnp.float32)

    for g in range(groups):
        for step in range(1, ny):
            column_copy(step, g).wait_send()
        for s in range(steps):
            scatter_copy(g, s).wait_send()
            gather_copy(g, s, False).wait_send()
    sides(lambda a, b: side_copy(a, b).wait_send(), 1)
    for a in (0, 2):

        @pl.when(exists(me_x + a - 1, nx))
        def _():
            back_copy(a).wait_send()


def gather_kernel(
    nx,
    ny,
    send_in,
    feats_ref,
    weight_ref,
    bias_ref,
    table_ref,
    turned_ref,
    full_ref,
    pre_ref,
    grad_ref,
    send_ref,
    own,
    stage,
    bias,
    lsem,
    xsend,
    xrecv,
    hsend,
    hrecv,
    wsend,
    wrecv,
):
    me_x, me_y = lax.axis_index("gx"), lax.axis_index("gy")
    blocks, rows, width = feats_ref.shape
    shared_count = stage.shape[0]
    f32 = jnp.float32
    barrier = pltpu.get_barrier_semaphore()
    expected = greet_neighbours(barrier, me_x, me_y, nx, ny) + greet_column(
        barrier, me_x, me_y, ny
    )
    load = pltpu.make_async_copy(feats_ref, own, lsem.at[0])
    load.start()
    pick = pltpu.make_async_copy(send_in, send_ref, lsem.at[3])
    pick.start()
    file = pltpu.make_async_copy(feats_ref, table_ref.at[pl.ds(0, blocks)], lsem.at[4])
    file.start()
    shift = pltpu.make_async_copy(bias_ref, bias, lsem.at[2])
    shift.start()
    keep = pltpu.make_async_copy(weight_ref, full_ref.at[:, me_y], lsem.at[1])
    keep.start()
    pick.wait()
    load.wait()
    for s in range(shared_count):
        stage[s] = own[send_ref[s]]
    pl.semaphore_wait(barrier, expected)

    def first(a, b):
        d = 3 * a + b
        return blocks + shared_count * (d - (d > 4))

    def place(a, b):
        return table_ref.at[pl.ds(first(a, b), shared_count)]

    def x_copy(a, device_x):
        return pltpu.make_async_remote_copy(
            src_ref=stage,
            dst_ref=place(a, 1),
            send_sem=xsend.at[a // 2],
            recv_sem=xrecv.at[a // 2],
            device_id=(device_x, me_y),
            device_id_type=MESH,
        )

    def y_copy(a, b, device_y):
        return pltpu.make_async_remote_copy(
            src_ref=stage if a == 1 else place(a, 1),
            dst_ref=place(a, b),
            send_sem=hsend.at[a, b // 2],
            recv_sem=hrecv.at[a, b // 2],
            device_id=(me_x, device_y),
            device_id_type=MESH,
        )

    def weight_copy(step, owner):
        return pltpu.make_async_remote_copy(
            src_ref=weight_ref,
            dst_ref=full_ref.at[:, owner],
            send_sem=wsend.at[step],
            recv_sem=wrecv.at[step],
            device_id=(me_x, lax.rem(me_y + step, ny)),
            device_id_type=MESH,
        )

    def to_column(a, act):
        for b in (0, 2):
            target = me_y + 1 - b

            @pl.when(exists(target, ny))
            def _():
                act(y_copy(a, b, target))

    def turn(t, count):
        for at in range(t, t + count):
            turned_ref[at] = table_ref[at].T

    def clear(a, b):
        for at in range(first(a, b), first(a, b) + shared_count):
            table_ref[at] = jnp.zeros((rows, width), table_ref.dtype)

    for a in (0, 2):
        target = me_x + 1 - a

        @pl.when(exists(target, nx))
        def _():
            x_copy(a, target).start()

    to_column(1, lambda copy: copy.start())
    for step in range(1, ny):
        weight_copy(step, me_y).start()
    for a in (0, 2):

        @pl.when(jnp.logical_not(exists(me_x + a - 1, nx)))
        def _():
            clear(a, 1)

        for b in (0, 2):

            @pl.when(jnp.logical_not(exists(me_x + a - 1, nx) & exists(me_y + b - 1, ny)))
            def _():
                clear(a, b)

    for b in (0, 2):

        @pl.when(jnp.logical_not(exists(me_y + b - 1, ny)))
        def _():
            clear(1, b)

    file.wait()
    turn(0, blocks)
    shift.wait()
    for b in range(blocks):
        pre_ref[b] = jnp.broadcast_to(bias[...], (rows, width))
    pre_ref[blocks] = jnp.zeros((rows, width), f32)

    def blank(t, carry):
        grad_ref[t] = jnp.zeros((rows, width), f32)
        return carry

    lax.fori_loop(0, grad_ref.shape[0], blank, 0)

    def arrive(a, b):
        @pl.when(exists(me_x + a - 1, nx) & exists(me_y + b - 1, ny))
        def _():
            y_copy(a, b, me_y + b - 1).wait_recv()

        turn(first(a, b), shared_count)

    for b in (0, 2):
        arrive(1, b)
    for a in (0, 2):

        @pl.when(exists(me_x + a - 1, nx))
        def _():
            x_copy(a, me_x + a - 1).wait_recv()
            to_column(a, lambda copy: copy.start())

        turn(first(a, 1), shared_count)
    for a in (0, 2):
        for b in (0, 2):
            arrive(a, b)

    for a in range(3):

        @pl.when(exists(me_x + a - 1, nx))
        def _():
            to_column(a, lambda copy: copy.wait_send())

    for a in (0, 2):
        target = me_x + 1 - a

        @pl.when(exists(target, nx))
        def _():
            x_copy(a, target).wait_send()

    for step in range(1, ny):
        weight_copy(step, lax.rem(me_y - step + ny, ny)).wait_recv()
        weight_copy(step, me_y).wait_send()
    keep.wait()


def layer_kernel(
    source_ref,
    target_ref,
    count_ref,
    table,
    weight_ref,
    cot_ref,
    pre_in,
    grad_in,
    out_ref,
    pre,
    grad,
    borrowed_ref,
    dpre_ref,
    out,
    osem,
):
    blocks, rows, width = cot_ref.shape
    slots = source_ref.shape[0]
    kvol = weight_ref.shape[0]
    total_blocks = table.shape[0]
    shared_count = borrowed_ref.shape[1]
    f32 = jnp.float32
    dpre_ref[blocks] = jnp.zeros((rows, width), dpre_ref.dtype)

    def forward(k, carry):
        live = count_ref[k]
        taken, targets = [], []
        for q in range(slots):
            taken.append(table[jnp.where(q < live, source_ref[q, k], 0)])
            targets.append(jnp.where(q < live, target_ref[q, k], blocks))
        made = jnp.dot(jnp.concatenate(taken, axis=0), weight_ref[k], preferred_element_type=f32)
        for q, target in enumerate(targets):
            pre[target] += made[q * rows : (q + 1) * rows]
        return carry

    lax.fori_loop(0, kvol, forward, 0, unroll=UNROLL)

    def activate(b, carry):
        value = pre[b]
        sig = jax.nn.sigmoid(value)
        out[b] = (value * sig).astype(out.dtype)
        dpre_ref[b] = (cot_ref[b].astype(f32) * sig * (1.0 + value * (1.0 - sig))).astype(
            dpre_ref.dtype
        )
        return carry

    lax.fori_loop(0, blocks, activate, 0)
    keep = pltpu.make_async_copy(out, out_ref, osem)
    keep.start()

    def backward(k, carry):
        live = count_ref[k]
        pulled, spread = [], []
        for q in range(slots):
            pulled.append(dpre_ref[jnp.where(q < live, target_ref[q, k], blocks)])
            spread.append(jnp.where(q < live, source_ref[q, k], total_blocks))
        back = lax.dot_general(
            jnp.concatenate(pulled, axis=0),
            weight_ref[k],
            (((1,), (1,)), ((), ())),
            preferred_element_type=f32,
        )
        for q, source in enumerate(spread):
            grad[source] += back[q * rows : (q + 1) * rows]
        return carry

    lax.fori_loop(0, kvol, backward, 0, unroll=UNROLL)
    at = blocks
    for d in range(9):
        for s in range(shared_count):
            if d != 4:
                borrowed_ref[d, s] = grad[at].astype(borrowed_ref.dtype)
                at += 1
    keep.wait()


def line_kernel(
    nx,
    ny,
    source_ref,
    target_ref,
    count_ref,
    send_in,
    turned_ref,
    dpre_ref,
    own_ref,
    borrowed_ref,
    wide_ref,
    feat_ref,
    send_ref,
    away,
    sums,
    back,
    work,
    yland,
    full_land,
    half_land,
    land,
    spare,
    side_land,
    column,
    x_land,
    ysend,
    csend,
    crecv,
    hsend,
    hrecv,
    bsend,
    brecv,
    picksem,
):
    me_x, me_y = lax.axis_index("gx"), lax.axis_index("gy")
    kvol, parts, deep, width = work.shape
    slots = source_ref.shape[0]
    blocks, rows = feat_ref.shape[:2]
    f32 = jnp.float32
    bit_x, bit_y, z = lax.rem(me_x, 2), lax.rem(me_x // 2, 2), me_x // 4
    high = z // 2
    beside = {"x": me_x + 1 - 2 * bit_x, "y": me_x + 2 - 4 * bit_y}
    inner = exists(z - 1, 2)
    near = jnp.where(inner, me_x - 4 + 8 * high, me_x + 4 - 8 * high)
    middle = me_x + 4 - 8 * high

    pick = pltpu.make_async_copy(send_in, send_ref, picksem)
    pick.start()
    barrier = pltpu.get_barrier_semaphore()
    expected = greet_neighbours(barrier, me_x, me_y, nx, ny) + greet_column(
        barrier, me_x, me_y, ny
    )
    for device in (beside["x"], beside["y"], near):
        pl.semaphore_signal(barrier, inc=1, device_id=(device, me_y), device_id_type=MESH)

    @pl.when(inner)
    def _():
        pl.semaphore_signal(barrier, inc=1, device_id=(middle, me_y), device_id_type=MESH)

    pl.semaphore_wait(barrier, expected + 3 + inner.astype(jnp.int32))

    pick.wait()

    def side_copy(a, b):
        return pltpu.make_async_remote_copy(
            src_ref=borrowed_ref.at[3 * a + b],
            dst_ref=side_land.at[a, b // 2],
            send_sem=hsend.at[a, b // 2],
            recv_sem=hrecv.at[a, b // 2],
            device_id=(me_x, me_y + b - 1),
            device_id_type=MESH,
        )

    def back_copy(a):
        return pltpu.make_async_remote_copy(
            src_ref=column.at[a // 2],
            dst_ref=x_land.at[a // 2],
            send_sem=bsend.at[a // 2],
            recv_sem=brecv.at[a // 2],
            device_id=(me_x + a - 1, me_y),
            device_id_type=MESH,
        )

    def sides(act, sign):
        for a in range(3):
            for b in (0, 2):

                @pl.when(exists(me_x + a - 1, nx) & exists(me_y + sign * (b - 1), ny))
                def _():
                    act(a, b)

    def column_copy(step, g):
        other = lax.rem(me_y + step, ny)
        return pltpu.make_async_remote_copy(
            src_ref=away.at[step - 1, g],
            dst_ref=yland.at[step - 1, g],
            send_sem=ysend.at[step - 1],
            recv_sem=crecv.at[4 + step - 1, g],
            device_id=(me_x, other),
            device_id_type=MESH,
        )

    def make(g, carry):
        live = count_ref[g]
        taken, pulled = [], []
        for q in range(slots):
            taken.append(turned_ref[jnp.where(q < live, source_ref[q, g], 0)])
            pulled.append(dpre_ref[jnp.where(q < live, target_ref[q, g], blocks)])
        part = jnp.dot(
            jnp.concatenate(taken, axis=1),
            jnp.concatenate(pulled, axis=0),
            preferred_element_type=f32,
        ).astype(work.dtype).reshape(ny, parts, deep, width)
        for y in range(ny):
            step = lax.rem(y - me_y + ny, ny)
            for d in range(ny):

                @pl.when(step == d)
                def _():
                    if d == 0:
                        work[g] = part[y]
                    else:
                        away[d - 1, g] = part[y]

        for step in range(1, ny):
            column_copy(step, g).start()
        return carry

    sides(lambda a, b: side_copy(a, b).start(), 1)

    def give_back():
        back[...] = jnp.zeros(back.shape, f32)
        for b in (0, 2):

            @pl.when(exists(me_y + 1 - b, ny))
            def _():
                side_copy(1, b).wait_recv()
                back[...] += side_land[1, b // 2].astype(f32)

        for a in (0, 2):

            @pl.when(exists(me_x + a - 1, nx))
            def _():
                for b in (0, 2):
                    missing = jnp.logical_not(exists(me_y + 1 - b, ny))

                    @pl.when(missing)
                    def _():
                        side_land[a, b // 2] = jnp.zeros(side_land.shape[2:], side_land.dtype)

                    @pl.when(jnp.logical_not(missing))
                    def _():
                        side_copy(a, b).wait_recv()

                column[a // 2] = (
                    borrowed_ref[3 * a + 1].astype(f32)
                    + side_land[a, 0].astype(f32)
                    + side_land[a, 1].astype(f32)
                ).astype(column.dtype)
                back_copy(a).start()

    def take_back():
        for a in (0, 2):

            @pl.when(exists(me_x + 1 - a, nx))
            def _():
                back_copy(a).wait_recv()
                back[...] += x_land[a // 2].astype(f32)

        for b in range(blocks):
            value = own_ref[b]
            for s in range(back.shape[0]):
                value = value + jnp.where(send_ref[s] == b, back[s], 0.0)
            feat_ref[b] = value.astype(feat_ref.dtype)

    def own_sum(g):
        value = work[g].astype(f32)
        for step in range(1, ny):
            column_copy(step, g).wait_recv()
            value = value + yland[step - 1, g].astype(f32)
        return value

    def copy(g, src, dst, leave, arrive, device):
        return pltpu.make_async_remote_copy(
            src_ref=src,
            dst_ref=dst,
            send_sem=csend.at[leave],
            recv_sem=crecv.at[arrive, g],
            device_id=(device, me_y),
            device_id_type=MESH,
        )

    def program(order, inside):
        sent = {}
        made = 0

        def send(g, src, dst, leave, arrive, device):
            copy(g, src, dst, leave, arrive, device).start()
            sent[leave] = sent.get(leave, 0) + math.prod(src.shape[:-2])

        def recv(g, dst, arrive):
            copy(g, dst, dst, 0, arrive, beside["x"]).wait_recv()

        def finish(g):
            wide_ref[g] = sums[g].reshape(parts * deep, width).astype(f32) * (1.0 / rows)

        def along(g, k):
            first = LINE_KINDS[g][1]
            second = "y" if first == "x" else "x"
            bits = {"x": bit_x, "y": bit_y}
            hb, qb = bits[first], bits[second]
            mine, other = 2 * hb + qb, 2 * hb + 1 - qb
            kept, gone = pl.ds(2 * hb, 2), pl.ds(2 - 2 * hb, 2)
            total, ours = sums.at[g], work.at[g]
            if k == 0:
                work[g] = own_sum(g).astype(work.dtype)
                send(g, ours.at[gone], half_land.at[g], 0, 0, beside[first])
            elif k == 1:
                recv(g, half_land.at[g], 0)
                work[g, kept] = (
                    work[g, kept].astype(f32) + half_land[g].astype(f32)
                ).astype(work.dtype)
                send(g, ours.at[other], land.at[0, g], 1, 1, beside[second])
            elif k == 2:
                recv(g, land.at[0, g], 1)
                work[g, mine] = (
                    work[g, mine].astype(f32) + land[0, g].astype(f32)
                ).astype(work.dtype)
                if not inside:
                    send(g, ours.at[mine], land.at[1, g], 2, 2, near)
            elif k == 3:
                recv(g, land.at[1, g], 2)
                work[g, mine] = (
                    work[g, mine].astype(f32) + land[1, g].astype(f32)
                ).astype(work.dtype)
                send(g, ours.at[mine], land.at[2, g], 3, 3, middle)
            elif k == 4:
                recv(g, land.at[2, g], 3)
                sums[g, mine] = (
                    work[g, mine].astype(f32) + land[2, g].astype(f32)
                ).astype(sums.dtype)
                send(g, total.at[mine], total.at[mine], 2, 2, near)
                send(g, total.at[mine], total.at[mine], 4, 0, beside[second])
            elif k == 5:
                recv(g, total.at[mine], 2)
                send(g, total.at[mine], total.at[mine], 4, 0, beside[second])
            elif k == 6:
                recv(g, total.at[other], 0)
                send(g, total.at[kept], total.at[kept], 5, 4, beside[first])
            elif k == 7:
                recv(g, total.at[gone], 4)
                finish(g)

        def fold(g, k):
            first = LINE_KINDS[g][1]
            second = "y" if first == "x" else "x"
            bits = {"x": bit_x, "y": bit_y}
            hb, qb = high, bits[first]
            mine, other = 2 * hb + qb, 2 * hb + 1 - qb
            kept, gone = pl.ds(2 * hb, 2), pl.ds(2 - 2 * hb, 2)
            total, ours = sums.at[g], work.at[g]
            if not inside:
                if k == 0:
                    work[g] = own_sum(g).astype(work.dtype)
                    send(g, ours, full_land.at[g], 6, 2, near)
                elif k == 6:
                    recv(g, total.at[kept], 2)
                elif k == 7:
                    recv(g, total.at[gone], 3)
                    finish(g)
            elif k == 1:
                value = own_sum(g)
                recv(g, full_land.at[g], 2)
                work[g] = (value + full_land[g].astype(f32)).astype(work.dtype)
                send(g, ours.at[gone], half_land.at[g], 7, 3, middle)
            elif k == 2:
                recv(g, half_land.at[g], 3)
                work[g, kept] = (
                    work[g, kept].astype(f32) + half_land[g].astype(f32)
                ).astype(work.dtype)
                send(g, ours.at[other], land.at[0, g], 1, 0, beside[first])
            elif k == 3:
                recv(g, land.at[0, g], 0)
                work[g, mine] = (
                    work[g, mine].astype(f32) + land[0, g].astype(f32)
                ).astype(work.dtype)
                send(g, ours.at[mine], land.at[1, g], 1, 1, beside[second])
            elif k == 4:
                recv(g, land.at[1, g], 1)
                sums[g, mine] = (
                    work[g, mine].astype(f32) + land[1, g].astype(f32)
                ).astype(sums.dtype)
                send(g, total.at[mine], total.at[mine], 4, 4, beside[first])
            elif k == 5:
                recv(g, total.at[other], 4)
                send(g, total.at[kept], total.at[kept], 8, 2, middle)
                send(g, total.at[kept], total.at[kept], 8, 2, near)
            elif k == 6:
                recv(g, total.at[gone], 2)
                send(g, total.at[gone], total.at[gone], 8, 3, near)
                finish(g)

        for event in order:
            g, k = divmod(event, 10)
            while made < kvol and g < kvol and made <= g + MAKE_LEAD:
                upto = min(kvol, made + MAKE_STEP)
                lax.fori_loop(made, upto, make, 0)
                made = upto
            if g == kvol:
                (give_back, take_back)[k]()
            elif LINE_KINDS[g][0] == "B":
                fold(g, k)
            else:
                along(g, k)
        for leave, pieces in sent.items():
            gone = spare.at[pl.ds(0, pieces)]
            copy(0, gone, gone, leave, 0, beside["x"]).wait_send()

    @pl.when(inner)
    def _():
        program(LINE_ORDERS[0], True)

    @pl.when(jnp.logical_not(inner))
    def _():
        program(LINE_ORDERS[1], False)

    for step in range(1, ny):
        other = lax.rem(me_y + step, ny)
        pltpu.make_async_remote_copy(
            src_ref=away.at[step - 1],
            dst_ref=yland.at[step - 1],
            send_sem=ysend.at[step - 1],
            recv_sem=crecv.at[4 + step - 1, 0],
            device_id=(me_x, other),
            device_id_type=MESH,
        ).wait_send()
    sides(lambda a, b: side_copy(a, b).wait_send(), 1)
    for a in (0, 2):

        @pl.when(exists(me_x + a - 1, nx))
        def _():
            back_copy(a).wait_send()


def finish_kernel(
    send_ref, total_ref, own_ref, returned_ref, weight_ref, feat_ref, wide, feats, wsem, fsem
):
    chunks = wsem.shape[0]
    kvol, share, width = wide.shape
    per = kvol // chunks
    blocks, rows = feat_ref.shape[:2]
    copies = []
    for c in range(chunks):
        at = pl.ds(c * per, per)
        for h in range(width // LANES):
            wide[at, :, h * LANES : (h + 1) * LANES] = total_ref[h, at].reshape(
                per, share, LANES
            ).astype(jnp.float32) * (1.0 / rows)
        copy = pltpu.make_async_copy(wide.at[at], weight_ref.at[at], wsem.at[c])
        copy.start()
        copies.append(copy)
    for b in range(blocks):
        value = own_ref[b]
        for s in range(returned_ref.shape[0]):
            value = value + jnp.where(send_ref[s] == b, returned_ref[s], 0.0)
        feats[b] = value.astype(feats.dtype)
        copy = pltpu.make_async_copy(feats.at[b], feat_ref.at[b], fsem.at[b])
        copy.start()
        copies.append(copy)
    for copy in copies:
        copy.wait()


def store_kernel(wide_ref, feat_ref, weight_out, feat_out, sem):
    chunks = sem.shape[0] - 1
    per = wide_ref.shape[0] // chunks
    copies = [pltpu.make_async_copy(feat_ref, feat_out, sem.at[chunks])]
    for c in range(chunks):
        at = pl.ds(c * per, per)
        copies.append(pltpu.make_async_copy(wide_ref.at[at], weight_out.at[at], sem.at[c]))
    for copy in copies:
        copy.start()
    for copy in copies:
        copy.wait()


def on_device(
    nx,
    ny,
    features,
    kernel_weight,
    channel_bias,
    send_list,
    rule_source,
    rule_target,
    live_counts,
    out_grad,
):
    feats = features[0, 0]
    blocks, rows, width = feats.shape
    shared = send_list[0, 0]
    shared_count = shared.shape[0]
    kvol, slots = rule_source.shape[2:]
    share = kernel_weight.shape[1]
    bf16, f32 = jnp.bfloat16, jnp.float32
    shape = jax.ShapeDtypeStruct
    vmem = pl.BlockSpec(memory_space=VMEM)
    smem = pl.BlockSpec(memory_space=SMEM)
    hbm = pl.BlockSpec(memory_space=pltpu.HBM)
    dma = pltpu.SemaphoreType.DMA
    squares = 9

    total_blocks = blocks + (squares - 1) * shared_count
    if nx == 4 * LINE_LENGTH and kvol == len(LINE_KINDS):
        stay = functools.partial(pltpu.with_memory_space_constraint, memory_space=pltpu.HBM)
        rules = (rule_source[0, 0].T, rule_target[0, 0].T, live_counts.reshape(-1))
        boundary = (shared_count, rows, width)
        quarters = (4, share // 4, width)
        table, turned, full, pre, grad = pl.pallas_call(
            functools.partial(gather_kernel, nx, ny),
            out_shape=(
                shape((total_blocks, rows, width), bf16),
                shape((total_blocks, width, rows), bf16),
                shape((kvol, ny, share, width), bf16),
                shape((blocks + 1, rows, width), f32),
                shape((total_blocks + 1, rows, width), f32),
            ),
            in_specs=[hbm] * 4,
            out_specs=(vmem,) * 5,
            scratch_shapes=[
                SMEM((shared_count,), jnp.int32),
                VMEM((blocks, rows, width), bf16),
                VMEM(boundary, bf16),
                VMEM((1, width), f32),
                dma((5,)),
                dma((2,)),
                dma((2,)),
                dma((3, 2)),
                dma((3, 2)),
                dma((ny,)),
                dma((ny,)),
            ],
            compiler_params=pltpu.CompilerParams(
                collective_id=3, has_side_effects=True, vmem_limit_bytes=GATHER_BYTES
            ),
        )(*(stay(v) for v in (shared, feats, kernel_weight, channel_bias.reshape(1, width))))
        outputs, _, grad, borrowed, dpre = pl.pallas_call(
            layer_kernel,
            out_shape=(
                shape((blocks, rows, width), bf16),
                shape((blocks + 1, rows, width), f32),
                shape((total_blocks + 1, rows, width), f32),
                shape((squares,) + boundary, bf16),
                shape((blocks + 1, rows, width), bf16),
            ),
            in_specs=[smem, smem, smem, vmem, vmem, vmem, vmem, vmem],
            out_specs=(hbm, vmem, vmem, vmem, vmem),
            scratch_shapes=[VMEM((blocks, rows, width), bf16), dma(())],
            input_output_aliases={6: 1, 7: 2},
            compiler_params=pltpu.CompilerParams(vmem_limit_bytes=LAYER_BYTES),
        )(
            *rules,
            table,
            full.reshape(kvol, width, width),
            out_grad[0, 0],
            pre,
            grad,
        )
        wide, feat = pl.pallas_call(
            functools.partial(line_kernel, nx, ny),
            out_shape=(shape((kvol, share, width), f32), shape((blocks, rows, width), bf16)),
            in_specs=[smem, smem, smem, hbm, vmem, vmem, vmem, vmem],
            out_specs=(vmem, vmem),
            scratch_shapes=[
                SMEM((shared_count,), jnp.int32),
                VMEM((max(ny - 1, 1), kvol) + quarters, bf16),
                VMEM((kvol,) + quarters, bf16),
                VMEM(boundary, f32),
                VMEM((kvol,) + quarters, bf16),
                VMEM((max(ny - 1, 1), kvol) + quarters, bf16),
                VMEM((kvol,) + quarters, bf16),
                VMEM((kvol, 2) + quarters[1:], bf16),
                VMEM((3, kvol) + quarters[1:], bf16),
                VMEM((8 * kvol,) + quarters[1:], bf16),
                VMEM((3, 2) + boundary, bf16),
                VMEM((2,) + boundary, bf16),
                VMEM((2,) + boundary, bf16),
                dma((max(ny - 1, 1),)),
                dma((9,)),
                dma((4 + max(ny - 1, 1), kvol)),
                dma((3, 2)),
                dma((3, 2)),
                dma((2,)),
                dma((2,)),
                dma(()),
            ],
            compiler_params=pltpu.CompilerParams(
                collective_id=2, has_side_effects=True, vmem_limit_bytes=LINE_BYTES
            ),
        )(*rules, stay(shared), turned, dpre, grad, borrowed)
        chunks = max(c for c in range(1, 10) if kvol % c == 0)
        weight_grad, feat_grad = pl.pallas_call(
            store_kernel,
            out_shape=(shape((kvol, share, width), f32), shape((blocks, rows, width), bf16)),
            in_specs=[vmem, vmem],
            out_specs=(hbm, hbm),
            scratch_shapes=[dma((chunks + 1,))],
            compiler_params=pltpu.CompilerParams(vmem_limit_bytes=VMEM_BYTES),
        )(wide, feat)
        return (outputs[None, None], feat_grad[None, None], weight_grad)

    halo, full = pl.pallas_call(
        functools.partial(exchange_kernel, nx, ny),
        out_shape=(
            shape((squares, shared_count, rows, width), bf16),
            shape((kvol, ny, share, width), bf16),
        ),
        in_specs=[smem, hbm, hbm],
        out_specs=(vmem, vmem),
        scratch_shapes=[
            VMEM((blocks, rows, width), bf16),
            dma((2,)),
            dma((2,)),
            dma((2,)),
            dma((3, 2)),
            dma((3, 2)),
            dma((ny,)),
            dma((ny,)),
        ],
        compiler_params=pltpu.CompilerParams(
            collective_id=0, has_side_effects=True, vmem_limit_bytes=EXCHANGE_BYTES
        ),
    )(shared, feats, kernel_weight)

    used = (width // LANES) * kvol * (share // TILE)
    groups = len(KINDS)
    unit = groups * nx
    tiles = -(-used // unit) * unit
    depth = tiles // unit
    outputs, own, borrowed, wpart = pl.pallas_call(
        compute_kernel,
        out_shape=(
            shape((blocks, rows, width), bf16),
            shape((blocks, rows, width), f32),
            shape((squares, shared_count, rows, width), bf16),
            shape((ny, tiles, TILE, LANES), bf16),
        ),
        in_specs=[smem, smem, smem, vmem, vmem, vmem, vmem, vmem],
        out_specs=(vmem, vmem, vmem, vmem),
        scratch_shapes=[
            VMEM((total_blocks, rows, width), bf16),
            VMEM((total_blocks, width, rows), bf16),
            VMEM((blocks + 1, rows, width), f32),
            VMEM((blocks + 1, rows, width), bf16),
            VMEM((total_blocks + 1, rows, width), f32),
        ],
        compiler_params=pltpu.CompilerParams(vmem_limit_bytes=VMEM_BYTES),
    )(
        rule_source[0, 0].T,
        rule_target[0, 0].T,
        live_counts.reshape(-1),
        feats,
        halo,
        full.reshape(kvol, width, width),
        channel_bias.reshape(1, width),
        out_grad[0, 0],
    )

    steps = nx.bit_length() - 1
    block = (depth, TILE, LANES)
    boundary = (shared_count, rows, width)
    total, returned = pl.pallas_call(
        functools.partial(reduce_kernel, nx, ny),
        out_shape=(
            shape((groups, nx) + block, bf16),
            shape(boundary, f32),
        ),
        in_specs=[vmem, vmem],
        out_specs=(vmem, vmem),
        scratch_shapes=[
            VMEM((groups, nx) + block, bf16),
            VMEM((max(ny - 1, 1), groups, nx) + block, bf16),
            VMEM((groups, nx) + block, bf16),
            VMEM((3, 2) + boundary, bf16),
            VMEM((2,) + boundary, bf16),
            VMEM((2,) + boundary, bf16),
            dma((max(ny - 1, 1), groups)),
            dma((max(ny - 1, 1), groups)),
            dma((steps, groups)),
            dma((steps, groups)),
            dma((steps, groups)),
            dma((steps, groups)),
            dma((3, 2)),
            dma((3, 2)),
            dma((2,)),
            dma((2,)),
        ],
        compiler_params=pltpu.CompilerParams(
            collective_id=1, has_side_effects=True, vmem_limit_bytes=VMEM_BYTES
        ),
    )(wpart.reshape((ny, groups, nx) + block), borrowed)

    halves, share_tiles = width // LANES, share // TILE
    chunks = max(c for c in range(1, 10) if kvol % c == 0)
    weight_grad, feat_grad = pl.pallas_call(
        finish_kernel,
        out_shape=(shape((kvol, share, width), f32), shape((blocks, rows, width), bf16)),
        in_specs=[smem, vmem, vmem, vmem],
        out_specs=(hbm, hbm),
        scratch_shapes=[
            VMEM((kvol, share, width), f32),
            VMEM((blocks, rows, width), bf16),
            dma((chunks,)),
            dma((blocks,)),
        ],
        compiler_params=pltpu.CompilerParams(vmem_limit_bytes=VMEM_BYTES),
    )(
        shared,
        total.reshape(tiles, TILE, LANES)[:used].reshape(halves, kvol, share_tiles, TILE, LANES),
        own,
        returned,
    )
    return (outputs[None, None], feat_grad[None, None], weight_grad)


def solution(mesh):
    return jax.shard_map(
        functools.partial(on_device, mesh.shape["gx"], mesh.shape["gy"]),
        mesh=mesh,
        in_specs=(
            P("gx", "gy", None, None, None),
            P(None, "gy", None),
            P(),
            P("gx", "gy", None),
            P("gx", "gy", None, None),
            P("gx", "gy", None, None),
            P("gx", "gy", None),
            P("gx", "gy", None, None, None),
        ),
        out_specs=(
            P("gx", "gy", None, None, None),
            P("gx", "gy", None, None, None),
            P(None, "gy", None),
        ),
        check_vma=False,
    )
```

```python
import functools
import math

import jax
import jax.numpy as jnp
from jax import lax
from jax.experimental import pallas as pl
from jax.experimental.pallas import tpu as pltpu
from jax.sharding import PartitionSpec as P

MESH = pl.DeviceIdType.MESH
VMEM = pltpu.VMEM
SMEM = pltpu.SMEM
LANES = 128
TILE = 16
KINDS = (2, 0, 1, 3, 0, 1, 0, 1, 0)
WAVES = (0,) * 9
STAGGER = 1
HALO_AT = 4
UNROLL = 9
VMEM_BYTES = 28 * 1024 * 1024
EXCHANGE_BYTES = 28 * 1024 * 1024
LINE_BYTES = 28 * 1024 * 1024
GATHER_BYTES = 40 * 1024 * 1024
LAYER_BYTES = 28 * 1024 * 1024
LINE_LENGTH = 4
MAKE_FIRST = 10
MAKE_STEP = 3
MAKE_LEAD = 3

LINE_KINDS = (
    'Cy', 'Ay', 'Ax', 'By', 'Ay', 'Ax', 'Ay', 'Ax', 'By',
    'Cy', 'Ay', 'Ax', 'Ay', 'Ax', 'By', 'Cy', 'Ay', 'Ax',
    'Ay', 'Ax', 'Ax', 'Ay', 'Ax', 'Ay', 'Ax', 'Ay', 'Ax',
)
LINE_ORDERS = (
(
    0, 10, 20, 40, 50, 60, 70, 90, 100, 110, 120, 130, 150, 160, 170, 180,
    190, 31, 21, 200, 210, 11, 51, 220, 81, 230, 41, 71, 240, 250, 141, 260,
    22, 111, 131, 61, 12, 171, 101, 52, 191, 121, 201, 161, 42, 221, 181, 72,
    32, 211, 241, 231, 82, 251, 112, 261, 270, 132, 23, 62, 142, 172, 13, 102,
    192, 53, 122, 202, 162, 222, 43, 182, 73, 212, 242, 232, 252, 113, 262, 24,
    133, 14, 63, 54, 103, 123, 44, 173, 74, 193, 163, 183, 33, 114, 203, 83,
    134, 213, 143, 64, 233, 104, 253, 124, 223, 174, 243, 194, 263, 271, 164, 184,
    34, 204, 84, 26, 214, 144, 234, 254, 16, 224, 244, 56, 264, 76, 35, 46,
    116, 27, 66, 136, 106, 17, 85, 176, 126, 57, 196, 166, 77, 145, 47, 206,
    186, 117, 6, 67, 226, 216, 137, 107, 246, 36, 236, 177, 96, 127, 266, 256,
    86, 197, 167, 207, 156, 187, 146, 227, 7, 217, 247, 237, 267, 97, 257, 157,
),
(
    10, 20, 30, 40, 50, 60, 70, 80, 100, 110, 120, 130, 140, 160, 170, 180,
    190, 1, 21, 200, 210, 11, 51, 220, 91, 230, 41, 71, 240, 250, 151, 260,
    111, 22, 131, 61, 12, 171, 101, 52, 191, 121, 201, 161, 42, 221, 181, 72,
    2, 211, 241, 231, 92, 251, 112, 261, 270, 132, 62, 102, 122, 172, 192, 162,
    182, 202, 152, 212, 232, 252, 222, 242, 262, 3, 93, 25, 153, 15, 55, 45,
    75, 271, 4, 94, 26, 154, 115, 65, 135, 105, 16, 125, 56, 175, 195, 165,
    5, 46, 185, 76, 27, 205, 66, 215, 95, 235, 225, 255, 17, 245, 116, 57,
    265, 155, 106, 136, 47, 126, 176, 77, 6, 166, 196, 67, 186, 206, 36, 117,
    96, 216, 226, 107, 137, 236, 246, 127, 177, 156, 256, 266, 167, 197, 37, 187,
    207, 217, 227, 86, 87, 237, 247, 257, 267, 146, 147,
),
)


def greet_neighbours(barrier, me_x, me_y, nx, ny):
    total = 0
    for sx, sy in ((-1, 0), (1, 0), (0, -1), (0, 1)):
        x, y = me_x + sx, me_y + sy
        there = (x >= 0) & (x < nx) & (y >= 0) & (y < ny)

        @pl.when(there)
        def _():
            pl.semaphore_signal(barrier, inc=1, device_id=(x, y), device_id_type=MESH)

        total = total + there.astype(jnp.int32)
    return total


def greet_column(barrier, me_x, me_y, ny):
    for step in range(1, ny):
        pl.semaphore_signal(
            barrier, inc=1, device_id=(me_x, lax.rem(me_y + step, ny)), device_id_type=MESH
        )
    return ny - 1


def exists(index, count):
    return (index >= 0) & (index < count)


def exchange_kernel(
    nx, ny, send_ref, feats_ref, weight_ref, halo_ref, full_ref, feats, lsem, xsend, xrecv, hsend, hrecv, wsend, wrecv
):
    me_x, me_y = lax.axis_index("gx"), lax.axis_index("gy")
    barrier = pltpu.get_barrier_semaphore()
    expected = greet_neighbours(barrier, me_x, me_y, nx, ny) + greet_column(
        barrier, me_x, me_y, ny
    )
    load = pltpu.make_async_copy(feats_ref, feats, lsem.at[0])
    load.start()
    keep = pltpu.make_async_copy(weight_ref, full_ref.at[:, me_y], lsem.at[1])
    keep.start()
    load.wait()
    for s in range(halo_ref.shape[1]):
        halo_ref[4, s] = feats[send_ref[s]]
    pl.semaphore_wait(barrier, expected)

    def x_copy(a, device_x):
        return pltpu.make_async_remote_copy(
            src_ref=halo_ref.at[4],
            dst_ref=halo_ref.at[3 * a + 1],
            send_sem=xsend.at[a // 2],
            recv_sem=xrecv.at[a // 2],
            device_id=(device_x, me_y),
            device_id_type=MESH,
        )

    def y_copy(a, b, device_y):
        return pltpu.make_async_remote_copy(
            src_ref=halo_ref.at[3 * a + 1],
            dst_ref=halo_ref.at[3 * a + b],
            send_sem=hsend.at[a, b // 2],
            recv_sem=hrecv.at[a, b // 2],
            device_id=(me_x, device_y),
            device_id_type=MESH,
        )

    def weight_copy(step, owner):
        return pltpu.make_async_remote_copy(
            src_ref=weight_ref,
            dst_ref=full_ref.at[:, owner],
            send_sem=wsend.at[step],
            recv_sem=wrecv.at[step],
            device_id=(me_x, lax.rem(me_y + step, ny)),
            device_id_type=MESH,
        )

    def to_column(a, act):
        for b in (0, 2):
            target = me_y + 1 - b

            @pl.when(exists(target, ny))
            def _():
                act(y_copy(a, b, target))

    for a in (0, 2):
        target = me_x + 1 - a

        @pl.when(exists(target, nx))
        def _():
            x_copy(a, target).start()

    to_column(1, lambda copy: copy.start())
    for step in range(1, ny):
        weight_copy(step, me_y).start()
    blank = jnp.zeros(halo_ref.shape[1:], halo_ref.dtype)
    for a in (0, 2):
        here = exists(me_x + a - 1, nx)

        @pl.when(jnp.logical_not(here))
        def _():
            halo_ref[3 * a + 1] = blank

        @pl.when(here)
        def _():
            x_copy(a, me_x + a - 1).wait_recv()
            to_column(a, lambda copy: copy.start())

    for a in range(3):
        for b in (0, 2):
            there = exists(me_x + a - 1, nx) & exists(me_y + b - 1, ny)

            @pl.when(jnp.logical_not(there))
            def _():
                halo_ref[3 * a + b] = blank

            @pl.when(there)
            def _():
                y_copy(a, b, me_y + b - 1).wait_recv()

        @pl.when(exists(me_x + a - 1, nx))
        def _():
            to_column(a, lambda copy: copy.wait_send())

    for a in (0, 2):
        target = me_x + 1 - a

        @pl.when(exists(target, nx))
        def _():
            x_copy(a, target).wait_send()

    for step in range(1, ny):
        weight_copy(step, lax.rem(me_y - step + ny, ny)).wait_recv()
        weight_copy(step, me_y).wait_send()
    keep.wait()


def compute_kernel(
    source_ref,
    target_ref,
    count_ref,
    feats_ref,
    halo_ref,
    weight_ref,
    bias_ref,
    cot_ref,
    out_ref,
    own_ref,
    borrowed_ref,
    wpart_ref,
    table,
    turned,
    pre,
    dpre,
    grad,
):
    blocks, rows, width = feats_ref.shape
    slots = source_ref.shape[0]
    kvol = weight_ref.shape[0]
    total_blocks = grad.shape[0] - 1
    shared_count = halo_ref.shape[1]
    ny, tiles = wpart_ref.shape[:2]
    share = width // ny
    share_tiles = share // TILE
    places = [(b, feats_ref.at[b]) for b in range(blocks)]
    at = blocks
    for d in range(9):
        if d != 4:
            for s in range(shared_count):
                places.append((at, halo_ref.at[d, s]))
                at += 1
    for t, ref in places:
        value = ref[...]
        table[t] = value
        turned[t] = value.T
    for b in range(blocks):
        pre[b] = jnp.broadcast_to(bias_ref[...], (rows, width))
    for t in range(total_blocks):
        grad[t] = jnp.zeros((rows, width), jnp.float32)
    pre[blocks] = jnp.zeros((rows, width), jnp.float32)
    grad[total_blocks] = jnp.zeros((rows, width), jnp.float32)
    dpre[blocks] = jnp.zeros((rows, width), dpre.dtype)

    def rules(k):
        live = count_ref[k]
        sources = [source_ref[q, k] for q in range(slots)]
        targets = [target_ref[q, k] for q in range(slots)]
        reads = [jnp.where(q < live, v, 0) for q, v in enumerate(sources)]
        spread = [jnp.where(q < live, v, total_blocks) for q, v in enumerate(sources)]
        targets = [jnp.where(q < live, v, blocks) for q, v in enumerate(targets)]
        return reads, spread, targets

    def forward(k, carry):
        reads, _, targets = rules(k)
        taken = jnp.concatenate([table[s] for s in reads], axis=0)
        made = jnp.dot(taken, weight_ref[k], preferred_element_type=jnp.float32)
        for q, target in enumerate(targets):
            pre[target] += made[q * rows : (q + 1) * rows]
        return carry

    lax.fori_loop(0, kvol, forward, 0, unroll=UNROLL)

    def activate(b, carry):
        value = pre[b]
        sig = jax.nn.sigmoid(value)
        out_ref[b] = (value * sig).astype(out_ref.dtype)
        dpre[b] = (cot_ref[b].astype(jnp.float32) * sig * (1.0 + value * (1.0 - sig))).astype(
            dpre.dtype
        )
        return carry

    lax.fori_loop(0, blocks, activate, 0)

    filled = 2 * kvol * share_tiles
    if filled < tiles:
        for y in range(ny):
            wpart_ref[y, filled:] = jnp.zeros((tiles - filled, TILE, LANES), wpart_ref.dtype)

    def backward(k, carry):
        reads, spread, targets = rules(k)
        pulled = jnp.concatenate([dpre[t] for t in targets], axis=0)
        taken = jnp.concatenate([turned[s] for s in reads], axis=1)
        part = jnp.dot(taken, pulled, preferred_element_type=jnp.float32).astype(wpart_ref.dtype)
        for y in range(ny):
            for h in range(width // LANES):
                piece = part[y * share : (y + 1) * share, h * LANES : (h + 1) * LANES]
                wpart_ref[y, pl.ds((h * kvol + k) * share_tiles, share_tiles)] = piece.reshape(
                    share_tiles, TILE, LANES
                )
        back = lax.dot_general(
            pulled, weight_ref[k], (((1,), (1,)), ((), ())), preferred_element_type=jnp.float32
        )
        for q, source in enumerate(spread):
            grad[source] += back[q * rows : (q + 1) * rows]
        return carry

    lax.fori_loop(0, kvol, backward, 0, unroll=UNROLL)
    for b in range(blocks):
        own_ref[b] = grad[b]
    at = blocks
    for d in range(9):
        for s in range(shared_count):
            if d == 4:
                borrowed_ref[d, s] = jnp.zeros((rows, width), borrowed_ref.dtype)
            else:
                borrowed_ref[d, s] = grad[at].astype(borrowed_ref.dtype)
                at += 1


def reduce_kernel(
    nx,
    ny,
    wpart_ref,
    borrowed_ref,
    sum_ref,
    returned_ref,
    work,
    yland,
    xland,
    side_land,
    column,
    x_land,
    ysend,
    yrecv,
    rsend,
    rrecv,
    gsend,
    grecv,
    hsend,
    hrecv,
    bsend,
    brecv,
):
    me_x, me_y = lax.axis_index("gx"), lax.axis_index("gy")
    groups = work.shape[0]
    steps = nx.bit_length() - 1
    bits = [lax.rem(me_x // (1 << b), 2) for b in range(steps)]
    partners = [me_x + (1 - 2 * bits[b]) * (1 << b) for b in range(steps)]

    barrier = pltpu.get_barrier_semaphore()
    expected = greet_neighbours(barrier, me_x, me_y, nx, ny) + greet_column(
        barrier, me_x, me_y, ny
    )
    for b in range(steps):
        pl.semaphore_signal(barrier, inc=1, device_id=(partners[b], me_y), device_id_type=MESH)
    pl.semaphore_wait(barrier, expected + steps)

    def side_copy(a, b):
        return pltpu.make_async_remote_copy(
            src_ref=borrowed_ref.at[3 * a + b],
            dst_ref=side_land.at[a, b // 2],
            send_sem=hsend.at[a, b // 2],
            recv_sem=hrecv.at[a, b // 2],
            device_id=(me_x, me_y + b - 1),
            device_id_type=MESH,
        )

    def back_copy(a):
        return pltpu.make_async_remote_copy(
            src_ref=column.at[a // 2],
            dst_ref=x_land.at[a // 2],
            send_sem=bsend.at[a // 2],
            recv_sem=brecv.at[a // 2],
            device_id=(me_x + a - 1, me_y),
            device_id_type=MESH,
        )

    def sides(act, sign):
        for a in range(3):
            for b in (0, 2):

                @pl.when(exists(me_x + a - 1, nx) & exists(me_y + sign * (b - 1), ny))
                def _():
                    act(a, b)

    def column_copy(step, g):
        other = lax.rem(me_y + step, ny)
        return pltpu.make_async_remote_copy(
            src_ref=wpart_ref.at[other, g],
            dst_ref=yland.at[step - 1, g],
            send_sem=ysend.at[step - 1, g],
            recv_sem=yrecv.at[step - 1, g],
            device_id=(me_x, other),
            device_id_type=MESH,
        )

    late = list(range(2, steps))
    kinds = [[0, 1] + late, [1, 0] + late, late + [0, 1], late + [1, 0]]
    orders = [kinds[kind] for kind in KINDS]
    starts = []
    for g in range(groups):
        at = [0]
        for s in range(steps):
            at.append(at[-1] + bits[orders[g][s]] * (nx >> (s + 1)))
        starts.append(at)

    def scatter_copy(g, s):
        half = nx >> (s + 1)
        bit = bits[orders[g][s]]
        away = starts[g][s] + (1 - bit) * half
        return pltpu.make_async_remote_copy(
            src_ref=work.at[g, pl.ds(away, half)],
            dst_ref=xland.at[g, pl.ds(nx - 2 * half, half)],
            send_sem=rsend.at[s, g],
            recv_sem=rrecv.at[s, g],
            device_id=(partners[orders[g][s]], me_y),
            device_id_type=MESH,
        )

    def gather_copy(g, s, landing):
        half = nx >> (s + 1)
        bit = bits[orders[g][s]]
        mine = starts[g][s + 1]
        place = starts[g][s] + (1 - bit) * half if landing else mine
        return pltpu.make_async_remote_copy(
            src_ref=sum_ref.at[g, pl.ds(mine, half)],
            dst_ref=sum_ref.at[g, pl.ds(place, half)],
            send_sem=gsend.at[s, g],
            recv_sem=grecv.at[s, g],
            device_id=(partners[orders[g][s]], me_y),
            device_id_type=MESH,
        )

    for g in range(groups):
        for step in range(1, ny):
            column_copy(step, g).start()
    sides(lambda a, b: side_copy(a, b).start(), 1)

    def begin(g):
        value = wpart_ref[me_y, g].astype(jnp.float32)
        for step in range(1, ny):
            column_copy(step, g).wait_recv()
            value = value + yland[step - 1, g].astype(jnp.float32)
        work[g] = value.astype(work.dtype)
        scatter_copy(g, 0).start()

    def scatter(g, s):
        half = nx >> (s + 1)
        scatter_copy(g, s).wait_recv()
        keep = pl.ds(starts[g][s + 1], half)
        value = work[g, keep].astype(jnp.float32) + xland[g, pl.ds(nx - 2 * half, half)].astype(
            jnp.float32
        )
        if s < steps - 1:
            work[g, keep] = value.astype(work.dtype)
            scatter_copy(g, s + 1).start()
        else:
            sum_ref[g, keep] = value.astype(sum_ref.dtype)
            gather_copy(g, s, False).start()

    def gather(g, s):
        gather_copy(g, s, True).wait_recv()
        if s > 0:
            gather_copy(g, s - 1, False).start()

    events = []
    for g in range(groups):
        events.append((WAVES[g] * STAGGER, g, functools.partial(begin, g)))
        for s in range(steps):
            events.append((WAVES[g] * STAGGER + s + 1, g, functools.partial(scatter, g, s)))
            events.append(
                (WAVES[g] * STAGGER + 2 * steps - s, g, functools.partial(gather, g, s))
            )
    events.sort(key=lambda event: event[:2])
    first = [event[2] for event in events if event[0] < HALO_AT]
    rest = [event[2] for event in events if event[0] >= HALO_AT]
    for event in first:
        event()

    returned_ref[...] = jnp.zeros(returned_ref.shape, jnp.float32)
    for b in (0, 2):

        @pl.when(exists(me_y + 1 - b, ny))
        def _():
            side_copy(1, b).wait_recv()
            returned_ref[...] += side_land[1, b // 2].astype(jnp.float32)

    for a in (0, 2):

        @pl.when(exists(me_x + a - 1, nx))
        def _():
            for b in (0, 2):
                missing = jnp.logical_not(exists(me_y + 1 - b, ny))

                @pl.when(missing)
                def _():
                    side_land[a, b // 2] = jnp.zeros(side_land.shape[2:], side_land.dtype)

                @pl.when(jnp.logical_not(missing))
                def _():
                    side_copy(a, b).wait_recv()

            column[a // 2] = (
                borrowed_ref[3 * a + 1].astype(jnp.float32)
                + side_land[a, 0].astype(jnp.float32)
                + side_land[a, 1].astype(jnp.float32)
            ).astype(column.dtype)
            back_copy(a).start()

    for event in rest:
        event()

    for a in (0, 2):

        @pl.when(exists(me_x + 1 - a, nx))
        def _():
            back_copy(a).wait_recv()
            returned_ref[...] += x_land[a // 2].astype(jnp.float32)

    for g in range(groups):
        for step in range(1, ny):
            column_copy(step, g).wait_send()
        for s in range(steps):
            scatter_copy(g, s).wait_send()
            gather_copy(g, s, False).wait_send()
    sides(lambda a, b: side_copy(a, b).wait_send(), 1)
    for a in (0, 2):

        @pl.when(exists(me_x + a - 1, nx))
        def _():
            back_copy(a).wait_send()


def gather_kernel(
    nx,
    ny,
    send_in,
    feats_ref,
    weight_ref,
    bias_ref,
    table_ref,
    turned_ref,
    full_ref,
    pre_ref,
    grad_ref,
    send_ref,
    own,
    stage,
    bias,
    lsem,
    xsend,
    xrecv,
    hsend,
    hrecv,
    wsend,
    wrecv,
):
    me_x, me_y = lax.axis_index("gx"), lax.axis_index("gy")
    blocks, rows, width = feats_ref.shape
    shared_count = stage.shape[0]
    f32 = jnp.float32
    barrier = pltpu.get_barrier_semaphore()
    expected = greet_neighbours(barrier, me_x, me_y, nx, ny) + greet_column(
        barrier, me_x, me_y, ny
    )
    load = pltpu.make_async_copy(feats_ref, own, lsem.at[0])
    load.start()
    pick = pltpu.make_async_copy(send_in, send_ref, lsem.at[3])
    pick.start()
    file = pltpu.make_async_copy(feats_ref, table_ref.at[pl.ds(0, blocks)], lsem.at[4])
    file.start()
    shift = pltpu.make_async_copy(bias_ref, bias, lsem.at[2])
    shift.start()
    keep = pltpu.make_async_copy(weight_ref, full_ref.at[:, me_y], lsem.at[1])
    keep.start()
    pick.wait()
    load.wait()
    for s in range(shared_count):
        stage[s] = own[send_ref[s]]
    pl.semaphore_wait(barrier, expected)

    def first(a, b):
        d = 3 * a + b
        return blocks + shared_count * (d - (d > 4))

    def place(a, b):
        return table_ref.at[pl.ds(first(a, b), shared_count)]

    def x_copy(a, device_x):
        return pltpu.make_async_remote_copy(
            src_ref=stage,
            dst_ref=place(a, 1),
            send_sem=xsend.at[a // 2],
            recv_sem=xrecv.at[a // 2],
            device_id=(device_x, me_y),
            device_id_type=MESH,
        )

    def y_copy(a, b, device_y):
        return pltpu.make_async_remote_copy(
            src_ref=stage if a == 1 else place(a, 1),
            dst_ref=place(a, b),
            send_sem=hsend.at[a, b // 2],
            recv_sem=hrecv.at[a, b // 2],
            device_id=(me_x, device_y),
            device_id_type=MESH,
        )

    def weight_copy(step, owner):
        return pltpu.make_async_remote_copy(
            src_ref=weight_ref,
            dst_ref=full_ref.at[:, owner],
            send_sem=wsend.at[step],
            recv_sem=wrecv.at[step],
            device_id=(me_x, lax.rem(me_y + step, ny)),
            device_id_type=MESH,
        )

    def to_column(a, act):
        for b in (0, 2):
            target = me_y + 1 - b

            @pl.when(exists(target, ny))
            def _():
                act(y_copy(a, b, target))

    def turn(t, count):
        for at in range(t, t + count):
            turned_ref[at] = table_ref[at].T

    def clear(a, b):
        for at in range(first(a, b), first(a, b) + shared_count):
            table_ref[at] = jnp.zeros((rows, width), table_ref.dtype)

    for a in (0, 2):
        target = me_x + 1 - a

        @pl.when(exists(target, nx))
        def _():
            x_copy(a, target).start()

    to_column(1, lambda copy: copy.start())
    for step in range(1, ny):
        weight_copy(step, me_y).start()
    for a in (0, 2):

        @pl.when(jnp.logical_not(exists(me_x + a - 1, nx)))
        def _():
            clear(a, 1)

        for b in (0, 2):

            @pl.when(jnp.logical_not(exists(me_x + a - 1, nx) & exists(me_y + b - 1, ny)))
            def _():
                clear(a, b)

    for b in (0, 2):

        @pl.when(jnp.logical_not(exists(me_y + b - 1, ny)))
        def _():
            clear(1, b)

    file.wait()
    turn(0, blocks)
    shift.wait()
    for b in range(blocks):
        pre_ref[b] = jnp.broadcast_to(bias[...], (rows, width))
    pre_ref[blocks] = jnp.zeros((rows, width), f32)

    def blank(t, carry):
        grad_ref[t] = jnp.zeros((rows, width), f32)
        return carry

    lax.fori_loop(0, grad_ref.shape[0], blank, 0)

    def arrive(a, b):
        @pl.when(exists(me_x + a - 1, nx) & exists(me_y + b - 1, ny))
        def _():
            y_copy(a, b, me_y + b - 1).wait_recv()

        turn(first(a, b), shared_count)

    for b in (0, 2):
        arrive(1, b)
    for a in (0, 2):

        @pl.when(exists(me_x + a - 1, nx))
        def _():
            x_copy(a, me_x + a - 1).wait_recv()
            to_column(a, lambda copy: copy.start())

        turn(first(a, 1), shared_count)
    for a in (0, 2):
        for b in (0, 2):
            arrive(a, b)

    for a in range(3):

        @pl.when(exists(me_x + a - 1, nx))
        def _():
            to_column(a, lambda copy: copy.wait_send())

    for a in (0, 2):
        target = me_x + 1 - a

        @pl.when(exists(target, nx))
        def _():
            x_copy(a, target).wait_send()

    for step in range(1, ny):
        weight_copy(step, lax.rem(me_y - step + ny, ny)).wait_recv()
        weight_copy(step, me_y).wait_send()
    keep.wait()


def layer_kernel(
    source_ref,
    target_ref,
    count_ref,
    table,
    weight_ref,
    cot_ref,
    pre_in,
    grad_in,
    out_ref,
    pre,
    grad,
    borrowed_ref,
    dpre_ref,
    out,
    osem,
):
    blocks, rows, width = cot_ref.shape
    slots = source_ref.shape[0]
    kvol = weight_ref.shape[0]
    total_blocks = table.shape[0]
    shared_count = borrowed_ref.shape[1]
    f32 = jnp.float32
    dpre_ref[blocks] = jnp.zeros((rows, width), dpre_ref.dtype)

    def forward(k, carry):
        live = count_ref[k]
        taken, targets = [], []
        for q in range(slots):
            taken.append(table[jnp.where(q < live, source_ref[q, k], 0)])
            targets.append(jnp.where(q < live, target_ref[q, k], blocks))
        made = jnp.dot(jnp.concatenate(taken, axis=0), weight_ref[k], preferred_element_type=f32)
        for q, target in enumerate(targets):
            pre[target] += made[q * rows : (q + 1) * rows]
        return carry

    lax.fori_loop(0, kvol, forward, 0, unroll=UNROLL)

    def activate(b, carry):
        value = pre[b]
        sig = jax.nn.sigmoid(value)
        out[b] = (value * sig).astype(out.dtype)
        dpre_ref[b] = (cot_ref[b].astype(f32) * sig * (1.0 + value * (1.0 - sig))).astype(
            dpre_ref.dtype
        )
        return carry

    lax.fori_loop(0, blocks, activate, 0)
    keep = pltpu.make_async_copy(out, out_ref, osem)
    keep.start()

    def backward(k, carry):
        live = count_ref[k]
        pulled, spread = [], []
        for q in range(slots):
            pulled.append(dpre_ref[jnp.where(q < live, target_ref[q, k], blocks)])
            spread.append(jnp.where(q < live, source_ref[q, k], total_blocks))
        back = lax.dot_general(
            jnp.concatenate(pulled, axis=0),
            weight_ref[k],
            (((1,), (1,)), ((), ())),
            preferred_element_type=f32,
        )
        for q, source in enumerate(spread):
            grad[source] += back[q * rows : (q + 1) * rows]
        return carry

    lax.fori_loop(0, kvol, backward, 0, unroll=UNROLL)
    at = blocks
    for d in range(9):
        for s in range(shared_count):
            if d != 4:
                borrowed_ref[d, s] = grad[at].astype(borrowed_ref.dtype)
                at += 1
    keep.wait()


def line_kernel(
    nx,
    ny,
    source_ref,
    target_ref,
    count_ref,
    send_in,
    turned_ref,
    dpre_ref,
    own_ref,
    borrowed_ref,
    wide_ref,
    feat_ref,
    send_ref,
    away,
    sums,
    back,
    work,
    yland,
    full_land,
    half_land,
    land,
    spare,
    side_land,
    column,
    x_land,
    ysend,
    csend,
    crecv,
    hsend,
    hrecv,
    bsend,
    brecv,
    picksem,
):
    me_x, me_y = lax.axis_index("gx"), lax.axis_index("gy")
    kvol, parts, deep, width = work.shape
    slots = source_ref.shape[0]
    blocks, rows = feat_ref.shape[:2]
    f32 = jnp.float32
    bit_x, bit_y, z = lax.rem(me_x, 2), lax.rem(me_x // 2, 2), me_x // 4
    high = z // 2
    beside = {"x": me_x + 1 - 2 * bit_x, "y": me_x + 2 - 4 * bit_y}
    inner = exists(z - 1, 2)
    near = jnp.where(inner, me_x - 4 + 8 * high, me_x + 4 - 8 * high)
    opposite = me_x + 12 - 8 * z

    pick = pltpu.make_async_copy(send_in, send_ref, picksem)
    pick.start()
    barrier = pltpu.get_barrier_semaphore()
    expected = greet_neighbours(barrier, me_x, me_y, nx, ny) + greet_column(
        barrier, me_x, me_y, ny
    )
    greeted = (beside["x"], beside["y"], near, opposite)
    for device in greeted:
        pl.semaphore_signal(barrier, inc=1, device_id=(device, me_y), device_id_type=MESH)

    def multiply(g, carry):
        live = count_ref[g]
        taken, pulled = [], []
        for q in range(slots):
            taken.append(turned_ref[jnp.where(q < live, source_ref[q, g], 0)])
            pulled.append(dpre_ref[jnp.where(q < live, target_ref[q, g], blocks)])
        part = jnp.dot(
            jnp.concatenate(taken, axis=1),
            jnp.concatenate(pulled, axis=0),
            preferred_element_type=f32,
        ).astype(work.dtype).reshape(ny, parts, deep, width)
        for y in range(ny):
            step = lax.rem(y - me_y + ny, ny)
            for d in range(ny):

                @pl.when(step == d)
                def _():
                    if d == 0:
                        work[g] = part[y]
                    else:
                        away[d - 1, g] = part[y]

        return carry

    lax.fori_loop(0, MAKE_FIRST, multiply, 0)

    pl.semaphore_wait(barrier, expected + len(greeted))

    pick.wait()

    def side_copy(a, b):
        return pltpu.make_async_remote_copy(
            src_ref=borrowed_ref.at[3 * a + b],
            dst_ref=side_land.at[a, b // 2],
            send_sem=hsend.at[a, b // 2],
            recv_sem=hrecv.at[a, b // 2],
            device_id=(me_x, me_y + b - 1),
            device_id_type=MESH,
        )

    def back_copy(a):
        return pltpu.make_async_remote_copy(
            src_ref=column.at[a // 2],
            dst_ref=x_land.at[a // 2],
            send_sem=bsend.at[a // 2],
            recv_sem=brecv.at[a // 2],
            device_id=(me_x + a - 1, me_y),
            device_id_type=MESH,
        )

    def sides(act, sign):
        for a in range(3):
            for b in (0, 2):

                @pl.when(exists(me_x + a - 1, nx) & exists(me_y + sign * (b - 1), ny))
                def _():
                    act(a, b)

    def column_copy(step, g):
        other = lax.rem(me_y + step, ny)
        return pltpu.make_async_remote_copy(
            src_ref=away.at[step - 1, g],
            dst_ref=yland.at[step - 1, g],
            send_sem=ysend.at[step - 1],
            recv_sem=crecv.at[4 + step - 1, g],
            device_id=(me_x, other),
            device_id_type=MESH,
        )

    def share(g, carry):
        for step in range(1, ny):
            column_copy(step, g).start()
        return carry

    def make(g, carry):
        return share(g, multiply(g, carry))

    lax.fori_loop(0, MAKE_FIRST, share, 0)
    sides(lambda a, b: side_copy(a, b).start(), 1)

    def give_back():
        back[...] = jnp.zeros(back.shape, f32)
        for b in (0, 2):

            @pl.when(exists(me_y + 1 - b, ny))
            def _():
                side_copy(1, b).wait_recv()
                back[...] += side_land[1, b // 2].astype(f32)

        for a in (0, 2):

            @pl.when(exists(me_x + a - 1, nx))
            def _():
                for b in (0, 2):
                    missing = jnp.logical_not(exists(me_y + 1 - b, ny))

                    @pl.when(missing)
                    def _():
                        side_land[a, b // 2] = jnp.zeros(side_land.shape[2:], side_land.dtype)

                    @pl.when(jnp.logical_not(missing))
                    def _():
                        side_copy(a, b).wait_recv()

                column[a // 2] = (
                    borrowed_ref[3 * a + 1].astype(f32)
                    + side_land[a, 0].astype(f32)
                    + side_land[a, 1].astype(f32)
                ).astype(column.dtype)
                back_copy(a).start()

    def take_back():
        for a in (0, 2):

            @pl.when(exists(me_x + 1 - a, nx))
            def _():
                back_copy(a).wait_recv()
                back[...] += x_land[a // 2].astype(f32)

        for b in range(blocks):
            value = own_ref[b]
            for s in range(back.shape[0]):
                value = value + jnp.where(send_ref[s] == b, back[s], 0.0)
            feat_ref[b] = value.astype(feat_ref.dtype)

    def own_sum(g):
        value = work[g].astype(f32)
        for step in range(1, ny):
            column_copy(step, g).wait_recv()
            value = value + yland[step - 1, g].astype(f32)
        return value

    def copy(g, src, dst, leave, arrive, device):
        return pltpu.make_async_remote_copy(
            src_ref=src,
            dst_ref=dst,
            send_sem=csend.at[leave],
            recv_sem=crecv.at[arrive, g],
            device_id=(device, me_y),
            device_id_type=MESH,
        )

    def program(order, inside):
        sent = {}
        made = MAKE_FIRST

        def send(g, src, dst, leave, arrive, device):
            copy(g, src, dst, leave, arrive, device).start()
            sent[leave] = sent.get(leave, 0) + math.prod(src.shape[:-2])

        def recv(g, dst, arrive):
            copy(g, dst, dst, 0, arrive, beside["x"]).wait_recv()

        def finish(g):
            wide_ref[g] = sums[g].reshape(parts * deep, width).astype(f32) * (1.0 / rows)

        def along(g, k):
            first = LINE_KINDS[g][1]
            second = "y" if first == "x" else "x"
            bits = {"x": bit_x, "y": bit_y}
            hb, qb = bits[first], bits[second]
            mine, other = 2 * hb + qb, 2 * hb + 1 - qb
            kept, gone = pl.ds(2 * hb, 2), pl.ds(2 - 2 * hb, 2)
            total, ours = sums.at[g], work.at[g]
            if k == 0:
                work[g] = own_sum(g).astype(work.dtype)
                send(g, ours.at[gone], half_land.at[g], 0, 0, beside[first])
            elif k == 1:
                recv(g, half_land.at[g], 0)
                work[g, kept] = (
                    work[g, kept].astype(f32) + half_land[g].astype(f32)
                ).astype(work.dtype)
                send(g, ours.at[other], land.at[0, g], 1, 1, beside[second])
            elif k == 2:
                recv(g, land.at[0, g], 1)
                work[g, mine] = (
                    work[g, mine].astype(f32) + land[0, g].astype(f32)
                ).astype(work.dtype)
                if not inside:
                    send(g, ours.at[mine], land.at[1, g], 2, 2, near)
            elif k == 3:
                recv(g, land.at[1, g], 2)
                work[g, mine] = (
                    work[g, mine].astype(f32) + land[1, g].astype(f32)
                ).astype(work.dtype)
                send(g, ours.at[mine], land.at[2, g], 3, 3, opposite)
            elif k == 4:
                recv(g, land.at[2, g], 3)
                sums[g, mine] = (
                    work[g, mine].astype(f32) + land[2, g].astype(f32)
                ).astype(sums.dtype)
                send(g, total.at[mine], total.at[mine], 2, 2, near)
                send(g, total.at[mine], total.at[mine], 4, 0, beside[second])
            elif k == 5:
                recv(g, total.at[mine], 2)
                send(g, total.at[mine], total.at[mine], 4, 0, beside[second])
            elif k == 6:
                recv(g, total.at[other], 0)
                send(g, total.at[kept], total.at[kept], 5, 4, beside[first])
            elif k == 7:
                recv(g, total.at[gone], 4)
                finish(g)

        def fold(g, k):
            first = LINE_KINDS[g][1]
            second = "y" if first == "x" else "x"
            bits = {"x": bit_x, "y": bit_y}
            hb, qb = high, bits[first]
            mine, other = 2 * hb + qb, 2 * hb + 1 - qb
            kept, gone = pl.ds(2 * hb, 2), pl.ds(2 - 2 * hb, 2)
            total, ours = sums.at[g], work.at[g]
            hub = inside if LINE_KINDS[g][0] == "B" else not inside
            if not hub:
                if k == 0:
                    work[g] = own_sum(g).astype(work.dtype)
                    send(g, ours, full_land.at[g], 6, 2, near)
                elif k == 6:
                    recv(g, total.at[kept], 2)
                elif k == 7:
                    recv(g, total.at[gone], 3)
                    finish(g)
            elif k == 1:
                value = own_sum(g)
                recv(g, full_land.at[g], 2)
                work[g] = (value + full_land[g].astype(f32)).astype(work.dtype)
                send(g, ours.at[gone], half_land.at[g], 7, 3, opposite)
            elif k == 2:
                recv(g, half_land.at[g], 3)
                work[g, kept] = (
                    work[g, kept].astype(f32) + half_land[g].astype(f32)
                ).astype(work.dtype)
                send(g, ours.at[other], land.at[0, g], 1, 0, beside[first])
            elif k == 3:
                recv(g, land.at[0, g], 0)
                work[g, mine] = (
                    work[g, mine].astype(f32) + land[0, g].astype(f32)
                ).astype(work.dtype)
                send(g, ours.at[mine], land.at[1, g], 1, 1, beside[second])
            elif k == 4:
                recv(g, land.at[1, g], 1)
                sums[g, mine] = (
                    work[g, mine].astype(f32) + land[1, g].astype(f32)
                ).astype(sums.dtype)
                send(g, total.at[mine], total.at[mine], 4, 4, beside[first])
            elif k == 5:
                recv(g, total.at[other], 4)
                send(g, total.at[kept], total.at[kept], 8, 2, opposite)
                send(g, total.at[kept], total.at[kept], 8, 2, near)
            elif k == 6:
                recv(g, total.at[gone], 2)
                send(g, total.at[gone], total.at[gone], 8, 3, near)
                finish(g)

        for event in order:
            g, k = divmod(event, 10)
            while made < kvol and g < kvol and made <= g + MAKE_LEAD:
                upto = min(kvol, made + MAKE_STEP)
                lax.fori_loop(made, upto, make, 0)
                made = upto
            if g == kvol:
                (give_back, take_back)[k]()
            elif LINE_KINDS[g][0] != "A":
                fold(g, k)
            else:
                along(g, k)
        for leave, pieces in sent.items():
            gone = spare.at[pl.ds(0, pieces)]
            copy(0, gone, gone, leave, 0, beside["x"]).wait_send()

    @pl.when(inner)
    def _():
        program(LINE_ORDERS[0], True)

    @pl.when(jnp.logical_not(inner))
    def _():
        program(LINE_ORDERS[1], False)

    for step in range(1, ny):
        other = lax.rem(me_y + step, ny)
        pltpu.make_async_remote_copy(
            src_ref=away.at[step - 1],
            dst_ref=yland.at[step - 1],
            send_sem=ysend.at[step - 1],
            recv_sem=crecv.at[4 + step - 1, 0],
            device_id=(me_x, other),
            device_id_type=MESH,
        ).wait_send()
    sides(lambda a, b: side_copy(a, b).wait_send(), 1)
    for a in (0, 2):

        @pl.when(exists(me_x + a - 1, nx))
        def _():
            back_copy(a).wait_send()


def finish_kernel(
    send_ref, total_ref, own_ref, returned_ref, weight_ref, feat_ref, wide, feats, wsem, fsem
):
    chunks = wsem.shape[0]
    kvol, share, width = wide.shape
    per = kvol // chunks
    blocks, rows = feat_ref.shape[:2]
    copies = []
    for c in range(chunks):
        at = pl.ds(c * per, per)
        for h in range(width // LANES):
            wide[at, :, h * LANES : (h + 1) * LANES] = total_ref[h, at].reshape(
                per, share, LANES
            ).astype(jnp.float32) * (1.0 / rows)
        copy = pltpu.make_async_copy(wide.at[at], weight_ref.at[at], wsem.at[c])
        copy.start()
        copies.append(copy)
    for b in range(blocks):
        value = own_ref[b]
        for s in range(returned_ref.shape[0]):
            value = value + jnp.where(send_ref[s] == b, returned_ref[s], 0.0)
        feats[b] = value.astype(feats.dtype)
        copy = pltpu.make_async_copy(feats.at[b], feat_ref.at[b], fsem.at[b])
        copy.start()
        copies.append(copy)
    for copy in copies:
        copy.wait()


def store_kernel(wide_ref, feat_ref, weight_out, feat_out, sem):
    chunks = sem.shape[0] - 1
    per = wide_ref.shape[0] // chunks
    copies = [pltpu.make_async_copy(feat_ref, feat_out, sem.at[chunks])]
    for c in range(chunks):
        at = pl.ds(c * per, per)
        copies.append(pltpu.make_async_copy(wide_ref.at[at], weight_out.at[at], sem.at[c]))
    for copy in copies:
        copy.start()
    for copy in copies:
        copy.wait()


def on_device(
    nx,
    ny,
    features,
    kernel_weight,
    channel_bias,
    send_list,
    rule_source,
    rule_target,
    live_counts,
    out_grad,
):
    feats = features[0, 0]
    blocks, rows, width = feats.shape
    shared = send_list[0, 0]
    shared_count = shared.shape[0]
    kvol, slots = rule_source.shape[2:]
    share = kernel_weight.shape[1]
    bf16, f32 = jnp.bfloat16, jnp.float32
    shape = jax.ShapeDtypeStruct
    vmem = pl.BlockSpec(memory_space=VMEM)
    smem = pl.BlockSpec(memory_space=SMEM)
    hbm = pl.BlockSpec(memory_space=pltpu.HBM)
    dma = pltpu.SemaphoreType.DMA
    squares = 9

    total_blocks = blocks + (squares - 1) * shared_count
    if nx == 4 * LINE_LENGTH and kvol == len(LINE_KINDS):
        stay = functools.partial(pltpu.with_memory_space_constraint, memory_space=pltpu.HBM)
        rules = (rule_source[0, 0].T, rule_target[0, 0].T, live_counts.reshape(-1))
        boundary = (shared_count, rows, width)
        quarters = (4, share // 4, width)
        table, turned, full, pre, grad = pl.pallas_call(
            functools.partial(gather_kernel, nx, ny),
            out_shape=(
                shape((total_blocks, rows, width), bf16),
                shape((total_blocks, width, rows), bf16),
                shape((kvol, ny, share, width), bf16),
                shape((blocks + 1, rows, width), f32),
                shape((total_blocks + 1, rows, width), f32),
            ),
            in_specs=[hbm] * 4,
            out_specs=(vmem,) * 5,
            scratch_shapes=[
                SMEM((shared_count,), jnp.int32),
                VMEM((blocks, rows, width), bf16),
                VMEM(boundary, bf16),
                VMEM((1, width), f32),
                dma((5,)),
                dma((2,)),
                dma((2,)),
                dma((3, 2)),
                dma((3, 2)),
                dma((ny,)),
                dma((ny,)),
            ],
            compiler_params=pltpu.CompilerParams(
                collective_id=3, has_side_effects=True, vmem_limit_bytes=GATHER_BYTES
            ),
        )(*(stay(v) for v in (shared, feats, kernel_weight, channel_bias.reshape(1, width))))
        outputs, _, grad, borrowed, dpre = pl.pallas_call(
            layer_kernel,
            out_shape=(
                shape((blocks, rows, width), bf16),
                shape((blocks + 1, rows, width), f32),
                shape((total_blocks + 1, rows, width), f32),
                shape((squares,) + boundary, bf16),
                shape((blocks + 1, rows, width), bf16),
            ),
            in_specs=[smem, smem, smem, vmem, vmem, vmem, vmem, vmem],
            out_specs=(hbm, vmem, vmem, vmem, vmem),
            scratch_shapes=[VMEM((blocks, rows, width), bf16), dma(())],
            input_output_aliases={6: 1, 7: 2},
            compiler_params=pltpu.CompilerParams(vmem_limit_bytes=LAYER_BYTES),
        )(
            *rules,
            table,
            full.reshape(kvol, width, width),
            out_grad[0, 0],
            pre,
            grad,
        )
        wide, feat = pl.pallas_call(
            functools.partial(line_kernel, nx, ny),
            out_shape=(shape((kvol, share, width), f32), shape((blocks, rows, width), bf16)),
            in_specs=[smem, smem, smem, hbm, vmem, vmem, vmem, vmem],
            out_specs=(vmem, vmem),
            scratch_shapes=[
                SMEM((shared_count,), jnp.int32),
                VMEM((max(ny - 1, 1), kvol) + quarters, bf16),
                VMEM((kvol,) + quarters, bf16),
                VMEM(boundary, f32),
                VMEM((kvol,) + quarters, bf16),
                VMEM((max(ny - 1, 1), kvol) + quarters, bf16),
                VMEM((kvol,) + quarters, bf16),
                VMEM((kvol, 2) + quarters[1:], bf16),
                VMEM((3, kvol) + quarters[1:], bf16),
                VMEM((8 * kvol,) + quarters[1:], bf16),
                VMEM((3, 2) + boundary, bf16),
                VMEM((2,) + boundary, bf16),
                VMEM((2,) + boundary, bf16),
                dma((max(ny - 1, 1),)),
                dma((9,)),
                dma((4 + max(ny - 1, 1), kvol)),
                dma((3, 2)),
                dma((3, 2)),
                dma((2,)),
                dma((2,)),
                dma(()),
            ],
            compiler_params=pltpu.CompilerParams(
                collective_id=2, has_side_effects=True, vmem_limit_bytes=LINE_BYTES
            ),
        )(*rules, stay(shared), turned, dpre, grad, borrowed)
        chunks = max(c for c in range(1, 10) if kvol % c == 0)
        weight_grad, feat_grad = pl.pallas_call(
            store_kernel,
            out_shape=(shape((kvol, share, width), f32), shape((blocks, rows, width), bf16)),
            in_specs=[vmem, vmem],
            out_specs=(hbm, hbm),
            scratch_shapes=[dma((chunks + 1,))],
            compiler_params=pltpu.CompilerParams(vmem_limit_bytes=VMEM_BYTES),
        )(wide, feat)
        return (outputs[None, None], feat_grad[None, None], weight_grad)

    halo, full = pl.pallas_call(
        functools.partial(exchange_kernel, nx, ny),
        out_shape=(
            shape((squares, shared_count, rows, width), bf16),
            shape((kvol, ny, share, width), bf16),
        ),
        in_specs=[smem, hbm, hbm],
        out_specs=(vmem, vmem),
        scratch_shapes=[
            VMEM((blocks, rows, width), bf16),
            dma((2,)),
            dma((2,)),
            dma((2,)),
            dma((3, 2)),
            dma((3, 2)),
            dma((ny,)),
            dma((ny,)),
        ],
        compiler_params=pltpu.CompilerParams(
            collective_id=0, has_side_effects=True, vmem_limit_bytes=EXCHANGE_BYTES
        ),
    )(shared, feats, kernel_weight)

    used = (width // LANES) * kvol * (share // TILE)
    groups = len(KINDS)
    unit = groups * nx
    tiles = -(-used // unit) * unit
    depth = tiles // unit
    outputs, own, borrowed, wpart = pl.pallas_call(
        compute_kernel,
        out_shape=(
            shape((blocks, rows, width), bf16),
            shape((blocks, rows, width), f32),
            shape((squares, shared_count, rows, width), bf16),
            shape((ny, tiles, TILE, LANES), bf16),
        ),
        in_specs=[smem, smem, smem, vmem, vmem, vmem, vmem, vmem],
        out_specs=(vmem, vmem, vmem, vmem),
        scratch_shapes=[
            VMEM((total_blocks, rows, width), bf16),
            VMEM((total_blocks, width, rows), bf16),
            VMEM((blocks + 1, rows, width), f32),
            VMEM((blocks + 1, rows, width), bf16),
            VMEM((total_blocks + 1, rows, width), f32),
        ],
        compiler_params=pltpu.CompilerParams(vmem_limit_bytes=VMEM_BYTES),
    )(
        rule_source[0, 0].T,
        rule_target[0, 0].T,
        live_counts.reshape(-1),
        feats,
        halo,
        full.reshape(kvol, width, width),
        channel_bias.reshape(1, width),
        out_grad[0, 0],
    )

    steps = nx.bit_length() - 1
    block = (depth, TILE, LANES)
    boundary = (shared_count, rows, width)
    total, returned = pl.pallas_call(
        functools.partial(reduce_kernel, nx, ny),
        out_shape=(
            shape((groups, nx) + block, bf16),
            shape(boundary, f32),
        ),
        in_specs=[vmem, vmem],
        out_specs=(vmem, vmem),
        scratch_shapes=[
            VMEM((groups, nx) + block, bf16),
            VMEM((max(ny - 1, 1), groups, nx) + block, bf16),
            VMEM((groups, nx) + block, bf16),
            VMEM((3, 2) + boundary, bf16),
            VMEM((2,) + boundary, bf16),
            VMEM((2,) + boundary, bf16),
            dma((max(ny - 1, 1), groups)),
            dma((max(ny - 1, 1), groups)),
            dma((steps, groups)),
            dma((steps, groups)),
            dma((steps, groups)),
            dma((steps, groups)),
            dma((3, 2)),
            dma((3, 2)),
            dma((2,)),
            dma((2,)),
        ],
        compiler_params=pltpu.CompilerParams(
            collective_id=1, has_side_effects=True, vmem_limit_bytes=VMEM_BYTES
        ),
    )(wpart.reshape((ny, groups, nx) + block), borrowed)

    halves, share_tiles = width // LANES, share // TILE
    chunks = max(c for c in range(1, 10) if kvol % c == 0)
    weight_grad, feat_grad = pl.pallas_call(
        finish_kernel,
        out_shape=(shape((kvol, share, width), f32), shape((blocks, rows, width), bf16)),
        in_specs=[smem, vmem, vmem, vmem],
        out_specs=(hbm, hbm),
        scratch_shapes=[
            VMEM((kvol, share, width), f32),
            VMEM((blocks, rows, width), bf16),
            dma((chunks,)),
            dma((blocks,)),
        ],
        compiler_params=pltpu.CompilerParams(vmem_limit_bytes=VMEM_BYTES),
    )(
        shared,
        total.reshape(tiles, TILE, LANES)[:used].reshape(halves, kvol, share_tiles, TILE, LANES),
        own,
        returned,
    )
    return (outputs[None, None], feat_grad[None, None], weight_grad)


def solution(mesh):
    return jax.shard_map(
        functools.partial(on_device, mesh.shape["gx"], mesh.shape["gy"]),
        mesh=mesh,
        in_specs=(
            P("gx", "gy", None, None, None),
            P(None, "gy", None),
            P(),
            P("gx", "gy", None),
            P("gx", "gy", None, None),
            P("gx", "gy", None, None),
            P("gx", "gy", None),
            P("gx", "gy", None, None, None),
        ),
        out_specs=(
            P("gx", "gy", None, None, None),
            P("gx", "gy", None, None, None),
            P(None, "gy", None),
        ),
        check_vma=False,
    )
```

```python
import functools
import math

import jax
import jax.numpy as jnp
from jax import lax
from jax.experimental import pallas as pl
from jax.experimental.pallas import tpu as pltpu
from jax.sharding import PartitionSpec as P

MESH = pl.DeviceIdType.MESH
VMEM = pltpu.VMEM
SMEM = pltpu.SMEM
LANES = 128
TILE = 16
KINDS = (2, 0, 1, 3, 0, 1, 0, 1, 0)
WAVES = (0,) * 9
STAGGER = 1
HALO_AT = 4
UNROLL = 9
VMEM_BYTES = 28 * 1024 * 1024
EXCHANGE_BYTES = 28 * 1024 * 1024
LINE_BYTES = 42 * 1024 * 1024
GATHER_BYTES = 40 * 1024 * 1024
LAYER_BYTES = 28 * 1024 * 1024
LINE_LENGTH = 4
MAKE_FIRST = 10
MAKE_STEP = 3
MAKE_LEAD = 3
CHORES_FROM = 12
PULL_STEP = 2
PILE_STEP = 6

LINE_KINDS = (
    'Cy', 'Ay', 'Ax', 'By', 'Ay', 'Ax', 'Ay', 'Ax', 'By',
    'Cy', 'Ay', 'Ax', 'Ay', 'Ax', 'By', 'Cy', 'Ay', 'Ax',
    'Ay', 'Ax', 'Ax', 'Ay', 'Ax', 'Ay', 'Ax', 'Ay', 'Ax',
)
LINE_FOLDED = [g for g, kind in enumerate(LINE_KINDS) if kind[0] != "A"]
LINE_ORDERS = (
(
    0, 10, 20, 40, 50, 60, 70, 90, 100, 110, 120, 130, 150, 160, 170, 180,
    190, 31, 21, 200, 210, 11, 51, 220, 81, 230, 41, 71, 240, 250, 141, 260,
    22, 111, 131, 61, 12, 171, 101, 52, 191, 121, 201, 161, 42, 221, 181, 72,
    32, 211, 241, 231, 82, 251, 112, 261, 270, 132, 23, 62, 142, 172, 13, 102,
    192, 53, 122, 202, 162, 222, 43, 182, 73, 212, 242, 232, 252, 113, 262, 24,
    133, 14, 63, 54, 103, 123, 44, 173, 74, 193, 163, 183, 33, 114, 203, 83,
    134, 213, 143, 64, 233, 104, 253, 124, 223, 174, 243, 194, 263, 271, 164, 184,
    34, 204, 84, 26, 214, 144, 234, 254, 16, 224, 244, 56, 264, 76, 35, 46,
    116, 27, 66, 136, 106, 17, 85, 176, 126, 57, 196, 166, 77, 145, 47, 206,
    186, 117, 6, 67, 226, 216, 137, 107, 246, 36, 236, 177, 96, 127, 266, 256,
    86, 197, 167, 207, 156, 187, 146, 227, 7, 217, 247, 237, 267, 97, 257, 157,
),
(
    10, 20, 30, 40, 50, 60, 70, 80, 100, 110, 120, 130, 140, 160, 170, 180,
    190, 1, 21, 200, 210, 11, 51, 220, 91, 230, 41, 71, 240, 250, 151, 260,
    111, 22, 131, 61, 12, 171, 101, 52, 191, 121, 201, 161, 42, 221, 181, 72,
    2, 211, 241, 231, 92, 251, 112, 261, 270, 132, 62, 102, 122, 172, 192, 162,
    182, 202, 152, 212, 232, 252, 222, 242, 262, 3, 93, 25, 153, 15, 55, 45,
    75, 271, 4, 94, 26, 154, 115, 65, 135, 105, 16, 125, 56, 175, 195, 165,
    5, 46, 185, 76, 27, 205, 66, 215, 95, 235, 225, 255, 17, 245, 116, 57,
    265, 155, 106, 136, 47, 126, 176, 77, 6, 166, 196, 67, 186, 206, 36, 117,
    96, 216, 226, 107, 137, 236, 246, 127, 177, 156, 256, 266, 167, 197, 37, 187,
    207, 217, 227, 86, 87, 237, 247, 257, 267, 146, 147,
),
)


def greet_neighbours(barrier, me_x, me_y, nx, ny):
    total = 0
    for sx, sy in ((-1, 0), (1, 0), (0, -1), (0, 1)):
        x, y = me_x + sx, me_y + sy
        there = (x >= 0) & (x < nx) & (y >= 0) & (y < ny)

        @pl.when(there)
        def _():
            pl.semaphore_signal(barrier, inc=1, device_id=(x, y), device_id_type=MESH)

        total = total + there.astype(jnp.int32)
    return total


def greet_column(barrier, me_x, me_y, ny):
    for step in range(1, ny):
        pl.semaphore_signal(
            barrier, inc=1, device_id=(me_x, lax.rem(me_y + step, ny)), device_id_type=MESH
        )
    return ny - 1


def exists(index, count):
    return (index >= 0) & (index < count)


def exchange_kernel(
    nx, ny, send_ref, feats_ref, weight_ref, halo_ref, full_ref, feats, lsem, xsend, xrecv, hsend, hrecv, wsend, wrecv
):
    me_x, me_y = lax.axis_index("gx"), lax.axis_index("gy")
    barrier = pltpu.get_barrier_semaphore()
    expected = greet_neighbours(barrier, me_x, me_y, nx, ny) + greet_column(
        barrier, me_x, me_y, ny
    )
    load = pltpu.make_async_copy(feats_ref, feats, lsem.at[0])
    load.start()
    keep = pltpu.make_async_copy(weight_ref, full_ref.at[:, me_y], lsem.at[1])
    keep.start()
    load.wait()
    for s in range(halo_ref.shape[1]):
        halo_ref[4, s] = feats[send_ref[s]]
    pl.semaphore_wait(barrier, expected)

    def x_copy(a, device_x):
        return pltpu.make_async_remote_copy(
            src_ref=halo_ref.at[4],
            dst_ref=halo_ref.at[3 * a + 1],
            send_sem=xsend.at[a // 2],
            recv_sem=xrecv.at[a // 2],
            device_id=(device_x, me_y),
            device_id_type=MESH,
        )

    def y_copy(a, b, device_y):
        return pltpu.make_async_remote_copy(
            src_ref=halo_ref.at[3 * a + 1],
            dst_ref=halo_ref.at[3 * a + b],
            send_sem=hsend.at[a, b // 2],
            recv_sem=hrecv.at[a, b // 2],
            device_id=(me_x, device_y),
            device_id_type=MESH,
        )

    def weight_copy(step, owner):
        return pltpu.make_async_remote_copy(
            src_ref=weight_ref,
            dst_ref=full_ref.at[:, owner],
            send_sem=wsend.at[step],
            recv_sem=wrecv.at[step],
            device_id=(me_x, lax.rem(me_y + step, ny)),
            device_id_type=MESH,
        )

    def to_column(a, act):
        for b in (0, 2):
            target = me_y + 1 - b

            @pl.when(exists(target, ny))
            def _():
                act(y_copy(a, b, target))

    for a in (0, 2):
        target = me_x + 1 - a

        @pl.when(exists(target, nx))
        def _():
            x_copy(a, target).start()

    to_column(1, lambda copy: copy.start())
    for step in range(1, ny):
        weight_copy(step, me_y).start()
    blank = jnp.zeros(halo_ref.shape[1:], halo_ref.dtype)
    for a in (0, 2):
        here = exists(me_x + a - 1, nx)

        @pl.when(jnp.logical_not(here))
        def _():
            halo_ref[3 * a + 1] = blank

        @pl.when(here)
        def _():
            x_copy(a, me_x + a - 1).wait_recv()
            to_column(a, lambda copy: copy.start())

    for a in range(3):
        for b in (0, 2):
            there = exists(me_x + a - 1, nx) & exists(me_y + b - 1, ny)

            @pl.when(jnp.logical_not(there))
            def _():
                halo_ref[3 * a + b] = blank

            @pl.when(there)
            def _():
                y_copy(a, b, me_y + b - 1).wait_recv()

        @pl.when(exists(me_x + a - 1, nx))
        def _():
            to_column(a, lambda copy: copy.wait_send())

    for a in (0, 2):
        target = me_x + 1 - a

        @pl.when(exists(target, nx))
        def _():
            x_copy(a, target).wait_send()

    for step in range(1, ny):
        weight_copy(step, lax.rem(me_y - step + ny, ny)).wait_recv()
        weight_copy(step, me_y).wait_send()
    keep.wait()


def compute_kernel(
    source_ref,
    target_ref,
    count_ref,
    feats_ref,
    halo_ref,
    weight_ref,
    bias_ref,
    cot_ref,
    out_ref,
    own_ref,
    borrowed_ref,
    wpart_ref,
    table,
    turned,
    pre,
    dpre,
    grad,
):
    blocks, rows, width = feats_ref.shape
    slots = source_ref.shape[0]
    kvol = weight_ref.shape[0]
    total_blocks = grad.shape[0] - 1
    shared_count = halo_ref.shape[1]
    ny, tiles = wpart_ref.shape[:2]
    share = width // ny
    share_tiles = share // TILE
    places = [(b, feats_ref.at[b]) for b in range(blocks)]
    at = blocks
    for d in range(9):
        if d != 4:
            for s in range(shared_count):
                places.append((at, halo_ref.at[d, s]))
                at += 1
    for t, ref in places:
        value = ref[...]
        table[t] = value
        turned[t] = value.T
    for b in range(blocks):
        pre[b] = jnp.broadcast_to(bias_ref[...], (rows, width))
    for t in range(total_blocks):
        grad[t] = jnp.zeros((rows, width), jnp.float32)
    pre[blocks] = jnp.zeros((rows, width), jnp.float32)
    grad[total_blocks] = jnp.zeros((rows, width), jnp.float32)
    dpre[blocks] = jnp.zeros((rows, width), dpre.dtype)

    def rules(k):
        live = count_ref[k]
        sources = [source_ref[q, k] for q in range(slots)]
        targets = [target_ref[q, k] for q in range(slots)]
        reads = [jnp.where(q < live, v, 0) for q, v in enumerate(sources)]
        spread = [jnp.where(q < live, v, total_blocks) for q, v in enumerate(sources)]
        targets = [jnp.where(q < live, v, blocks) for q, v in enumerate(targets)]
        return reads, spread, targets

    def forward(k, carry):
        reads, _, targets = rules(k)
        taken = jnp.concatenate([table[s] for s in reads], axis=0)
        made = jnp.dot(taken, weight_ref[k], preferred_element_type=jnp.float32)
        for q, target in enumerate(targets):
            pre[target] += made[q * rows : (q + 1) * rows]
        return carry

    lax.fori_loop(0, kvol, forward, 0, unroll=UNROLL)

    def activate(b, carry):
        value = pre[b]
        sig = jax.nn.sigmoid(value)
        out_ref[b] = (value * sig).astype(out_ref.dtype)
        dpre[b] = (cot_ref[b].astype(jnp.float32) * sig * (1.0 + value * (1.0 - sig))).astype(
            dpre.dtype
        )
        return carry

    lax.fori_loop(0, blocks, activate, 0)

    filled = 2 * kvol * share_tiles
    if filled < tiles:
        for y in range(ny):
            wpart_ref[y, filled:] = jnp.zeros((tiles - filled, TILE, LANES), wpart_ref.dtype)

    def backward(k, carry):
        reads, spread, targets = rules(k)
        pulled = jnp.concatenate([dpre[t] for t in targets], axis=0)
        taken = jnp.concatenate([turned[s] for s in reads], axis=1)
        part = jnp.dot(taken, pulled, preferred_element_type=jnp.float32).astype(wpart_ref.dtype)
        for y in range(ny):
            for h in range(width // LANES):
                piece = part[y * share : (y + 1) * share, h * LANES : (h + 1) * LANES]
                wpart_ref[y, pl.ds((h * kvol + k) * share_tiles, share_tiles)] = piece.reshape(
                    share_tiles, TILE, LANES
                )
        back = lax.dot_general(
            pulled, weight_ref[k], (((1,), (1,)), ((), ())), preferred_element_type=jnp.float32
        )
        for q, source in enumerate(spread):
            grad[source] += back[q * rows : (q + 1) * rows]
        return carry

    lax.fori_loop(0, kvol, backward, 0, unroll=UNROLL)
    for b in range(blocks):
        own_ref[b] = grad[b]
    at = blocks
    for d in range(9):
        for s in range(shared_count):
            if d == 4:
                borrowed_ref[d, s] = jnp.zeros((rows, width), borrowed_ref.dtype)
            else:
                borrowed_ref[d, s] = grad[at].astype(borrowed_ref.dtype)
                at += 1


def reduce_kernel(
    nx,
    ny,
    wpart_ref,
    borrowed_ref,
    sum_ref,
    returned_ref,
    work,
    yland,
    xland,
    side_land,
    column,
    x_land,
    ysend,
    yrecv,
    rsend,
    rrecv,
    gsend,
    grecv,
    hsend,
    hrecv,
    bsend,
    brecv,
):
    me_x, me_y = lax.axis_index("gx"), lax.axis_index("gy")
    groups = work.shape[0]
    steps = nx.bit_length() - 1
    bits = [lax.rem(me_x // (1 << b), 2) for b in range(steps)]
    partners = [me_x + (1 - 2 * bits[b]) * (1 << b) for b in range(steps)]

    barrier = pltpu.get_barrier_semaphore()
    expected = greet_neighbours(barrier, me_x, me_y, nx, ny) + greet_column(
        barrier, me_x, me_y, ny
    )
    for b in range(steps):
        pl.semaphore_signal(barrier, inc=1, device_id=(partners[b], me_y), device_id_type=MESH)
    pl.semaphore_wait(barrier, expected + steps)

    def side_copy(a, b):
        return pltpu.make_async_remote_copy(
            src_ref=borrowed_ref.at[3 * a + b],
            dst_ref=side_land.at[a, b // 2],
            send_sem=hsend.at[a, b // 2],
            recv_sem=hrecv.at[a, b // 2],
            device_id=(me_x, me_y + b - 1),
            device_id_type=MESH,
        )

    def back_copy(a):
        return pltpu.make_async_remote_copy(
            src_ref=column.at[a // 2],
            dst_ref=x_land.at[a // 2],
            send_sem=bsend.at[a // 2],
            recv_sem=brecv.at[a // 2],
            device_id=(me_x + a - 1, me_y),
            device_id_type=MESH,
        )

    def sides(act, sign):
        for a in range(3):
            for b in (0, 2):

                @pl.when(exists(me_x + a - 1, nx) & exists(me_y + sign * (b - 1), ny))
                def _():
                    act(a, b)

    def column_copy(step, g):
        other = lax.rem(me_y + step, ny)
        return pltpu.make_async_remote_copy(
            src_ref=wpart_ref.at[other, g],
            dst_ref=yland.at[step - 1, g],
            send_sem=ysend.at[step - 1, g],
            recv_sem=yrecv.at[step - 1, g],
            device_id=(me_x, other),
            device_id_type=MESH,
        )

    late = list(range(2, steps))
    kinds = [[0, 1] + late, [1, 0] + late, late + [0, 1], late + [1, 0]]
    orders = [kinds[kind] for kind in KINDS]
    starts = []
    for g in range(groups):
        at = [0]
        for s in range(steps):
            at.append(at[-1] + bits[orders[g][s]] * (nx >> (s + 1)))
        starts.append(at)

    def scatter_copy(g, s):
        half = nx >> (s + 1)
        bit = bits[orders[g][s]]
        away = starts[g][s] + (1 - bit) * half
        return pltpu.make_async_remote_copy(
            src_ref=work.at[g, pl.ds(away, half)],
            dst_ref=xland.at[g, pl.ds(nx - 2 * half, half)],
            send_sem=rsend.at[s, g],
            recv_sem=rrecv.at[s, g],
            device_id=(partners[orders[g][s]], me_y),
            device_id_type=MESH,
        )

    def gather_copy(g, s, landing):
        half = nx >> (s + 1)
        bit = bits[orders[g][s]]
        mine = starts[g][s + 1]
        place = starts[g][s] + (1 - bit) * half if landing else mine
        return pltpu.make_async_remote_copy(
            src_ref=sum_ref.at[g, pl.ds(mine, half)],
            dst_ref=sum_ref.at[g, pl.ds(place, half)],
            send_sem=gsend.at[s, g],
            recv_sem=grecv.at[s, g],
            device_id=(partners[orders[g][s]], me_y),
            device_id_type=MESH,
        )

    for g in range(groups):
        for step in range(1, ny):
            column_copy(step, g).start()
    sides(lambda a, b: side_copy(a, b).start(), 1)

    def begin(g):
        value = wpart_ref[me_y, g].astype(jnp.float32)
        for step in range(1, ny):
            column_copy(step, g).wait_recv()
            value = value + yland[step - 1, g].astype(jnp.float32)
        work[g] = value.astype(work.dtype)
        scatter_copy(g, 0).start()

    def scatter(g, s):
        half = nx >> (s + 1)
        scatter_copy(g, s).wait_recv()
        keep = pl.ds(starts[g][s + 1], half)
        value = work[g, keep].astype(jnp.float32) + xland[g, pl.ds(nx - 2 * half, half)].astype(
            jnp.float32
        )
        if s < steps - 1:
            work[g, keep] = value.astype(work.dtype)
            scatter_copy(g, s + 1).start()
        else:
            sum_ref[g, keep] = value.astype(sum_ref.dtype)
            gather_copy(g, s, False).start()

    def gather(g, s):
        gather_copy(g, s, True).wait_recv()
        if s > 0:
            gather_copy(g, s - 1, False).start()

    events = []
    for g in range(groups):
        events.append((WAVES[g] * STAGGER, g, functools.partial(begin, g)))
        for s in range(steps):
            events.append((WAVES[g] * STAGGER + s + 1, g, functools.partial(scatter, g, s)))
            events.append(
                (WAVES[g] * STAGGER + 2 * steps - s, g, functools.partial(gather, g, s))
            )
    events.sort(key=lambda event: event[:2])
    first = [event[2] for event in events if event[0] < HALO_AT]
    rest = [event[2] for event in events if event[0] >= HALO_AT]
    for event in first:
        event()

    returned_ref[...] = jnp.zeros(returned_ref.shape, jnp.float32)
    for b in (0, 2):

        @pl.when(exists(me_y + 1 - b, ny))
        def _():
            side_copy(1, b).wait_recv()
            returned_ref[...] += side_land[1, b // 2].astype(jnp.float32)

    for a in (0, 2):

        @pl.when(exists(me_x + a - 1, nx))
        def _():
            for b in (0, 2):
                missing = jnp.logical_not(exists(me_y + 1 - b, ny))

                @pl.when(missing)
                def _():
                    side_land[a, b // 2] = jnp.zeros(side_land.shape[2:], side_land.dtype)

                @pl.when(jnp.logical_not(missing))
                def _():
                    side_copy(a, b).wait_recv()

            column[a // 2] = (
                borrowed_ref[3 * a + 1].astype(jnp.float32)
                + side_land[a, 0].astype(jnp.float32)
                + side_land[a, 1].astype(jnp.float32)
            ).astype(column.dtype)
            back_copy(a).start()

    for event in rest:
        event()

    for a in (0, 2):

        @pl.when(exists(me_x + 1 - a, nx))
        def _():
            back_copy(a).wait_recv()
            returned_ref[...] += x_land[a // 2].astype(jnp.float32)

    for g in range(groups):
        for step in range(1, ny):
            column_copy(step, g).wait_send()
        for s in range(steps):
            scatter_copy(g, s).wait_send()
            gather_copy(g, s, False).wait_send()
    sides(lambda a, b: side_copy(a, b).wait_send(), 1)
    for a in (0, 2):

        @pl.when(exists(me_x + a - 1, nx))
        def _():
            back_copy(a).wait_send()


def gather_kernel(
    nx,
    ny,
    send_in,
    feats_ref,
    weight_ref,
    bias_ref,
    table_ref,
    turned_ref,
    full_ref,
    pre_ref,
    send_ref,
    own,
    stage,
    bias,
    lsem,
    xsend,
    xrecv,
    hsend,
    hrecv,
    wsend,
    wrecv,
):
    me_x, me_y = lax.axis_index("gx"), lax.axis_index("gy")
    blocks, rows, width = feats_ref.shape
    shared_count = stage.shape[0]
    f32 = jnp.float32
    barrier = pltpu.get_barrier_semaphore()
    expected = greet_neighbours(barrier, me_x, me_y, nx, ny) + greet_column(
        barrier, me_x, me_y, ny
    )
    load = pltpu.make_async_copy(feats_ref, own, lsem.at[0])
    load.start()
    pick = pltpu.make_async_copy(send_in, send_ref, lsem.at[3])
    pick.start()
    file = pltpu.make_async_copy(feats_ref, table_ref.at[pl.ds(0, blocks)], lsem.at[4])
    file.start()
    shift = pltpu.make_async_copy(bias_ref, bias, lsem.at[2])
    shift.start()
    keep = pltpu.make_async_copy(weight_ref, full_ref.at[:, me_y], lsem.at[1])
    keep.start()
    pick.wait()
    load.wait()
    for s in range(shared_count):
        stage[s] = own[send_ref[s]]
    pl.semaphore_wait(barrier, expected)

    def first(a, b):
        d = 3 * a + b
        return blocks + shared_count * (d - (d > 4))

    def place(a, b):
        return table_ref.at[pl.ds(first(a, b), shared_count)]

    def x_copy(a, device_x):
        return pltpu.make_async_remote_copy(
            src_ref=stage,
            dst_ref=place(a, 1),
            send_sem=xsend.at[a // 2],
            recv_sem=xrecv.at[a // 2],
            device_id=(device_x, me_y),
            device_id_type=MESH,
        )

    def y_copy(a, b, device_y):
        return pltpu.make_async_remote_copy(
            src_ref=stage if a == 1 else place(a, 1),
            dst_ref=place(a, b),
            send_sem=hsend.at[a, b // 2],
            recv_sem=hrecv.at[a, b // 2],
            device_id=(me_x, device_y),
            device_id_type=MESH,
        )

    def weight_copy(step, owner):
        return pltpu.make_async_remote_copy(
            src_ref=weight_ref,
            dst_ref=full_ref.at[:, owner],
            send_sem=wsend.at[step],
            recv_sem=wrecv.at[step],
            device_id=(me_x, lax.rem(me_y + step, ny)),
            device_id_type=MESH,
        )

    def to_column(a, act):
        for b in (0, 2):
            target = me_y + 1 - b

            @pl.when(exists(target, ny))
            def _():
                act(y_copy(a, b, target))

    def turn(t, count):
        for at in range(t, t + count):
            turned_ref[at] = table_ref[at].T

    def clear(a, b):
        for at in range(first(a, b), first(a, b) + shared_count):
            table_ref[at] = jnp.zeros((rows, width), table_ref.dtype)

    for a in (0, 2):
        target = me_x + 1 - a

        @pl.when(exists(target, nx))
        def _():
            x_copy(a, target).start()

    to_column(1, lambda copy: copy.start())
    for step in range(1, ny):
        weight_copy(step, me_y).start()
    for a in (0, 2):

        @pl.when(jnp.logical_not(exists(me_x + a - 1, nx)))
        def _():
            clear(a, 1)

        for b in (0, 2):

            @pl.when(jnp.logical_not(exists(me_x + a - 1, nx) & exists(me_y + b - 1, ny)))
            def _():
                clear(a, b)

    for b in (0, 2):

        @pl.when(jnp.logical_not(exists(me_y + b - 1, ny)))
        def _():
            clear(1, b)

    file.wait()
    turn(0, blocks)
    shift.wait()
    for b in range(blocks):
        pre_ref[b] = jnp.broadcast_to(bias[...], (rows, width))
    pre_ref[blocks] = jnp.zeros((rows, width), f32)

    def arrive(a, b):
        @pl.when(exists(me_x + a - 1, nx) & exists(me_y + b - 1, ny))
        def _():
            y_copy(a, b, me_y + b - 1).wait_recv()

        turn(first(a, b), shared_count)

    for b in (0, 2):
        arrive(1, b)
    for a in (0, 2):

        @pl.when(exists(me_x + a - 1, nx))
        def _():
            x_copy(a, me_x + a - 1).wait_recv()
            to_column(a, lambda copy: copy.start())

        turn(first(a, 1), shared_count)
    for a in (0, 2):
        for b in (0, 2):
            arrive(a, b)

    for a in range(3):

        @pl.when(exists(me_x + a - 1, nx))
        def _():
            to_column(a, lambda copy: copy.wait_send())

    for a in (0, 2):
        target = me_x + 1 - a

        @pl.when(exists(target, nx))
        def _():
            x_copy(a, target).wait_send()

    for step in range(1, ny):
        weight_copy(step, lax.rem(me_y - step + ny, ny)).wait_recv()
        weight_copy(step, me_y).wait_send()
    keep.wait()


def layer_kernel(
    source_ref,
    target_ref,
    count_ref,
    table,
    weight_ref,
    cot_ref,
    pre_in,
    out_ref,
    pre,
    dpre_ref,
    plan_ref,
    out,
    tally,
    osem,
):
    blocks, rows, width = cot_ref.shape
    slots = source_ref.shape[0]
    kvol = weight_ref.shape[0]
    total_blocks = table.shape[0]
    f32 = jnp.float32
    for t in range(total_blocks + 1):
        tally[t] = 0
    dpre_ref[blocks] = jnp.zeros((rows, width), dpre_ref.dtype)

    def forward(k, carry):
        live = count_ref[k]
        taken, targets = [], []
        for q in range(slots):
            taken.append(table[jnp.where(q < live, source_ref[q, k], 0)])
            targets.append(jnp.where(q < live, target_ref[q, k], blocks))
            key = jnp.where(q < live, source_ref[q, k], total_blocks)
            tally[key] = tally[key] + 1
        made = jnp.dot(jnp.concatenate(taken, axis=0), weight_ref[k], preferred_element_type=f32)
        for q, target in enumerate(targets):
            pre[target] += made[q * rows : (q + 1) * rows]
        return carry

    lax.fori_loop(0, kvol, forward, 0, unroll=UNROLL)

    def keep_on(i, carry):
        plan_ref[1, i] = 1
        return carry

    lax.fori_loop(0, plan_ref.shape[1], keep_on, 0, unroll=16)
    run = 0
    for t in range(total_blocks + 1):
        count = tally[t]
        plan_ref[1, run] = 0
        plan_ref[2, t] = jnp.where(count > 0, run + count - 1, -1)
        tally[t] = run
        run = run + count

    def arrange(k, carry):
        live = count_ref[k]
        for q in range(slots):
            key = jnp.where(q < live, source_ref[q, k], total_blocks)
            place = tally[key]
            tally[key] = place + 1
            plan_ref[0, place] = slots * k + q
        return carry

    lax.fori_loop(0, kvol, arrange, 0, unroll=3)

    def activate(b, carry):
        value = pre[b]
        sig = jax.nn.sigmoid(value)
        out[b] = (value * sig).astype(out.dtype)
        dpre_ref[b] = (cot_ref[b].astype(f32) * sig * (1.0 + value * (1.0 - sig))).astype(
            dpre_ref.dtype
        )
        return carry

    lax.fori_loop(0, blocks, activate, 0)
    keep = pltpu.make_async_copy(out, out_ref, osem)
    keep.start()

    keep.wait()


def line_kernel(
    nx,
    ny,
    source_ref,
    target_ref,
    count_ref,
    send_in,
    turned_ref,
    dpre_ref,
    weight_ref,
    plan_in,
    wide_ref,
    feat_ref,
    send_ref,
    away,
    sums,
    back,
    work,
    yland,
    full_land,
    half_land,
    land,
    spare,
    pulls,
    piles,
    borrowed_ref,
    side_land,
    column,
    x_land,
    ysend,
    csend,
    crecv,
    hsend,
    hrecv,
    bsend,
    brecv,
    picksem,
):
    me_x, me_y = lax.axis_index("gx"), lax.axis_index("gy")
    kvol, parts, deep, width = work.shape
    slots = source_ref.shape[0]
    blocks, rows = feat_ref.shape[:2]
    f32 = jnp.float32
    bit_x, bit_y, z = lax.rem(me_x, 2), lax.rem(me_x // 2, 2), me_x // 4
    high = z // 2
    beside = {"x": me_x + 1 - 2 * bit_x, "y": me_x + 2 - 4 * bit_y}
    inner = exists(z - 1, 2)
    near = jnp.where(inner, me_x - 4 + 8 * high, me_x + 4 - 8 * high)
    opposite = me_x + 12 - 8 * z

    pick = pltpu.make_async_copy(send_in, send_ref, picksem)
    pick.start()
    barrier = pltpu.get_barrier_semaphore()
    expected = greet_neighbours(barrier, me_x, me_y, nx, ny) + greet_column(
        barrier, me_x, me_y, ny
    )
    greeted = (beside["x"], beside["y"], near, opposite)
    for device in greeted:
        pl.semaphore_signal(barrier, inc=1, device_id=(device, me_y), device_id_type=MESH)

    def multiply(g, carry):
        live = count_ref[g]
        taken, pulled = [], []
        for q in range(slots):
            taken.append(turned_ref[jnp.where(q < live, source_ref[q, g], 0)])
            pulled.append(dpre_ref[jnp.where(q < live, target_ref[q, g], blocks)])
        part = jnp.dot(
            jnp.concatenate(taken, axis=1),
            jnp.concatenate(pulled, axis=0),
            preferred_element_type=f32,
        ).astype(work.dtype).reshape(ny, parts, deep, width)
        for y in range(ny):
            step = lax.rem(y - me_y + ny, ny)
            for d in range(ny):

                @pl.when(step == d)
                def _():
                    if d == 0:
                        work[g] = part[y]
                    else:
                        away[d - 1, g] = part[y]

        return carry

    lax.fori_loop(0, MAKE_FIRST, multiply, 0)

    pl.semaphore_wait(barrier, expected + len(greeted))

    pick.wait()

    def side_copy(a, b):
        return pltpu.make_async_remote_copy(
            src_ref=borrowed_ref.at[3 * a + b],
            dst_ref=side_land.at[a, b // 2],
            send_sem=hsend.at[a, b // 2],
            recv_sem=hrecv.at[a, b // 2],
            device_id=(me_x, me_y + b - 1),
            device_id_type=MESH,
        )

    def back_copy(a):
        return pltpu.make_async_remote_copy(
            src_ref=column.at[a // 2],
            dst_ref=x_land.at[a // 2],
            send_sem=bsend.at[a // 2],
            recv_sem=brecv.at[a // 2],
            device_id=(me_x + a - 1, me_y),
            device_id_type=MESH,
        )

    def sides(act, sign):
        for a in range(3):
            for b in (0, 2):

                @pl.when(exists(me_x + a - 1, nx) & exists(me_y + sign * (b - 1), ny))
                def _():
                    act(a, b)

    def column_copy(step, g):
        other = lax.rem(me_y + step, ny)
        return pltpu.make_async_remote_copy(
            src_ref=away.at[step - 1, g],
            dst_ref=yland.at[step - 1, g],
            send_sem=ysend.at[step - 1],
            recv_sem=crecv.at[4 + step - 1, g],
            device_id=(me_x, other),
            device_id_type=MESH,
        )

    def share(g, carry):
        for step in range(1, ny):
            column_copy(step, g).start()
        return carry

    def make(g, carry):
        return share(g, multiply(g, carry))

    lax.fori_loop(0, MAKE_FIRST, share, 0)
    total_slots = kvol * slots

    def pull(k, carry):
        live = count_ref[k]
        taken = [
            dpre_ref[jnp.where(q < live, target_ref[q, k], blocks)] for q in range(slots)
        ]
        made = lax.dot_general(
            jnp.concatenate(taken, axis=0),
            weight_ref[k],
            (((1,), (1,)), ((), ())),
            preferred_element_type=f32,
        )
        pulls[pl.ds(slots * k, slots)] = made.reshape(slots, rows, width)
        return carry

    def pile(i, total):
        total = jnp.where(plan_in[1, i] == 0, 0.0, total) + pulls[plan_in[0, i]]
        piles[i] = total
        return total

    def table_grad(t):
        place = plan_in[2, t]
        return jnp.where(place >= 0, piles[jnp.maximum(place, 0)], 0.0)

    def pull_some(k, upto):
        lax.fori_loop(k, upto, pull, 0)

    def pile_some(i, upto):
        start = piles[i - 1] if i else jnp.zeros((rows, width), f32)
        lax.fori_loop(i, upto, pile, start)

    def lend():
        at = blocks
        for d in range(9):
            for s in range(borrowed_ref.shape[1]):
                if d != 4:
                    borrowed_ref[d, s] = table_grad(at).astype(borrowed_ref.dtype)
                    at += 1
        sides(lambda a, b: side_copy(a, b).start(), 1)

    chores = [functools.partial(pull_some, k, min(k + PULL_STEP, kvol)) for k in range(0, kvol, PULL_STEP)]
    chores += [
        functools.partial(pile_some, i, min(i + PILE_STEP, total_slots))
        for i in range(0, total_slots, PILE_STEP)
    ]
    chores.append(lend)

    def give_back():
        back[...] = jnp.zeros(back.shape, f32)
        for b in (0, 2):

            @pl.when(exists(me_y + 1 - b, ny))
            def _():
                side_copy(1, b).wait_recv()
                back[...] += side_land[1, b // 2].astype(f32)

        for a in (0, 2):

            @pl.when(exists(me_x + a - 1, nx))
            def _():
                for b in (0, 2):
                    missing = jnp.logical_not(exists(me_y + 1 - b, ny))

                    @pl.when(missing)
                    def _():
                        side_land[a, b // 2] = jnp.zeros(side_land.shape[2:], side_land.dtype)

                    @pl.when(jnp.logical_not(missing))
                    def _():
                        side_copy(a, b).wait_recv()

                column[a // 2] = (
                    borrowed_ref[3 * a + 1].astype(f32)
                    + side_land[a, 0].astype(f32)
                    + side_land[a, 1].astype(f32)
                ).astype(column.dtype)
                back_copy(a).start()

    def take_back():
        for a in (0, 2):

            @pl.when(exists(me_x + 1 - a, nx))
            def _():
                back_copy(a).wait_recv()
                back[...] += x_land[a // 2].astype(f32)

        for b in range(blocks):
            value = table_grad(b)
            for s in range(back.shape[0]):
                value = value + jnp.where(send_ref[s] == b, back[s], 0.0)
            feat_ref[b] = value.astype(feat_ref.dtype)

    def own_sum(g):
        value = work[g].astype(f32)
        for step in range(1, ny):
            column_copy(step, g).wait_recv()
            value = value + yland[step - 1, g].astype(f32)
        return value

    def copy(g, src, dst, leave, arrive, device):
        return pltpu.make_async_remote_copy(
            src_ref=src,
            dst_ref=dst,
            send_sem=csend.at[leave],
            recv_sem=crecv.at[arrive, g],
            device_id=(device, me_y),
            device_id_type=MESH,
        )

    def program(order, inside):
        sent = {}
        made = MAKE_FIRST

        def send(g, src, dst, leave, arrive, device):
            copy(g, src, dst, leave, arrive, device).start()
            sent[leave] = sent.get(leave, 0) + math.prod(src.shape[:-2])

        def recv(g, dst, arrive):
            copy(g, dst, dst, 0, arrive, beside["x"]).wait_recv()

        def finish(g):
            wide_ref[g] = sums[g].reshape(parts * deep, width).astype(f32) * (1.0 / rows)

        def along(g, k):
            first = LINE_KINDS[g][1]
            second = "y" if first == "x" else "x"
            bits = {"x": bit_x, "y": bit_y}
            hb, qb = bits[first], bits[second]
            mine, other = 2 * hb + qb, 2 * hb + 1 - qb
            kept, gone = pl.ds(2 * hb, 2), pl.ds(2 - 2 * hb, 2)
            total, ours = sums.at[g], work.at[g]
            if k == 0:
                work[g] = own_sum(g).astype(work.dtype)
                send(g, ours.at[gone], half_land.at[g], 0, 0, beside[first])
            elif k == 1:
                recv(g, half_land.at[g], 0)
                work[g, kept] = (
                    work[g, kept].astype(f32) + half_land[g].astype(f32)
                ).astype(work.dtype)
                send(g, ours.at[other], land.at[0, g], 1, 1, beside[second])
            elif k == 2:
                recv(g, land.at[0, g], 1)
                work[g, mine] = (
                    work[g, mine].astype(f32) + land[0, g].astype(f32)
                ).astype(work.dtype)
                if not inside:
                    send(g, ours.at[mine], land.at[1, g], 2, 2, near)
            elif k == 3:
                recv(g, land.at[1, g], 2)
                work[g, mine] = (
                    work[g, mine].astype(f32) + land[1, g].astype(f32)
                ).astype(work.dtype)
                send(g, ours.at[mine], land.at[2, g], 3, 3, opposite)
            elif k == 4:
                recv(g, land.at[2, g], 3)
                sums[g, mine] = (
                    work[g, mine].astype(f32) + land[2, g].astype(f32)
                ).astype(sums.dtype)
                send(g, total.at[mine], total.at[mine], 2, 2, near)
                send(g, total.at[mine], total.at[mine], 4, 0, beside[second])
            elif k == 5:
                recv(g, total.at[mine], 2)
                send(g, total.at[mine], total.at[mine], 4, 0, beside[second])
            elif k == 6:
                recv(g, total.at[other], 0)
                send(g, total.at[kept], total.at[kept], 5, 4, beside[first])
            elif k == 7:
                recv(g, total.at[gone], 4)
                finish(g)

        def fold(g, k):
            first = LINE_KINDS[g][1]
            second = "y" if first == "x" else "x"
            bits = {"x": bit_x, "y": bit_y}
            hb, qb = high, bits[first]
            mine, other = 2 * hb + qb, 2 * hb + 1 - qb
            kept, gone = pl.ds(2 * hb, 2), pl.ds(2 - 2 * hb, 2)
            total, ours = sums.at[g], work.at[g]
            hub = inside if LINE_KINDS[g][0] == "B" else not inside
            if not hub:
                if k == 0:
                    work[g] = own_sum(g).astype(work.dtype)
                    send(g, ours, full_land.at[LINE_FOLDED.index(g)], 6, 2, near)
                elif k == 6:
                    recv(g, total.at[kept], 2)
                elif k == 7:
                    recv(g, total.at[gone], 3)
                    finish(g)
            elif k == 1:
                value = own_sum(g)
                recv(g, full_land.at[LINE_FOLDED.index(g)], 2)
                work[g] = (value + full_land[LINE_FOLDED.index(g)].astype(f32)).astype(work.dtype)
                send(g, ours.at[gone], half_land.at[g], 7, 3, opposite)
            elif k == 2:
                recv(g, half_land.at[g], 3)
                work[g, kept] = (
                    work[g, kept].astype(f32) + half_land[g].astype(f32)
                ).astype(work.dtype)
                send(g, ours.at[other], land.at[0, g], 1, 0, beside[first])
            elif k == 3:
                recv(g, land.at[0, g], 0)
                work[g, mine] = (
                    work[g, mine].astype(f32) + land[0, g].astype(f32)
                ).astype(work.dtype)
                send(g, ours.at[mine], land.at[1, g], 1, 1, beside[second])
            elif k == 4:
                recv(g, land.at[1, g], 1)
                sums[g, mine] = (
                    work[g, mine].astype(f32) + land[1, g].astype(f32)
                ).astype(sums.dtype)
                send(g, total.at[mine], total.at[mine], 4, 4, beside[first])
            elif k == 5:
                recv(g, total.at[other], 4)
                send(g, total.at[kept], total.at[kept], 8, 2, opposite)
                send(g, total.at[kept], total.at[kept], 8, 2, near)
            elif k == 6:
                recv(g, total.at[gone], 2)
                send(g, total.at[gone], total.at[gone], 8, 3, near)
                finish(g)

        waiting = list(chores)
        for at, event in enumerate(order):
            g, k = divmod(event, 10)
            if event == 10 * kvol:
                while waiting:
                    waiting.pop(0)()
            elif at >= CHORES_FROM and waiting:
                waiting.pop(0)()
            while made < kvol and g < kvol and made <= g + MAKE_LEAD:
                upto = min(kvol, made + MAKE_STEP)
                lax.fori_loop(made, upto, make, 0)
                made = upto
            if g == kvol:
                (give_back, take_back)[k]()
            elif LINE_KINDS[g][0] != "A":
                fold(g, k)
            else:
                along(g, k)
        for leave, pieces in sent.items():
            gone = spare.at[pl.ds(0, pieces)]
            copy(0, gone, gone, leave, 0, beside["x"]).wait_send()

    @pl.when(inner)
    def _():
        program(LINE_ORDERS[0], True)

    @pl.when(jnp.logical_not(inner))
    def _():
        program(LINE_ORDERS[1], False)

    for step in range(1, ny):
        other = lax.rem(me_y + step, ny)
        pltpu.make_async_remote_copy(
            src_ref=away.at[step - 1],
            dst_ref=yland.at[step - 1],
            send_sem=ysend.at[step - 1],
            recv_sem=crecv.at[4 + step - 1, 0],
            device_id=(me_x, other),
            device_id_type=MESH,
        ).wait_send()
    sides(lambda a, b: side_copy(a, b).wait_send(), 1)
    for a in (0, 2):

        @pl.when(exists(me_x + a - 1, nx))
        def _():
            back_copy(a).wait_send()


def finish_kernel(
    send_ref, total_ref, own_ref, returned_ref, weight_ref, feat_ref, wide, feats, wsem, fsem
):
    chunks = wsem.shape[0]
    kvol, share, width = wide.shape
    per = kvol // chunks
    blocks, rows = feat_ref.shape[:2]
    copies = []
    for c in range(chunks):
        at = pl.ds(c * per, per)
        for h in range(width // LANES):
            wide[at, :, h * LANES : (h + 1) * LANES] = total_ref[h, at].reshape(
                per, share, LANES
            ).astype(jnp.float32) * (1.0 / rows)
        copy = pltpu.make_async_copy(wide.at[at], weight_ref.at[at], wsem.at[c])
        copy.start()
        copies.append(copy)
    for b in range(blocks):
        value = own_ref[b]
        for s in range(returned_ref.shape[0]):
            value = value + jnp.where(send_ref[s] == b, returned_ref[s], 0.0)
        feats[b] = value.astype(feats.dtype)
        copy = pltpu.make_async_copy(feats.at[b], feat_ref.at[b], fsem.at[b])
        copy.start()
        copies.append(copy)
    for copy in copies:
        copy.wait()


def store_kernel(wide_ref, feat_ref, weight_out, feat_out, sem):
    chunks = sem.shape[0] - 1
    per = wide_ref.shape[0] // chunks
    copies = [pltpu.make_async_copy(feat_ref, feat_out, sem.at[chunks])]
    for c in range(chunks):
        at = pl.ds(c * per, per)
        copies.append(pltpu.make_async_copy(wide_ref.at[at], weight_out.at[at], sem.at[c]))
    for copy in copies:
        copy.start()
    for copy in copies:
        copy.wait()


def on_device(
    nx,
    ny,
    features,
    kernel_weight,
    channel_bias,
    send_list,
    rule_source,
    rule_target,
    live_counts,
    out_grad,
):
    feats = features[0, 0]
    blocks, rows, width = feats.shape
    shared = send_list[0, 0]
    shared_count = shared.shape[0]
    kvol, slots = rule_source.shape[2:]
    share = kernel_weight.shape[1]
    bf16, f32 = jnp.bfloat16, jnp.float32
    shape = jax.ShapeDtypeStruct
    vmem = pl.BlockSpec(memory_space=VMEM)
    smem = pl.BlockSpec(memory_space=SMEM)
    hbm = pl.BlockSpec(memory_space=pltpu.HBM)
    dma = pltpu.SemaphoreType.DMA
    squares = 9

    total_blocks = blocks + (squares - 1) * shared_count
    if nx == 4 * LINE_LENGTH and kvol == len(LINE_KINDS):
        stay = functools.partial(pltpu.with_memory_space_constraint, memory_space=pltpu.HBM)
        rules = (rule_source[0, 0].T, rule_target[0, 0].T, live_counts.reshape(-1))
        boundary = (shared_count, rows, width)
        quarters = (4, share // 4, width)
        table, turned, full, pre = pl.pallas_call(
            functools.partial(gather_kernel, nx, ny),
            out_shape=(
                shape((total_blocks, rows, width), bf16),
                shape((total_blocks, width, rows), bf16),
                shape((kvol, ny, share, width), bf16),
                shape((blocks + 1, rows, width), f32),
            ),
            in_specs=[hbm] * 4,
            out_specs=(vmem,) * 4,
            scratch_shapes=[
                SMEM((shared_count,), jnp.int32),
                VMEM((blocks, rows, width), bf16),
                VMEM(boundary, bf16),
                VMEM((1, width), f32),
                dma((5,)),
                dma((2,)),
                dma((2,)),
                dma((3, 2)),
                dma((3, 2)),
                dma((ny,)),
                dma((ny,)),
            ],
            compiler_params=pltpu.CompilerParams(
                collective_id=3, has_side_effects=True, vmem_limit_bytes=GATHER_BYTES
            ),
        )(*(stay(v) for v in (shared, feats, kernel_weight, channel_bias.reshape(1, width))))
        outputs, _, dpre, plan = pl.pallas_call(
            layer_kernel,
            out_shape=(
                shape((blocks, rows, width), bf16),
                shape((blocks + 1, rows, width), f32),
                shape((blocks + 1, rows, width), bf16),
                shape((3, -(-(kvol * slots + 1) // LANES) * LANES), jnp.int32),
            ),
            in_specs=[smem, smem, smem, vmem, vmem, vmem, vmem],
            out_specs=(hbm, vmem, vmem, smem),
            scratch_shapes=[
                VMEM((blocks, rows, width), bf16),
                SMEM((total_blocks + 1,), jnp.int32),
                dma(()),
            ],
            input_output_aliases={6: 1},
            compiler_params=pltpu.CompilerParams(vmem_limit_bytes=LAYER_BYTES),
        )(
            *rules,
            table,
            full.reshape(kvol, width, width),
            out_grad[0, 0],
            pre,
        )
        wide, feat = pl.pallas_call(
            functools.partial(line_kernel, nx, ny),
            out_shape=(shape((kvol, share, width), f32), shape((blocks, rows, width), bf16)),
            in_specs=[smem, smem, smem, hbm, vmem, vmem, vmem, smem],
            out_specs=(vmem, vmem),
            scratch_shapes=[
                SMEM((shared_count,), jnp.int32),
                VMEM((max(ny - 1, 1), kvol) + quarters, bf16),
                VMEM((kvol,) + quarters, bf16),
                VMEM(boundary, f32),
                VMEM((kvol,) + quarters, bf16),
                VMEM((max(ny - 1, 1), kvol) + quarters, bf16),
                VMEM((len(LINE_FOLDED),) + quarters, bf16),
                VMEM((kvol, 2) + quarters[1:], bf16),
                VMEM((3, kvol) + quarters[1:], bf16),
                VMEM((2 * kvol,) + quarters[1:], bf16),
                VMEM((kvol * slots, rows, width), f32),
                VMEM((kvol * slots, rows, width), f32),
                VMEM((squares,) + boundary, bf16),
                VMEM((3, 2) + boundary, bf16),
                VMEM((2,) + boundary, bf16),
                VMEM((2,) + boundary, bf16),
                dma((max(ny - 1, 1),)),
                dma((9,)),
                dma((4 + max(ny - 1, 1), kvol)),
                dma((3, 2)),
                dma((3, 2)),
                dma((2,)),
                dma((2,)),
                dma(()),
            ],
            compiler_params=pltpu.CompilerParams(
                collective_id=2, has_side_effects=True, vmem_limit_bytes=LINE_BYTES
            ),
        )(*rules, stay(shared), turned, dpre, full.reshape(kvol, width, width), plan)
        chunks = max(c for c in range(1, 10) if kvol % c == 0)
        weight_grad, feat_grad = pl.pallas_call(
            store_kernel,
            out_shape=(shape((kvol, share, width), f32), shape((blocks, rows, width), bf16)),
            in_specs=[vmem, vmem],
            out_specs=(hbm, hbm),
            scratch_shapes=[dma((chunks + 1,))],
            compiler_params=pltpu.CompilerParams(vmem_limit_bytes=VMEM_BYTES),
        )(wide, feat)
        return (outputs[None, None], feat_grad[None, None], weight_grad)

    halo, full = pl.pallas_call(
        functools.partial(exchange_kernel, nx, ny),
        out_shape=(
            shape((squares, shared_count, rows, width), bf16),
            shape((kvol, ny, share, width), bf16),
        ),
        in_specs=[smem, hbm, hbm],
        out_specs=(vmem, vmem),
        scratch_shapes=[
            VMEM((blocks, rows, width), bf16),
            dma((2,)),
            dma((2,)),
            dma((2,)),
            dma((3, 2)),
            dma((3, 2)),
            dma((ny,)),
            dma((ny,)),
        ],
        compiler_params=pltpu.CompilerParams(
            collective_id=0, has_side_effects=True, vmem_limit_bytes=EXCHANGE_BYTES
        ),
    )(shared, feats, kernel_weight)

    used = (width // LANES) * kvol * (share // TILE)
    groups = len(KINDS)
    unit = groups * nx
    tiles = -(-used // unit) * unit
    depth = tiles // unit
    outputs, own, borrowed, wpart = pl.pallas_call(
        compute_kernel,
        out_shape=(
            shape((blocks, rows, width), bf16),
            shape((blocks, rows, width), f32),
            shape((squares, shared_count, rows, width), bf16),
            shape((ny, tiles, TILE, LANES), bf16),
        ),
        in_specs=[smem, smem, smem, vmem, vmem, vmem, vmem, vmem],
        out_specs=(vmem, vmem, vmem, vmem),
        scratch_shapes=[
            VMEM((total_blocks, rows, width), bf16),
            VMEM((total_blocks, width, rows), bf16),
            VMEM((blocks + 1, rows, width), f32),
            VMEM((blocks + 1, rows, width), bf16),
            VMEM((total_blocks + 1, rows, width), f32),
        ],
        compiler_params=pltpu.CompilerParams(vmem_limit_bytes=VMEM_BYTES),
    )(
        rule_source[0, 0].T,
        rule_target[0, 0].T,
        live_counts.reshape(-1),
        feats,
        halo,
        full.reshape(kvol, width, width),
        channel_bias.reshape(1, width),
        out_grad[0, 0],
    )

    steps = nx.bit_length() - 1
    block = (depth, TILE, LANES)
    boundary = (shared_count, rows, width)
    total, returned = pl.pallas_call(
        functools.partial(reduce_kernel, nx, ny),
        out_shape=(
            shape((groups, nx) + block, bf16),
            shape(boundary, f32),
        ),
        in_specs=[vmem, vmem],
        out_specs=(vmem, vmem),
        scratch_shapes=[
            VMEM((groups, nx) + block, bf16),
            VMEM((max(ny - 1, 1), groups, nx) + block, bf16),
            VMEM((groups, nx) + block, bf16),
            VMEM((3, 2) + boundary, bf16),
            VMEM((2,) + boundary, bf16),
            VMEM((2,) + boundary, bf16),
            dma((max(ny - 1, 1), groups)),
            dma((max(ny - 1, 1), groups)),
            dma((steps, groups)),
            dma((steps, groups)),
            dma((steps, groups)),
            dma((steps, groups)),
            dma((3, 2)),
            dma((3, 2)),
            dma((2,)),
            dma((2,)),
        ],
        compiler_params=pltpu.CompilerParams(
            collective_id=1, has_side_effects=True, vmem_limit_bytes=VMEM_BYTES
        ),
    )(wpart.reshape((ny, groups, nx) + block), borrowed)

    halves, share_tiles = width // LANES, share // TILE
    chunks = max(c for c in range(1, 10) if kvol % c == 0)
    weight_grad, feat_grad = pl.pallas_call(
        finish_kernel,
        out_shape=(shape((kvol, share, width), f32), shape((blocks, rows, width), bf16)),
        in_specs=[smem, vmem, vmem, vmem],
        out_specs=(hbm, hbm),
        scratch_shapes=[
            VMEM((kvol, share, width), f32),
            VMEM((blocks, rows, width), bf16),
            dma((chunks,)),
            dma((blocks,)),
        ],
        compiler_params=pltpu.CompilerParams(vmem_limit_bytes=VMEM_BYTES),
    )(
        shared,
        total.reshape(tiles, TILE, LANES)[:used].reshape(halves, kvol, share_tiles, TILE, LANES),
        own,
        returned,
    )
    return (outputs[None, None], feat_grad[None, None], weight_grad)


def solution(mesh):
    return jax.shard_map(
        functools.partial(on_device, mesh.shape["gx"], mesh.shape["gy"]),
        mesh=mesh,
        in_specs=(
            P("gx", "gy", None, None, None),
            P(None, "gy", None),
            P(),
            P("gx", "gy", None),
            P("gx", "gy", None, None),
            P("gx", "gy", None, None),
            P("gx", "gy", None),
            P("gx", "gy", None, None, None),
        ),
        out_specs=(
            P("gx", "gy", None, None, None),
            P("gx", "gy", None, None, None),
            P(None, "gy", None),
        ),
        check_vma=False,
    )
```

```python
import functools
import math

import jax
import jax.numpy as jnp
from jax import lax
from jax.experimental import pallas as pl
from jax.experimental.pallas import tpu as pltpu
from jax.sharding import PartitionSpec as P

MESH = pl.DeviceIdType.MESH
VMEM = pltpu.VMEM
SMEM = pltpu.SMEM
LANES = 128
TILE = 16
KINDS = (2, 0, 1, 3, 0, 1, 0, 1, 0)
WAVES = (0,) * 9
STAGGER = 1
HALO_AT = 4
UNROLL = 9
VMEM_BYTES = 28 * 1024 * 1024
EXCHANGE_BYTES = 28 * 1024 * 1024
LINE_BYTES = 28 * 1024 * 1024
GATHER_BYTES = 40 * 1024 * 1024
LAYER_BYTES = 28 * 1024 * 1024
LINE_LENGTH = 4
MAKE_FIRST = 10
MAKE_STEP = 3
MAKE_LEAD = 3

LINE_KINDS = (
    'Cy', 'Ay', 'Ax', 'By', 'Ay', 'Ax', 'Ay', 'Ax', 'By',
    'Cy', 'Ay', 'Ax', 'Ay', 'Ax', 'By', 'Cy', 'Ay', 'Ax',
    'Ay', 'Ax', 'Ax', 'Ay', 'Ax', 'Ay', 'Ax', 'Ay', 'Ax',
)
LINE_ORDERS = (
(
    0, 10, 20, 40, 50, 60, 70, 90, 100, 110, 120, 130, 150, 160, 170, 180,
    190, 31, 21, 200, 210, 11, 51, 220, 81, 230, 41, 71, 240, 250, 141, 260,
    22, 111, 131, 61, 12, 171, 101, 52, 191, 121, 201, 161, 42, 221, 181, 72,
    32, 211, 241, 231, 82, 251, 112, 261, 132, 23, 62, 142, 172, 13, 102, 192,
    53, 122, 270, 202, 162, 222, 43, 182, 73, 212, 242, 232, 252, 113, 262, 24,
    133, 14, 63, 54, 103, 123, 44, 173, 74, 193, 163, 183, 33, 114, 203, 83,
    134, 213, 143, 64, 233, 104, 253, 124, 223, 174, 243, 194, 263, 271, 164, 184,
    34, 204, 84, 26, 214, 144, 234, 254, 16, 224, 244, 56, 264, 76, 35, 46,
    116, 27, 66, 136, 106, 17, 85, 176, 126, 57, 196, 166, 77, 145, 47, 206,
    186, 117, 6, 67, 226, 216, 137, 107, 246, 36, 236, 177, 96, 127, 266, 256,
    86, 197, 167, 207, 156, 187, 146, 227, 7, 217, 247, 237, 267, 97, 257, 157,
),
(
    10, 20, 30, 40, 50, 60, 70, 80, 100, 110, 120, 130, 140, 160, 170, 180,
    190, 1, 21, 200, 210, 11, 51, 220, 91, 230, 41, 71, 240, 250, 151, 260,
    111, 22, 131, 61, 12, 171, 101, 52, 191, 121, 201, 161, 42, 221, 181, 72,
    2, 211, 241, 231, 92, 251, 112, 261, 132, 62, 102, 122, 172, 192, 162, 182,
    202, 152, 270, 212, 232, 252, 222, 242, 262, 3, 93, 25, 153, 15, 55, 45,
    75, 271, 4, 94, 26, 154, 115, 65, 135, 105, 16, 125, 56, 175, 195, 165,
    5, 46, 185, 76, 27, 205, 66, 215, 95, 235, 225, 255, 17, 245, 116, 57,
    265, 155, 106, 136, 47, 126, 176, 77, 6, 166, 196, 67, 186, 206, 36, 117,
    96, 216, 226, 107, 137, 236, 246, 127, 177, 156, 256, 266, 167, 197, 37, 187,
    207, 217, 227, 86, 87, 237, 247, 257, 267, 146, 147,
),
)


def greet_neighbours(barrier, me_x, me_y, nx, ny):
    total = 0
    for sx, sy in ((-1, 0), (1, 0), (0, -1), (0, 1)):
        x, y = me_x + sx, me_y + sy
        there = (x >= 0) & (x < nx) & (y >= 0) & (y < ny)

        @pl.when(there)
        def _():
            pl.semaphore_signal(barrier, inc=1, device_id=(x, y), device_id_type=MESH)

        total = total + there.astype(jnp.int32)
    return total


def greet_column(barrier, me_x, me_y, ny):
    for step in range(1, ny):
        pl.semaphore_signal(
            barrier, inc=1, device_id=(me_x, lax.rem(me_y + step, ny)), device_id_type=MESH
        )
    return ny - 1


def exists(index, count):
    return (index >= 0) & (index < count)


def exchange_kernel(
    nx, ny, send_ref, feats_ref, weight_ref, halo_ref, full_ref, feats, lsem, xsend, xrecv, hsend, hrecv, wsend, wrecv
):
    me_x, me_y = lax.axis_index("gx"), lax.axis_index("gy")
    barrier = pltpu.get_barrier_semaphore()
    expected = greet_neighbours(barrier, me_x, me_y, nx, ny) + greet_column(
        barrier, me_x, me_y, ny
    )
    load = pltpu.make_async_copy(feats_ref, feats, lsem.at[0])
    load.start()
    keep = pltpu.make_async_copy(weight_ref, full_ref.at[:, me_y], lsem.at[1])
    keep.start()
    load.wait()
    for s in range(halo_ref.shape[1]):
        halo_ref[4, s] = feats[send_ref[s]]
    pl.semaphore_wait(barrier, expected)

    def x_copy(a, device_x):
        return pltpu.make_async_remote_copy(
            src_ref=halo_ref.at[4],
            dst_ref=halo_ref.at[3 * a + 1],
            send_sem=xsend.at[a // 2],
            recv_sem=xrecv.at[a // 2],
            device_id=(device_x, me_y),
            device_id_type=MESH,
        )

    def y_copy(a, b, device_y):
        return pltpu.make_async_remote_copy(
            src_ref=halo_ref.at[3 * a + 1],
            dst_ref=halo_ref.at[3 * a + b],
            send_sem=hsend.at[a, b // 2],
            recv_sem=hrecv.at[a, b // 2],
            device_id=(me_x, device_y),
            device_id_type=MESH,
        )

    def weight_copy(step, owner):
        return pltpu.make_async_remote_copy(
            src_ref=weight_ref,
            dst_ref=full_ref.at[:, owner],
            send_sem=wsend.at[step],
            recv_sem=wrecv.at[step],
            device_id=(me_x, lax.rem(me_y + step, ny)),
            device_id_type=MESH,
        )

    def to_column(a, act):
        for b in (0, 2):
            target = me_y + 1 - b

            @pl.when(exists(target, ny))
            def _():
                act(y_copy(a, b, target))

    for a in (0, 2):
        target = me_x + 1 - a

        @pl.when(exists(target, nx))
        def _():
            x_copy(a, target).start()

    to_column(1, lambda copy: copy.start())
    for step in range(1, ny):
        weight_copy(step, me_y).start()
    blank = jnp.zeros(halo_ref.shape[1:], halo_ref.dtype)
    for a in (0, 2):
        here = exists(me_x + a - 1, nx)

        @pl.when(jnp.logical_not(here))
        def _():
            halo_ref[3 * a + 1] = blank

        @pl.when(here)
        def _():
            x_copy(a, me_x + a - 1).wait_recv()
            to_column(a, lambda copy: copy.start())

    for a in range(3):
        for b in (0, 2):
            there = exists(me_x + a - 1, nx) & exists(me_y + b - 1, ny)

            @pl.when(jnp.logical_not(there))
            def _():
                halo_ref[3 * a + b] = blank

            @pl.when(there)
            def _():
                y_copy(a, b, me_y + b - 1).wait_recv()

        @pl.when(exists(me_x + a - 1, nx))
        def _():
            to_column(a, lambda copy: copy.wait_send())

    for a in (0, 2):
        target = me_x + 1 - a

        @pl.when(exists(target, nx))
        def _():
            x_copy(a, target).wait_send()

    for step in range(1, ny):
        weight_copy(step, lax.rem(me_y - step + ny, ny)).wait_recv()
        weight_copy(step, me_y).wait_send()
    keep.wait()


def compute_kernel(
    source_ref,
    target_ref,
    count_ref,
    feats_ref,
    halo_ref,
    weight_ref,
    bias_ref,
    cot_ref,
    out_ref,
    own_ref,
    borrowed_ref,
    wpart_ref,
    table,
    turned,
    pre,
    dpre,
    grad,
):
    blocks, rows, width = feats_ref.shape
    slots = source_ref.shape[0]
    kvol = weight_ref.shape[0]
    total_blocks = grad.shape[0] - 1
    shared_count = halo_ref.shape[1]
    ny, tiles = wpart_ref.shape[:2]
    share = width // ny
    share_tiles = share // TILE
    places = [(b, feats_ref.at[b]) for b in range(blocks)]
    at = blocks
    for d in range(9):
        if d != 4:
            for s in range(shared_count):
                places.append((at, halo_ref.at[d, s]))
                at += 1
    for t, ref in places:
        value = ref[...]
        table[t] = value
        turned[t] = value.T
    for b in range(blocks):
        pre[b] = jnp.broadcast_to(bias_ref[...], (rows, width))
    for t in range(total_blocks):
        grad[t] = jnp.zeros((rows, width), jnp.float32)
    pre[blocks] = jnp.zeros((rows, width), jnp.float32)
    grad[total_blocks] = jnp.zeros((rows, width), jnp.float32)
    dpre[blocks] = jnp.zeros((rows, width), dpre.dtype)

    def rules(k):
        live = count_ref[k]
        sources = [source_ref[q, k] for q in range(slots)]
        targets = [target_ref[q, k] for q in range(slots)]
        reads = [jnp.where(q < live, v, 0) for q, v in enumerate(sources)]
        spread = [jnp.where(q < live, v, total_blocks) for q, v in enumerate(sources)]
        targets = [jnp.where(q < live, v, blocks) for q, v in enumerate(targets)]
        return reads, spread, targets

    def forward(k, carry):
        reads, _, targets = rules(k)
        taken = jnp.concatenate([table[s] for s in reads], axis=0)
        made = jnp.dot(taken, weight_ref[k], preferred_element_type=jnp.float32)
        for q, target in enumerate(targets):
            pre[target] += made[q * rows : (q + 1) * rows]
        return carry

    lax.fori_loop(0, kvol, forward, 0, unroll=UNROLL)

    def activate(b, carry):
        value = pre[b]
        sig = jax.nn.sigmoid(value)
        out_ref[b] = (value * sig).astype(out_ref.dtype)
        dpre[b] = (cot_ref[b].astype(jnp.float32) * sig * (1.0 + value * (1.0 - sig))).astype(
            dpre.dtype
        )
        return carry

    lax.fori_loop(0, blocks, activate, 0)

    filled = 2 * kvol * share_tiles
    if filled < tiles:
        for y in range(ny):
            wpart_ref[y, filled:] = jnp.zeros((tiles - filled, TILE, LANES), wpart_ref.dtype)

    def backward(k, carry):
        reads, spread, targets = rules(k)
        pulled = jnp.concatenate([dpre[t] for t in targets], axis=0)
        taken = jnp.concatenate([turned[s] for s in reads], axis=1)
        part = jnp.dot(taken, pulled, preferred_element_type=jnp.float32).astype(wpart_ref.dtype)
        for y in range(ny):
            for h in range(width // LANES):
                piece = part[y * share : (y + 1) * share, h * LANES : (h + 1) * LANES]
                wpart_ref[y, pl.ds((h * kvol + k) * share_tiles, share_tiles)] = piece.reshape(
                    share_tiles, TILE, LANES
                )
        back = lax.dot_general(
            pulled, weight_ref[k], (((1,), (1,)), ((), ())), preferred_element_type=jnp.float32
        )
        for q, source in enumerate(spread):
            grad[source] += back[q * rows : (q + 1) * rows]
        return carry

    lax.fori_loop(0, kvol, backward, 0, unroll=UNROLL)
    for b in range(blocks):
        own_ref[b] = grad[b]
    at = blocks
    for d in range(9):
        for s in range(shared_count):
            if d == 4:
                borrowed_ref[d, s] = jnp.zeros((rows, width), borrowed_ref.dtype)
            else:
                borrowed_ref[d, s] = grad[at].astype(borrowed_ref.dtype)
                at += 1


def reduce_kernel(
    nx,
    ny,
    wpart_ref,
    borrowed_ref,
    sum_ref,
    returned_ref,
    work,
    yland,
    xland,
    side_land,
    column,
    x_land,
    ysend,
    yrecv,
    rsend,
    rrecv,
    gsend,
    grecv,
    hsend,
    hrecv,
    bsend,
    brecv,
):
    me_x, me_y = lax.axis_index("gx"), lax.axis_index("gy")
    groups = work.shape[0]
    steps = nx.bit_length() - 1
    bits = [lax.rem(me_x // (1 << b), 2) for b in range(steps)]
    partners = [me_x + (1 - 2 * bits[b]) * (1 << b) for b in range(steps)]

    barrier = pltpu.get_barrier_semaphore()
    expected = greet_neighbours(barrier, me_x, me_y, nx, ny) + greet_column(
        barrier, me_x, me_y, ny
    )
    for b in range(steps):
        pl.semaphore_signal(barrier, inc=1, device_id=(partners[b], me_y), device_id_type=MESH)
    pl.semaphore_wait(barrier, expected + steps)

    def side_copy(a, b):
        return pltpu.make_async_remote_copy(
            src_ref=borrowed_ref.at[3 * a + b],
            dst_ref=side_land.at[a, b // 2],
            send_sem=hsend.at[a, b // 2],
            recv_sem=hrecv.at[a, b // 2],
            device_id=(me_x, me_y + b - 1),
            device_id_type=MESH,
        )

    def back_copy(a):
        return pltpu.make_async_remote_copy(
            src_ref=column.at[a // 2],
            dst_ref=x_land.at[a // 2],
            send_sem=bsend.at[a // 2],
            recv_sem=brecv.at[a // 2],
            device_id=(me_x + a - 1, me_y),
            device_id_type=MESH,
        )

    def sides(act, sign):
        for a in range(3):
            for b in (0, 2):

                @pl.when(exists(me_x + a - 1, nx) & exists(me_y + sign * (b - 1), ny))
                def _():
                    act(a, b)

    def column_copy(step, g):
        other = lax.rem(me_y + step, ny)
        return pltpu.make_async_remote_copy(
            src_ref=wpart_ref.at[other, g],
            dst_ref=yland.at[step - 1, g],
            send_sem=ysend.at[step - 1, g],
            recv_sem=yrecv.at[step - 1, g],
            device_id=(me_x, other),
            device_id_type=MESH,
        )

    late = list(range(2, steps))
    kinds = [[0, 1] + late, [1, 0] + late, late + [0, 1], late + [1, 0]]
    orders = [kinds[kind] for kind in KINDS]
    starts = []
    for g in range(groups):
        at = [0]
        for s in range(steps):
            at.append(at[-1] + bits[orders[g][s]] * (nx >> (s + 1)))
        starts.append(at)

    def scatter_copy(g, s):
        half = nx >> (s + 1)
        bit = bits[orders[g][s]]
        away = starts[g][s] + (1 - bit) * half
        return pltpu.make_async_remote_copy(
            src_ref=work.at[g, pl.ds(away, half)],
            dst_ref=xland.at[g, pl.ds(nx - 2 * half, half)],
            send_sem=rsend.at[s, g],
            recv_sem=rrecv.at[s, g],
            device_id=(partners[orders[g][s]], me_y),
            device_id_type=MESH,
        )

    def gather_copy(g, s, landing):
        half = nx >> (s + 1)
        bit = bits[orders[g][s]]
        mine = starts[g][s + 1]
        place = starts[g][s] + (1 - bit) * half if landing else mine
        return pltpu.make_async_remote_copy(
            src_ref=sum_ref.at[g, pl.ds(mine, half)],
            dst_ref=sum_ref.at[g, pl.ds(place, half)],
            send_sem=gsend.at[s, g],
            recv_sem=grecv.at[s, g],
            device_id=(partners[orders[g][s]], me_y),
            device_id_type=MESH,
        )

    for g in range(groups):
        for step in range(1, ny):
            column_copy(step, g).start()
    sides(lambda a, b: side_copy(a, b).start(), 1)

    def begin(g):
        value = wpart_ref[me_y, g].astype(jnp.float32)
        for step in range(1, ny):
            column_copy(step, g).wait_recv()
            value = value + yland[step - 1, g].astype(jnp.float32)
        work[g] = value.astype(work.dtype)
        scatter_copy(g, 0).start()

    def scatter(g, s):
        half = nx >> (s + 1)
        scatter_copy(g, s).wait_recv()
        keep = pl.ds(starts[g][s + 1], half)
        value = work[g, keep].astype(jnp.float32) + xland[g, pl.ds(nx - 2 * half, half)].astype(
            jnp.float32
        )
        if s < steps - 1:
            work[g, keep] = value.astype(work.dtype)
            scatter_copy(g, s + 1).start()
        else:
            sum_ref[g, keep] = value.astype(sum_ref.dtype)
            gather_copy(g, s, False).start()

    def gather(g, s):
        gather_copy(g, s, True).wait_recv()
        if s > 0:
            gather_copy(g, s - 1, False).start()

    events = []
    for g in range(groups):
        events.append((WAVES[g] * STAGGER, g, functools.partial(begin, g)))
        for s in range(steps):
            events.append((WAVES[g] * STAGGER + s + 1, g, functools.partial(scatter, g, s)))
            events.append(
                (WAVES[g] * STAGGER + 2 * steps - s, g, functools.partial(gather, g, s))
            )
    events.sort(key=lambda event: event[:2])
    first = [event[2] for event in events if event[0] < HALO_AT]
    rest = [event[2] for event in events if event[0] >= HALO_AT]
    for event in first:
        event()

    returned_ref[...] = jnp.zeros(returned_ref.shape, jnp.float32)
    for b in (0, 2):

        @pl.when(exists(me_y + 1 - b, ny))
        def _():
            side_copy(1, b).wait_recv()
            returned_ref[...] += side_land[1, b // 2].astype(jnp.float32)

    for a in (0, 2):

        @pl.when(exists(me_x + a - 1, nx))
        def _():
            for b in (0, 2):
                missing = jnp.logical_not(exists(me_y + 1 - b, ny))

                @pl.when(missing)
                def _():
                    side_land[a, b // 2] = jnp.zeros(side_land.shape[2:], side_land.dtype)

                @pl.when(jnp.logical_not(missing))
                def _():
                    side_copy(a, b).wait_recv()

            column[a // 2] = (
                borrowed_ref[3 * a + 1].astype(jnp.float32)
                + side_land[a, 0].astype(jnp.float32)
                + side_land[a, 1].astype(jnp.float32)
            ).astype(column.dtype)
            back_copy(a).start()

    for event in rest:
        event()

    for a in (0, 2):

        @pl.when(exists(me_x + 1 - a, nx))
        def _():
            back_copy(a).wait_recv()
            returned_ref[...] += x_land[a // 2].astype(jnp.float32)

    for g in range(groups):
        for step in range(1, ny):
            column_copy(step, g).wait_send()
        for s in range(steps):
            scatter_copy(g, s).wait_send()
            gather_copy(g, s, False).wait_send()
    sides(lambda a, b: side_copy(a, b).wait_send(), 1)
    for a in (0, 2):

        @pl.when(exists(me_x + a - 1, nx))
        def _():
            back_copy(a).wait_send()


def gather_kernel(
    nx,
    ny,
    send_in,
    feats_ref,
    weight_ref,
    bias_ref,
    table_ref,
    turned_ref,
    full_ref,
    pre_ref,
    grad_ref,
    send_ref,
    own,
    stage,
    bias,
    lsem,
    xsend,
    xrecv,
    hsend,
    hrecv,
    wsend,
    wrecv,
):
    me_x, me_y = lax.axis_index("gx"), lax.axis_index("gy")
    blocks, rows, width = feats_ref.shape
    shared_count = stage.shape[0]
    f32 = jnp.float32
    barrier = pltpu.get_barrier_semaphore()
    expected = greet_neighbours(barrier, me_x, me_y, nx, ny) + greet_column(
        barrier, me_x, me_y, ny
    )
    load = pltpu.make_async_copy(feats_ref, own, lsem.at[0])
    load.start()
    pick = pltpu.make_async_copy(send_in, send_ref, lsem.at[3])
    pick.start()
    file = pltpu.make_async_copy(feats_ref, table_ref.at[pl.ds(0, blocks)], lsem.at[4])
    file.start()
    shift = pltpu.make_async_copy(bias_ref, bias, lsem.at[2])
    shift.start()
    keep = pltpu.make_async_copy(weight_ref, full_ref.at[:, me_y], lsem.at[1])
    keep.start()
    pick.wait()
    load.wait()
    for s in range(shared_count):
        stage[s] = own[send_ref[s]]
    pl.semaphore_wait(barrier, expected)

    def first(a, b):
        d = 3 * a + b
        return blocks + shared_count * (d - (d > 4))

    def place(a, b):
        return table_ref.at[pl.ds(first(a, b), shared_count)]

    def x_copy(a, device_x):
        return pltpu.make_async_remote_copy(
            src_ref=stage,
            dst_ref=place(a, 1),
            send_sem=xsend.at[a // 2],
            recv_sem=xrecv.at[a // 2],
            device_id=(device_x, me_y),
            device_id_type=MESH,
        )

    def y_copy(a, b, device_y):
        return pltpu.make_async_remote_copy(
            src_ref=stage if a == 1 else place(a, 1),
            dst_ref=place(a, b),
            send_sem=hsend.at[a, b // 2],
            recv_sem=hrecv.at[a, b // 2],
            device_id=(me_x, device_y),
            device_id_type=MESH,
        )

    def weight_copy(step, owner):
        return pltpu.make_async_remote_copy(
            src_ref=weight_ref,
            dst_ref=full_ref.at[:, owner],
            send_sem=wsend.at[step],
            recv_sem=wrecv.at[step],
            device_id=(me_x, lax.rem(me_y + step, ny)),
            device_id_type=MESH,
        )

    def to_column(a, act):
        for b in (0, 2):
            target = me_y + 1 - b

            @pl.when(exists(target, ny))
            def _():
                act(y_copy(a, b, target))

    def turn(t, count):
        for at in range(t, t + count):
            turned_ref[at] = table_ref[at].T

    def clear(a, b):
        for at in range(first(a, b), first(a, b) + shared_count):
            table_ref[at] = jnp.zeros((rows, width), table_ref.dtype)

    for a in (0, 2):
        target = me_x + 1 - a

        @pl.when(exists(target, nx))
        def _():
            x_copy(a, target).start()

    to_column(1, lambda copy: copy.start())
    for step in range(1, ny):
        weight_copy(step, me_y).start()
    for a in (0, 2):

        @pl.when(jnp.logical_not(exists(me_x + a - 1, nx)))
        def _():
            clear(a, 1)

        for b in (0, 2):

            @pl.when(jnp.logical_not(exists(me_x + a - 1, nx) & exists(me_y + b - 1, ny)))
            def _():
                clear(a, b)

    for b in (0, 2):

        @pl.when(jnp.logical_not(exists(me_y + b - 1, ny)))
        def _():
            clear(1, b)

    file.wait()
    turn(0, blocks)
    shift.wait()
    for b in range(blocks):
        pre_ref[b] = jnp.broadcast_to(bias[...], (rows, width))
    pre_ref[blocks] = jnp.zeros((rows, width), f32)

    def blank(t, carry):
        grad_ref[t] = jnp.zeros((rows, width), f32)
        return carry

    lax.fori_loop(0, grad_ref.shape[0], blank, 0)

    def arrive(a, b):
        @pl.when(exists(me_x + a - 1, nx) & exists(me_y + b - 1, ny))
        def _():
            y_copy(a, b, me_y + b - 1).wait_recv()

        turn(first(a, b), shared_count)

    for b in (0, 2):
        arrive(1, b)
    for a in (0, 2):

        @pl.when(exists(me_x + a - 1, nx))
        def _():
            x_copy(a, me_x + a - 1).wait_recv()
            to_column(a, lambda copy: copy.start())

        turn(first(a, 1), shared_count)
    for a in (0, 2):
        for b in (0, 2):
            arrive(a, b)

    for a in range(3):

        @pl.when(exists(me_x + a - 1, nx))
        def _():
            to_column(a, lambda copy: copy.wait_send())

    for a in (0, 2):
        target = me_x + 1 - a

        @pl.when(exists(target, nx))
        def _():
            x_copy(a, target).wait_send()

    for step in range(1, ny):
        weight_copy(step, lax.rem(me_y - step + ny, ny)).wait_recv()
        weight_copy(step, me_y).wait_send()
    keep.wait()


def layer_kernel(
    source_ref,
    target_ref,
    count_ref,
    table,
    weight_ref,
    cot_ref,
    pre_in,
    grad_in,
    out_ref,
    pre,
    grad,
    borrowed_ref,
    dpre_ref,
    out,
    osem,
):
    blocks, rows, width = cot_ref.shape
    slots = source_ref.shape[0]
    kvol = weight_ref.shape[0]
    total_blocks = table.shape[0]
    shared_count = borrowed_ref.shape[1]
    f32 = jnp.float32
    dpre_ref[blocks] = jnp.zeros((rows, width), dpre_ref.dtype)

    def forward(k, carry):
        live = count_ref[k]
        taken, targets = [], []
        for q in range(slots):
            taken.append(table[jnp.where(q < live, source_ref[q, k], 0)])
            targets.append(jnp.where(q < live, target_ref[q, k], blocks))
        made = jnp.dot(jnp.concatenate(taken, axis=0), weight_ref[k], preferred_element_type=f32)
        for q, target in enumerate(targets):
            pre[target] += made[q * rows : (q + 1) * rows]
        return carry

    lax.fori_loop(0, kvol, forward, 0, unroll=UNROLL)

    def activate(b, carry):
        value = pre[b]
        sig = jax.nn.sigmoid(value)
        out[b] = (value * sig).astype(out.dtype)
        dpre_ref[b] = (cot_ref[b].astype(f32) * sig * (1.0 + value * (1.0 - sig))).astype(
            dpre_ref.dtype
        )
        return carry

    lax.fori_loop(0, blocks, activate, 0)
    keep = pltpu.make_async_copy(out, out_ref, osem)
    keep.start()

    def backward(k, carry):
        live = count_ref[k]
        pulled, spread = [], []
        for q in range(slots):
            pulled.append(dpre_ref[jnp.where(q < live, target_ref[q, k], blocks)])
            spread.append(jnp.where(q < live, source_ref[q, k], total_blocks))
        back = lax.dot_general(
            jnp.concatenate(pulled, axis=0),
            weight_ref[k],
            (((1,), (1,)), ((), ())),
            preferred_element_type=f32,
        )
        for q, source in enumerate(spread):
            grad[source] += back[q * rows : (q + 1) * rows]
        return carry

    lax.fori_loop(0, kvol, backward, 0, unroll=UNROLL)
    at = blocks
    for d in range(9):
        for s in range(shared_count):
            if d != 4:
                borrowed_ref[d, s] = grad[at].astype(borrowed_ref.dtype)
                at += 1
    keep.wait()


def line_kernel(
    nx,
    ny,
    source_ref,
    target_ref,
    count_ref,
    send_in,
    turned_ref,
    dpre_ref,
    own_ref,
    borrowed_ref,
    wide_ref,
    feat_ref,
    send_ref,
    away,
    sums,
    back,
    work,
    yland,
    full_land,
    half_land,
    land,
    spare,
    side_land,
    column,
    x_land,
    ysend,
    csend,
    crecv,
    hsend,
    hrecv,
    bsend,
    brecv,
    picksem,
):
    me_x, me_y = lax.axis_index("gx"), lax.axis_index("gy")
    kvol, parts, deep, width = work.shape
    slots = source_ref.shape[0]
    blocks, rows = feat_ref.shape[:2]
    f32 = jnp.float32
    bit_x, bit_y, z = lax.rem(me_x, 2), lax.rem(me_x // 2, 2), me_x // 4
    high = z // 2
    beside = {"x": me_x + 1 - 2 * bit_x, "y": me_x + 2 - 4 * bit_y}
    inner = exists(z - 1, 2)
    near = jnp.where(inner, me_x - 4 + 8 * high, me_x + 4 - 8 * high)
    opposite = me_x + 12 - 8 * z

    pick = pltpu.make_async_copy(send_in, send_ref, picksem)
    pick.start()
    barrier = pltpu.get_barrier_semaphore()
    expected = greet_neighbours(barrier, me_x, me_y, nx, ny) + greet_column(
        barrier, me_x, me_y, ny
    )
    greeted = (beside["x"], beside["y"], near, opposite)
    for device in greeted:
        pl.semaphore_signal(barrier, inc=1, device_id=(device, me_y), device_id_type=MESH)

    def multiply(g, carry):
        live = count_ref[g]
        taken, pulled = [], []
        for q in range(slots):
            taken.append(turned_ref[jnp.where(q < live, source_ref[q, g], 0)])
            pulled.append(dpre_ref[jnp.where(q < live, target_ref[q, g], blocks)])
        part = jnp.dot(
            jnp.concatenate(taken, axis=1),
            jnp.concatenate(pulled, axis=0),
            preferred_element_type=f32,
        ).astype(work.dtype).reshape(ny, parts, deep, width)
        for y in range(ny):
            step = lax.rem(y - me_y + ny, ny)
            for d in range(ny):

                @pl.when(step == d)
                def _():
                    if d == 0:
                        work[g] = part[y]
                    else:
                        away[d - 1, g] = part[y]

        return carry

    lax.fori_loop(0, MAKE_FIRST, multiply, 0)

    pl.semaphore_wait(barrier, expected + len(greeted))

    pick.wait()

    def side_copy(a, b):
        return pltpu.make_async_remote_copy(
            src_ref=borrowed_ref.at[3 * a + b],
            dst_ref=side_land.at[a, b // 2],
            send_sem=hsend.at[a, b // 2],
            recv_sem=hrecv.at[a, b // 2],
            device_id=(me_x, me_y + b - 1),
            device_id_type=MESH,
        )

    def back_copy(a):
        return pltpu.make_async_remote_copy(
            src_ref=column.at[a // 2],
            dst_ref=x_land.at[a // 2],
            send_sem=bsend.at[a // 2],
            recv_sem=brecv.at[a // 2],
            device_id=(me_x + a - 1, me_y),
            device_id_type=MESH,
        )

    def sides(act, sign):
        for a in range(3):
            for b in (0, 2):

                @pl.when(exists(me_x + a - 1, nx) & exists(me_y + sign * (b - 1), ny))
                def _():
                    act(a, b)

    def column_copy(step, g):
        other = lax.rem(me_y + step, ny)
        return pltpu.make_async_remote_copy(
            src_ref=away.at[step - 1, g],
            dst_ref=yland.at[step - 1, g],
            send_sem=ysend.at[step - 1],
            recv_sem=crecv.at[4 + step - 1, g],
            device_id=(me_x, other),
            device_id_type=MESH,
        )

    def share(g, carry):
        for step in range(1, ny):
            column_copy(step, g).start()
        return carry

    def make(g, carry):
        return share(g, multiply(g, carry))

    lax.fori_loop(0, MAKE_FIRST, share, 0)
    sides(lambda a, b: side_copy(a, b).start(), 1)

    def give_back():
        back[...] = jnp.zeros(back.shape, f32)
        for b in (0, 2):

            @pl.when(exists(me_y + 1 - b, ny))
            def _():
                side_copy(1, b).wait_recv()
                back[...] += side_land[1, b // 2].astype(f32)

        for a in (0, 2):

            @pl.when(exists(me_x + a - 1, nx))
            def _():
                for b in (0, 2):
                    missing = jnp.logical_not(exists(me_y + 1 - b, ny))

                    @pl.when(missing)
                    def _():
                        side_land[a, b // 2] = jnp.zeros(side_land.shape[2:], side_land.dtype)

                    @pl.when(jnp.logical_not(missing))
                    def _():
                        side_copy(a, b).wait_recv()

                column[a // 2] = (
                    borrowed_ref[3 * a + 1].astype(f32)
                    + side_land[a, 0].astype(f32)
                    + side_land[a, 1].astype(f32)
                ).astype(column.dtype)
                back_copy(a).start()

    def take_back():
        for a in (0, 2):

            @pl.when(exists(me_x + 1 - a, nx))
            def _():
                back_copy(a).wait_recv()
                back[...] += x_land[a // 2].astype(f32)

        for b in range(blocks):
            value = own_ref[b]
            for s in range(back.shape[0]):
                value = value + jnp.where(send_ref[s] == b, back[s], 0.0)
            feat_ref[b] = value.astype(feat_ref.dtype)

    def own_sum(g):
        value = work[g].astype(f32)
        for step in range(1, ny):
            column_copy(step, g).wait_recv()
            value = value + yland[step - 1, g].astype(f32)
        return value

    def copy(g, src, dst, leave, arrive, device):
        return pltpu.make_async_remote_copy(
            src_ref=src,
            dst_ref=dst,
            send_sem=csend.at[leave],
            recv_sem=crecv.at[arrive, g],
            device_id=(device, me_y),
            device_id_type=MESH,
        )

    def program(order, inside):
        sent = {}
        made = MAKE_FIRST

        def send(g, src, dst, leave, arrive, device):
            copy(g, src, dst, leave, arrive, device).start()
            sent[leave] = sent.get(leave, 0) + math.prod(src.shape[:-2])

        def recv(g, dst, arrive):
            copy(g, dst, dst, 0, arrive, beside["x"]).wait_recv()

        def finish(g):
            wide_ref[g] = sums[g].reshape(parts * deep, width).astype(f32) * (1.0 / rows)

        def along(g, k):
            first = LINE_KINDS[g][1]
            second = "y" if first == "x" else "x"
            bits = {"x": bit_x, "y": bit_y}
            hb, qb = bits[first], bits[second]
            mine, other = 2 * hb + qb, 2 * hb + 1 - qb
            kept, gone = pl.ds(2 * hb, 2), pl.ds(2 - 2 * hb, 2)
            total, ours = sums.at[g], work.at[g]
            if k == 0:
                work[g] = own_sum(g).astype(work.dtype)
                send(g, ours.at[gone], half_land.at[g], 0, 0, beside[first])
            elif k == 1:
                recv(g, half_land.at[g], 0)
                work[g, kept] = (
                    work[g, kept].astype(f32) + half_land[g].astype(f32)
                ).astype(work.dtype)
                send(g, ours.at[other], land.at[0, g], 1, 1, beside[second])
            elif k == 2:
                recv(g, land.at[0, g], 1)
                work[g, mine] = (
                    work[g, mine].astype(f32) + land[0, g].astype(f32)
                ).astype(work.dtype)
                if not inside:
                    send(g, ours.at[mine], land.at[1, g], 2, 2, near)
            elif k == 3:
                recv(g, land.at[1, g], 2)
                work[g, mine] = (
                    work[g, mine].astype(f32) + land[1, g].astype(f32)
                ).astype(work.dtype)
                send(g, ours.at[mine], land.at[2, g], 3, 3, opposite)
            elif k == 4:
                recv(g, land.at[2, g], 3)
                sums[g, mine] = (
                    work[g, mine].astype(f32) + land[2, g].astype(f32)
                ).astype(sums.dtype)
                send(g, total.at[mine], total.at[mine], 2, 2, near)
                send(g, total.at[mine], total.at[mine], 4, 0, beside[second])
            elif k == 5:
                recv(g, total.at[mine], 2)
                send(g, total.at[mine], total.at[mine], 4, 0, beside[second])
            elif k == 6:
                recv(g, total.at[other], 0)
                send(g, total.at[kept], total.at[kept], 5, 4, beside[first])
            elif k == 7:
                recv(g, total.at[gone], 4)
                finish(g)

        def fold(g, k):
            first = LINE_KINDS[g][1]
            second = "y" if first == "x" else "x"
            bits = {"x": bit_x, "y": bit_y}
            hb, qb = high, bits[first]
            mine, other = 2 * hb + qb, 2 * hb + 1 - qb
            kept, gone = pl.ds(2 * hb, 2), pl.ds(2 - 2 * hb, 2)
            total, ours = sums.at[g], work.at[g]
            hub = inside if LINE_KINDS[g][0] == "B" else not inside
            if not hub:
                if k == 0:
                    work[g] = own_sum(g).astype(work.dtype)
                    send(g, ours, full_land.at[g], 6, 2, near)
                elif k == 6:
                    recv(g, total.at[kept], 2)
                elif k == 7:
                    recv(g, total.at[gone], 3)
                    finish(g)
            elif k == 1:
                value = own_sum(g)
                recv(g, full_land.at[g], 2)
                work[g] = (value + full_land[g].astype(f32)).astype(work.dtype)
                send(g, ours.at[gone], half_land.at[g], 7, 3, opposite)
            elif k == 2:
                recv(g, half_land.at[g], 3)
                work[g, kept] = (
                    work[g, kept].astype(f32) + half_land[g].astype(f32)
                ).astype(work.dtype)
                send(g, ours.at[other], land.at[0, g], 1, 0, beside[first])
            elif k == 3:
                recv(g, land.at[0, g], 0)
                work[g, mine] = (
                    work[g, mine].astype(f32) + land[0, g].astype(f32)
                ).astype(work.dtype)
                send(g, ours.at[mine], land.at[1, g], 1, 1, beside[second])
            elif k == 4:
                recv(g, land.at[1, g], 1)
                sums[g, mine] = (
                    work[g, mine].astype(f32) + land[1, g].astype(f32)
                ).astype(sums.dtype)
                send(g, total.at[mine], total.at[mine], 4, 4, beside[first])
            elif k == 5:
                recv(g, total.at[other], 4)
                send(g, total.at[kept], total.at[kept], 8, 2, opposite)
                send(g, total.at[kept], total.at[kept], 8, 2, near)
            elif k == 6:
                recv(g, total.at[gone], 2)
                send(g, total.at[gone], total.at[gone], 8, 3, near)
                finish(g)

        for event in order:
            g, k = divmod(event, 10)
            while made < kvol and g < kvol and made <= g + MAKE_LEAD:
                upto = min(kvol, made + MAKE_STEP)
                lax.fori_loop(made, upto, make, 0)
                made = upto
            if g == kvol:
                (give_back, take_back)[k]()
            elif LINE_KINDS[g][0] != "A":
                fold(g, k)
            else:
                along(g, k)
        for leave, pieces in sent.items():
            gone = spare.at[pl.ds(0, pieces)]
            copy(0, gone, gone, leave, 0, beside["x"]).wait_send()

    @pl.when(inner)
    def _():
        program(LINE_ORDERS[0], True)

    @pl.when(jnp.logical_not(inner))
    def _():
        program(LINE_ORDERS[1], False)

    for step in range(1, ny):
        other = lax.rem(me_y + step, ny)
        pltpu.make_async_remote_copy(
            src_ref=away.at[step - 1],
            dst_ref=yland.at[step - 1],
            send_sem=ysend.at[step - 1],
            recv_sem=crecv.at[4 + step - 1, 0],
            device_id=(me_x, other),
            device_id_type=MESH,
        ).wait_send()
    sides(lambda a, b: side_copy(a, b).wait_send(), 1)
    for a in (0, 2):

        @pl.when(exists(me_x + a - 1, nx))
        def _():
            back_copy(a).wait_send()


def finish_kernel(
    send_ref, total_ref, own_ref, returned_ref, weight_ref, feat_ref, wide, feats, wsem, fsem
):
    chunks = wsem.shape[0]
    kvol, share, width = wide.shape
    per = kvol // chunks
    blocks, rows = feat_ref.shape[:2]
    copies = []
    for c in range(chunks):
        at = pl.ds(c * per, per)
        for h in range(width // LANES):
            wide[at, :, h * LANES : (h + 1) * LANES] = total_ref[h, at].reshape(
                per, share, LANES
            ).astype(jnp.float32) * (1.0 / rows)
        copy = pltpu.make_async_copy(wide.at[at], weight_ref.at[at], wsem.at[c])
        copy.start()
        copies.append(copy)
    for b in range(blocks):
        value = own_ref[b]
        for s in range(returned_ref.shape[0]):
            value = value + jnp.where(send_ref[s] == b, returned_ref[s], 0.0)
        feats[b] = value.astype(feats.dtype)
        copy = pltpu.make_async_copy(feats.at[b], feat_ref.at[b], fsem.at[b])
        copy.start()
        copies.append(copy)
    for copy in copies:
        copy.wait()


def store_kernel(wide_ref, feat_ref, weight_out, feat_out, sem):
    chunks = sem.shape[0] - 1
    per = wide_ref.shape[0] // chunks
    copies = [pltpu.make_async_copy(feat_ref, feat_out, sem.at[chunks])]
    for c in range(chunks):
        at = pl.ds(c * per, per)
        copies.append(pltpu.make_async_copy(wide_ref.at[at], weight_out.at[at], sem.at[c]))
    for copy in copies:
        copy.start()
    for copy in copies:
        copy.wait()


def on_device(
    nx,
    ny,
    features,
    kernel_weight,
    channel_bias,
    send_list,
    rule_source,
    rule_target,
    live_counts,
    out_grad,
):
    feats = features[0, 0]
    blocks, rows, width = feats.shape
    shared = send_list[0, 0]
    shared_count = shared.shape[0]
    kvol, slots = rule_source.shape[2:]
    share = kernel_weight.shape[1]
    bf16, f32 = jnp.bfloat16, jnp.float32
    shape = jax.ShapeDtypeStruct
    vmem = pl.BlockSpec(memory_space=VMEM)
    smem = pl.BlockSpec(memory_space=SMEM)
    hbm = pl.BlockSpec(memory_space=pltpu.HBM)
    dma = pltpu.SemaphoreType.DMA
    squares = 9

    total_blocks = blocks + (squares - 1) * shared_count
    if nx == 4 * LINE_LENGTH and kvol == len(LINE_KINDS):
        stay = functools.partial(pltpu.with_memory_space_constraint, memory_space=pltpu.HBM)
        rules = (rule_source[0, 0].T, rule_target[0, 0].T, live_counts.reshape(-1))
        boundary = (shared_count, rows, width)
        quarters = (4, share // 4, width)
        table, turned, full, pre, grad = pl.pallas_call(
            functools.partial(gather_kernel, nx, ny),
            out_shape=(
                shape((total_blocks, rows, width), bf16),
                shape((total_blocks, width, rows), bf16),
                shape((kvol, ny, share, width), bf16),
                shape((blocks + 1, rows, width), f32),
                shape((total_blocks + 1, rows, width), f32),
            ),
            in_specs=[hbm] * 4,
            out_specs=(vmem,) * 5,
            scratch_shapes=[
                SMEM((shared_count,), jnp.int32),
                VMEM((blocks, rows, width), bf16),
                VMEM(boundary, bf16),
                VMEM((1, width), f32),
                dma((5,)),
                dma((2,)),
                dma((2,)),
                dma((3, 2)),
                dma((3, 2)),
                dma((ny,)),
                dma((ny,)),
            ],
            compiler_params=pltpu.CompilerParams(
                collective_id=3, has_side_effects=True, vmem_limit_bytes=GATHER_BYTES
            ),
        )(*(stay(v) for v in (shared, feats, kernel_weight, channel_bias.reshape(1, width))))
        outputs, _, grad, borrowed, dpre = pl.pallas_call(
            layer_kernel,
            out_shape=(
                shape((blocks, rows, width), bf16),
                shape((blocks + 1, rows, width), f32),
                shape((total_blocks + 1, rows, width), f32),
                shape((squares,) + boundary, bf16),
                shape((blocks + 1, rows, width), bf16),
            ),
            in_specs=[smem, smem, smem, vmem, vmem, vmem, vmem, vmem],
            out_specs=(hbm, vmem, vmem, vmem, vmem),
            scratch_shapes=[VMEM((blocks, rows, width), bf16), dma(())],
            input_output_aliases={6: 1, 7: 2},
            compiler_params=pltpu.CompilerParams(vmem_limit_bytes=LAYER_BYTES),
        )(
            *rules,
            table,
            full.reshape(kvol, width, width),
            out_grad[0, 0],
            pre,
            grad,
        )
        wide, feat = pl.pallas_call(
            functools.partial(line_kernel, nx, ny),
            out_shape=(shape((kvol, share, width), f32), shape((blocks, rows, width), bf16)),
            in_specs=[smem, smem, smem, hbm, vmem, vmem, vmem, vmem],
            out_specs=(vmem, vmem),
            scratch_shapes=[
                SMEM((shared_count,), jnp.int32),
                VMEM((max(ny - 1, 1), kvol) + quarters, bf16),
                VMEM((kvol,) + quarters, bf16),
                VMEM(boundary, f32),
                VMEM((kvol,) + quarters, bf16),
                VMEM((max(ny - 1, 1), kvol) + quarters, bf16),
                VMEM((kvol,) + quarters, bf16),
                VMEM((kvol, 2) + quarters[1:], bf16),
                VMEM((3, kvol) + quarters[1:], bf16),
                VMEM((8 * kvol,) + quarters[1:], bf16),
                VMEM((3, 2) + boundary, bf16),
                VMEM((2,) + boundary, bf16),
                VMEM((2,) + boundary, bf16),
                dma((max(ny - 1, 1),)),
                dma((9,)),
                dma((4 + max(ny - 1, 1), kvol)),
                dma((3, 2)),
                dma((3, 2)),
                dma((2,)),
                dma((2,)),
                dma(()),
            ],
            compiler_params=pltpu.CompilerParams(
                collective_id=2, has_side_effects=True, vmem_limit_bytes=LINE_BYTES
            ),
        )(*rules, stay(shared), turned, dpre, grad, borrowed)
        chunks = max(c for c in range(1, 10) if kvol % c == 0)
        weight_grad, feat_grad = pl.pallas_call(
            store_kernel,
            out_shape=(shape((kvol, share, width), f32), shape((blocks, rows, width), bf16)),
            in_specs=[vmem, vmem],
            out_specs=(hbm, hbm),
            scratch_shapes=[dma((chunks + 1,))],
            compiler_params=pltpu.CompilerParams(vmem_limit_bytes=VMEM_BYTES),
        )(wide, feat)
        return (outputs[None, None], feat_grad[None, None], weight_grad)

    halo, full = pl.pallas_call(
        functools.partial(exchange_kernel, nx, ny),
        out_shape=(
            shape((squares, shared_count, rows, width), bf16),
            shape((kvol, ny, share, width), bf16),
        ),
        in_specs=[smem, hbm, hbm],
        out_specs=(vmem, vmem),
        scratch_shapes=[
            VMEM((blocks, rows, width), bf16),
            dma((2,)),
            dma((2,)),
            dma((2,)),
            dma((3, 2)),
            dma((3, 2)),
            dma((ny,)),
            dma((ny,)),
        ],
        compiler_params=pltpu.CompilerParams(
            collective_id=0, has_side_effects=True, vmem_limit_bytes=EXCHANGE_BYTES
        ),
    )(shared, feats, kernel_weight)

    used = (width // LANES) * kvol * (share // TILE)
    groups = len(KINDS)
    unit = groups * nx
    tiles = -(-used // unit) * unit
    depth = tiles // unit
    outputs, own, borrowed, wpart = pl.pallas_call(
        compute_kernel,
        out_shape=(
            shape((blocks, rows, width), bf16),
            shape((blocks, rows, width), f32),
            shape((squares, shared_count, rows, width), bf16),
            shape((ny, tiles, TILE, LANES), bf16),
        ),
        in_specs=[smem, smem, smem, vmem, vmem, vmem, vmem, vmem],
        out_specs=(vmem, vmem, vmem, vmem),
        scratch_shapes=[
            VMEM((total_blocks, rows, width), bf16),
            VMEM((total_blocks, width, rows), bf16),
            VMEM((blocks + 1, rows, width), f32),
            VMEM((blocks + 1, rows, width), bf16),
            VMEM((total_blocks + 1, rows, width), f32),
        ],
        compiler_params=pltpu.CompilerParams(vmem_limit_bytes=VMEM_BYTES),
    )(
        rule_source[0, 0].T,
        rule_target[0, 0].T,
        live_counts.reshape(-1),
        feats,
        halo,
        full.reshape(kvol, width, width),
        channel_bias.reshape(1, width),
        out_grad[0, 0],
    )

    steps = nx.bit_length() - 1
    block = (depth, TILE, LANES)
    boundary = (shared_count, rows, width)
    total, returned = pl.pallas_call(
        functools.partial(reduce_kernel, nx, ny),
        out_shape=(
            shape((groups, nx) + block, bf16),
            shape(boundary, f32),
        ),
        in_specs=[vmem, vmem],
        out_specs=(vmem, vmem),
        scratch_shapes=[
            VMEM((groups, nx) + block, bf16),
            VMEM((max(ny - 1, 1), groups, nx) + block, bf16),
            VMEM((groups, nx) + block, bf16),
            VMEM((3, 2) + boundary, bf16),
            VMEM((2,) + boundary, bf16),
            VMEM((2,) + boundary, bf16),
            dma((max(ny - 1, 1), groups)),
            dma((max(ny - 1, 1), groups)),
            dma((steps, groups)),
            dma((steps, groups)),
            dma((steps, groups)),
            dma((steps, groups)),
            dma((3, 2)),
            dma((3, 2)),
            dma((2,)),
            dma((2,)),
        ],
        compiler_params=pltpu.CompilerParams(
            collective_id=1, has_side_effects=True, vmem_limit_bytes=VMEM_BYTES
        ),
    )(wpart.reshape((ny, groups, nx) + block), borrowed)

    halves, share_tiles = width // LANES, share // TILE
    chunks = max(c for c in range(1, 10) if kvol % c == 0)
    weight_grad, feat_grad = pl.pallas_call(
        finish_kernel,
        out_shape=(shape((kvol, share, width), f32), shape((blocks, rows, width), bf16)),
        in_specs=[smem, vmem, vmem, vmem],
        out_specs=(hbm, hbm),
        scratch_shapes=[
            VMEM((kvol, share, width), f32),
            VMEM((blocks, rows, width), bf16),
            dma((chunks,)),
            dma((blocks,)),
        ],
        compiler_params=pltpu.CompilerParams(vmem_limit_bytes=VMEM_BYTES),
    )(
        shared,
        total.reshape(tiles, TILE, LANES)[:used].reshape(halves, kvol, share_tiles, TILE, LANES),
        own,
        returned,
    )
    return (outputs[None, None], feat_grad[None, None], weight_grad)


def solution(mesh):
    return jax.shard_map(
        functools.partial(on_device, mesh.shape["gx"], mesh.shape["gy"]),
        mesh=mesh,
        in_specs=(
            P("gx", "gy", None, None, None),
            P(None, "gy", None),
            P(),
            P("gx", "gy", None),
            P("gx", "gy", None, None),
            P("gx", "gy", None, None),
            P("gx", "gy", None),
            P("gx", "gy", None, None, None),
        ),
        out_specs=(
            P("gx", "gy", None, None, None),
            P("gx", "gy", None, None, None),
            P(None, "gy", None),
        ),
        check_vma=False,
    )
```

```python
import functools
import math

import jax
import jax.numpy as jnp
from jax import lax
from jax.experimental import pallas as pl
from jax.experimental.pallas import tpu as pltpu
from jax.sharding import PartitionSpec as P

MESH = pl.DeviceIdType.MESH
VMEM = pltpu.VMEM
SMEM = pltpu.SMEM
LANES = 128
TILE = 16
KINDS = (2, 0, 1, 3, 0, 1, 0, 1, 0)
WAVES = (0,) * 9
STAGGER = 1
HALO_AT = 4
UNROLL = 9
VMEM_BYTES = 28 * 1024 * 1024
EXCHANGE_BYTES = 28 * 1024 * 1024
LINE_BYTES = 28 * 1024 * 1024
GATHER_BYTES = 40 * 1024 * 1024
LAYER_BYTES = 28 * 1024 * 1024
LINE_LENGTH = 4
MAKE_FIRST = 10
MAKE_STEP = 3
MAKE_LEAD = 3

LINE_KINDS = (
    'Cy', 'Ay', 'Ax', 'By', 'Ay', 'Ax', 'Ay', 'Ax', 'By',
    'Cy', 'Ay', 'Ax', 'Ay', 'Ax', 'By', 'Cy', 'Ay', 'Ax',
    'Ay', 'Ax', 'Ax', 'Ay', 'Ax', 'Ay', 'Ax', 'Ay', 'Ax',
)
LINE_ORDERS = (
(
    0, 10, 20, 40, 50, 60, 70, 90, 100, 110, 120, 130, 150, 160, 170, 180,
    190, 31, 21, 200, 210, 11, 51, 220, 81, 230, 41, 71, 240, 250, 141, 260,
    22, 111, 131, 61, 12, 171, 101, 52, 191, 121, 201, 161, 42, 221, 181, 72,
    32, 211, 241, 231, 82, 251, 112, 261, 132, 23, 62, 142, 172, 13, 102, 192,
    53, 122, 270, 202, 162, 222, 43, 182, 73, 212, 242, 232, 252, 113, 262, 24,
    133, 14, 63, 54, 103, 123, 44, 173, 74, 193, 163, 183, 33, 114, 203, 83,
    134, 213, 143, 64, 233, 104, 253, 124, 223, 174, 243, 194, 263, 271, 164, 184,
    34, 204, 84, 26, 214, 144, 234, 254, 16, 224, 244, 56, 264, 76, 35, 46,
    116, 27, 66, 136, 106, 17, 85, 176, 126, 57, 196, 166, 77, 145, 47, 206,
    186, 117, 6, 67, 226, 216, 137, 107, 246, 36, 236, 177, 96, 127, 266, 256,
    86, 197, 167, 207, 156, 187, 146, 227, 7, 217, 247, 237, 267, 97, 257, 157,
),
(
    10, 20, 30, 40, 50, 60, 70, 80, 100, 110, 120, 130, 140, 160, 170, 180,
    190, 1, 21, 200, 210, 11, 51, 220, 91, 230, 41, 71, 240, 250, 151, 260,
    111, 22, 131, 61, 12, 171, 101, 52, 191, 121, 201, 161, 42, 221, 181, 72,
    2, 211, 241, 231, 92, 251, 112, 261, 132, 62, 102, 122, 172, 192, 162, 182,
    202, 152, 270, 212, 232, 252, 222, 242, 262, 3, 93, 25, 153, 15, 55, 45,
    75, 271, 4, 94, 26, 154, 115, 65, 135, 105, 16, 125, 56, 175, 195, 165,
    5, 46, 185, 76, 27, 205, 66, 215, 95, 235, 225, 255, 17, 245, 116, 57,
    265, 155, 106, 136, 47, 126, 176, 77, 6, 166, 196, 67, 186, 206, 36, 117,
    96, 216, 226, 107, 137, 236, 246, 127, 177, 156, 256, 266, 167, 197, 37, 187,
    207, 217, 227, 86, 87, 237, 247, 257, 267, 146, 147,
),
)


def greet_neighbours(barrier, me_x, me_y, nx, ny):
    total = 0
    for sx, sy in ((-1, 0), (1, 0), (0, -1), (0, 1)):
        x, y = me_x + sx, me_y + sy
        there = (x >= 0) & (x < nx) & (y >= 0) & (y < ny)

        @pl.when(there)
        def _():
            pl.semaphore_signal(barrier, inc=1, device_id=(x, y), device_id_type=MESH)

        total = total + there.astype(jnp.int32)
    return total


def greet_column(barrier, me_x, me_y, ny):
    for step in range(1, ny):
        pl.semaphore_signal(
            barrier, inc=1, device_id=(me_x, lax.rem(me_y + step, ny)), device_id_type=MESH
        )
    return ny - 1


def exists(index, count):
    return (index >= 0) & (index < count)


def exchange_kernel(
    nx, ny, send_ref, feats_ref, weight_ref, halo_ref, full_ref, feats, lsem, xsend, xrecv, hsend, hrecv, wsend, wrecv
):
    me_x, me_y = lax.axis_index("gx"), lax.axis_index("gy")
    barrier = pltpu.get_barrier_semaphore()
    expected = greet_neighbours(barrier, me_x, me_y, nx, ny) + greet_column(
        barrier, me_x, me_y, ny
    )
    load = pltpu.make_async_copy(feats_ref, feats, lsem.at[0])
    load.start()
    keep = pltpu.make_async_copy(weight_ref, full_ref.at[:, me_y], lsem.at[1])
    keep.start()
    load.wait()
    for s in range(halo_ref.shape[1]):
        halo_ref[4, s] = feats[send_ref[s]]
    pl.semaphore_wait(barrier, expected)

    def x_copy(a, device_x):
        return pltpu.make_async_remote_copy(
            src_ref=halo_ref.at[4],
            dst_ref=halo_ref.at[3 * a + 1],
            send_sem=xsend.at[a // 2],
            recv_sem=xrecv.at[a // 2],
            device_id=(device_x, me_y),
            device_id_type=MESH,
        )

    def y_copy(a, b, device_y):
        return pltpu.make_async_remote_copy(
            src_ref=halo_ref.at[3 * a + 1],
            dst_ref=halo_ref.at[3 * a + b],
            send_sem=hsend.at[a, b // 2],
            recv_sem=hrecv.at[a, b // 2],
            device_id=(me_x, device_y),
            device_id_type=MESH,
        )

    def weight_copy(step, owner):
        return pltpu.make_async_remote_copy(
            src_ref=weight_ref,
            dst_ref=full_ref.at[:, owner],
            send_sem=wsend.at[step],
            recv_sem=wrecv.at[step],
            device_id=(me_x, lax.rem(me_y + step, ny)),
            device_id_type=MESH,
        )

    def to_column(a, act):
        for b in (0, 2):
            target = me_y + 1 - b

            @pl.when(exists(target, ny))
            def _():
                act(y_copy(a, b, target))

    for a in (0, 2):
        target = me_x + 1 - a

        @pl.when(exists(target, nx))
        def _():
            x_copy(a, target).start()

    to_column(1, lambda copy: copy.start())
    for step in range(1, ny):
        weight_copy(step, me_y).start()
    blank = jnp.zeros(halo_ref.shape[1:], halo_ref.dtype)
    for a in (0, 2):
        here = exists(me_x + a - 1, nx)

        @pl.when(jnp.logical_not(here))
        def _():
            halo_ref[3 * a + 1] = blank

        @pl.when(here)
        def _():
            x_copy(a, me_x + a - 1).wait_recv()
            to_column(a, lambda copy: copy.start())

    for a in range(3):
        for b in (0, 2):
            there = exists(me_x + a - 1, nx) & exists(me_y + b - 1, ny)

            @pl.when(jnp.logical_not(there))
            def _():
                halo_ref[3 * a + b] = blank

            @pl.when(there)
            def _():
                y_copy(a, b, me_y + b - 1).wait_recv()

        @pl.when(exists(me_x + a - 1, nx))
        def _():
            to_column(a, lambda copy: copy.wait_send())

    for a in (0, 2):
        target = me_x + 1 - a

        @pl.when(exists(target, nx))
        def _():
            x_copy(a, target).wait_send()

    for step in range(1, ny):
        weight_copy(step, lax.rem(me_y - step + ny, ny)).wait_recv()
        weight_copy(step, me_y).wait_send()
    keep.wait()


def compute_kernel(
    source_ref,
    target_ref,
    count_ref,
    feats_ref,
    halo_ref,
    weight_ref,
    bias_ref,
    cot_ref,
    out_ref,
    own_ref,
    borrowed_ref,
    wpart_ref,
    table,
    turned,
    pre,
    dpre,
    grad,
):
    blocks, rows, width = feats_ref.shape
    slots = source_ref.shape[0]
    kvol = weight_ref.shape[0]
    total_blocks = grad.shape[0] - 1
    shared_count = halo_ref.shape[1]
    ny, tiles = wpart_ref.shape[:2]
    share = width // ny
    share_tiles = share // TILE
    places = [(b, feats_ref.at[b]) for b in range(blocks)]
    at = blocks
    for d in range(9):
        if d != 4:
            for s in range(shared_count):
                places.append((at, halo_ref.at[d, s]))
                at += 1
    for t, ref in places:
        value = ref[...]
        table[t] = value
        turned[t] = value.T
    for b in range(blocks):
        pre[b] = jnp.broadcast_to(bias_ref[...], (rows, width))
    for t in range(total_blocks):
        grad[t] = jnp.zeros((rows, width), jnp.float32)
    pre[blocks] = jnp.zeros((rows, width), jnp.float32)
    grad[total_blocks] = jnp.zeros((rows, width), jnp.float32)
    dpre[blocks] = jnp.zeros((rows, width), dpre.dtype)

    def rules(k):
        live = count_ref[k]
        sources = [source_ref[q, k] for q in range(slots)]
        targets = [target_ref[q, k] for q in range(slots)]
        reads = [jnp.where(q < live, v, 0) for q, v in enumerate(sources)]
        spread = [jnp.where(q < live, v, total_blocks) for q, v in enumerate(sources)]
        targets = [jnp.where(q < live, v, blocks) for q, v in enumerate(targets)]
        return reads, spread, targets

    def forward(k, carry):
        reads, _, targets = rules(k)
        taken = jnp.concatenate([table[s] for s in reads], axis=0)
        made = jnp.dot(taken, weight_ref[k], preferred_element_type=jnp.float32)
        for q, target in enumerate(targets):
            pre[target] += made[q * rows : (q + 1) * rows]
        return carry

    lax.fori_loop(0, kvol, forward, 0, unroll=UNROLL)

    def activate(b, carry):
        value = pre[b]
        sig = jax.nn.sigmoid(value)
        out_ref[b] = (value * sig).astype(out_ref.dtype)
        dpre[b] = (cot_ref[b].astype(jnp.float32) * sig * (1.0 + value * (1.0 - sig))).astype(
            dpre.dtype
        )
        return carry

    lax.fori_loop(0, blocks, activate, 0)

    filled = 2 * kvol * share_tiles
    if filled < tiles:
        for y in range(ny):
            wpart_ref[y, filled:] = jnp.zeros((tiles - filled, TILE, LANES), wpart_ref.dtype)

    def backward(k, carry):
        reads, spread, targets = rules(k)
        pulled = jnp.concatenate([dpre[t] for t in targets], axis=0)
        taken = jnp.concatenate([turned[s] for s in reads], axis=1)
        part = jnp.dot(taken, pulled, preferred_element_type=jnp.float32).astype(wpart_ref.dtype)
        for y in range(ny):
            for h in range(width // LANES):
                piece = part[y * share : (y + 1) * share, h * LANES : (h + 1) * LANES]
                wpart_ref[y, pl.ds((h * kvol + k) * share_tiles, share_tiles)] = piece.reshape(
                    share_tiles, TILE, LANES
                )
        back = lax.dot_general(
            pulled, weight_ref[k], (((1,), (1,)), ((), ())), preferred_element_type=jnp.float32
        )
        for q, source in enumerate(spread):
            grad[source] += back[q * rows : (q + 1) * rows]
        return carry

    lax.fori_loop(0, kvol, backward, 0, unroll=UNROLL)
    for b in range(blocks):
        own_ref[b] = grad[b]
    at = blocks
    for d in range(9):
        for s in range(shared_count):
            if d == 4:
                borrowed_ref[d, s] = jnp.zeros((rows, width), borrowed_ref.dtype)
            else:
                borrowed_ref[d, s] = grad[at].astype(borrowed_ref.dtype)
                at += 1


def reduce_kernel(
    nx,
    ny,
    wpart_ref,
    borrowed_ref,
    sum_ref,
    returned_ref,
    work,
    yland,
    xland,
    side_land,
    column,
    x_land,
    ysend,
    yrecv,
    rsend,
    rrecv,
    gsend,
    grecv,
    hsend,
    hrecv,
    bsend,
    brecv,
):
    me_x, me_y = lax.axis_index("gx"), lax.axis_index("gy")
    groups = work.shape[0]
    steps = nx.bit_length() - 1
    bits = [lax.rem(me_x // (1 << b), 2) for b in range(steps)]
    partners = [me_x + (1 - 2 * bits[b]) * (1 << b) for b in range(steps)]

    barrier = pltpu.get_barrier_semaphore()
    expected = greet_neighbours(barrier, me_x, me_y, nx, ny) + greet_column(
        barrier, me_x, me_y, ny
    )
    for b in range(steps):
        pl.semaphore_signal(barrier, inc=1, device_id=(partners[b], me_y), device_id_type=MESH)
    pl.semaphore_wait(barrier, expected + steps)

    def side_copy(a, b):
        return pltpu.make_async_remote_copy(
            src_ref=borrowed_ref.at[3 * a + b],
            dst_ref=side_land.at[a, b // 2],
            send_sem=hsend.at[a, b // 2],
            recv_sem=hrecv.at[a, b // 2],
            device_id=(me_x, me_y + b - 1),
            device_id_type=MESH,
        )

    def back_copy(a):
        return pltpu.make_async_remote_copy(
            src_ref=column.at[a // 2],
            dst_ref=x_land.at[a // 2],
            send_sem=bsend.at[a // 2],
            recv_sem=brecv.at[a // 2],
            device_id=(me_x + a - 1, me_y),
            device_id_type=MESH,
        )

    def sides(act, sign):
        for a in range(3):
            for b in (0, 2):

                @pl.when(exists(me_x + a - 1, nx) & exists(me_y + sign * (b - 1), ny))
                def _():
                    act(a, b)

    def column_copy(step, g):
        other = lax.rem(me_y + step, ny)
        return pltpu.make_async_remote_copy(
            src_ref=wpart_ref.at[other, g],
            dst_ref=yland.at[step - 1, g],
            send_sem=ysend.at[step - 1, g],
            recv_sem=yrecv.at[step - 1, g],
            device_id=(me_x, other),
            device_id_type=MESH,
        )

    late = list(range(2, steps))
    kinds = [[0, 1] + late, [1, 0] + late, late + [0, 1], late + [1, 0]]
    orders = [kinds[kind] for kind in KINDS]
    starts = []
    for g in range(groups):
        at = [0]
        for s in range(steps):
            at.append(at[-1] + bits[orders[g][s]] * (nx >> (s + 1)))
        starts.append(at)

    def scatter_copy(g, s):
        half = nx >> (s + 1)
        bit = bits[orders[g][s]]
        away = starts[g][s] + (1 - bit) * half
        return pltpu.make_async_remote_copy(
            src_ref=work.at[g, pl.ds(away, half)],
            dst_ref=xland.at[g, pl.ds(nx - 2 * half, half)],
            send_sem=rsend.at[s, g],
            recv_sem=rrecv.at[s, g],
            device_id=(partners[orders[g][s]], me_y),
            device_id_type=MESH,
        )

    def gather_copy(g, s, landing):
        half = nx >> (s + 1)
        bit = bits[orders[g][s]]
        mine = starts[g][s + 1]
        place = starts[g][s] + (1 - bit) * half if landing else mine
        return pltpu.make_async_remote_copy(
            src_ref=sum_ref.at[g, pl.ds(mine, half)],
            dst_ref=sum_ref.at[g, pl.ds(place, half)],
            send_sem=gsend.at[s, g],
            recv_sem=grecv.at[s, g],
            device_id=(partners[orders[g][s]], me_y),
            device_id_type=MESH,
        )

    for g in range(groups):
        for step in range(1, ny):
            column_copy(step, g).start()
    sides(lambda a, b: side_copy(a, b).start(), 1)

    def begin(g):
        value = wpart_ref[me_y, g].astype(jnp.float32)
        for step in range(1, ny):
            column_copy(step, g).wait_recv()
            value = value + yland[step - 1, g].astype(jnp.float32)
        work[g] = value.astype(work.dtype)
        scatter_copy(g, 0).start()

    def scatter(g, s):
        half = nx >> (s + 1)
        scatter_copy(g, s).wait_recv()
        keep = pl.ds(starts[g][s + 1], half)
        value = work[g, keep].astype(jnp.float32) + xland[g, pl.ds(nx - 2 * half, half)].astype(
            jnp.float32
        )
        if s < steps - 1:
            work[g, keep] = value.astype(work.dtype)
            scatter_copy(g, s + 1).start()
        else:
            sum_ref[g, keep] = value.astype(sum_ref.dtype)
            gather_copy(g, s, False).start()

    def gather(g, s):
        gather_copy(g, s, True).wait_recv()
        if s > 0:
            gather_copy(g, s - 1, False).start()

    events = []
    for g in range(groups):
        events.append((WAVES[g] * STAGGER, g, functools.partial(begin, g)))
        for s in range(steps):
            events.append((WAVES[g] * STAGGER + s + 1, g, functools.partial(scatter, g, s)))
            events.append(
                (WAVES[g] * STAGGER + 2 * steps - s, g, functools.partial(gather, g, s))
            )
    events.sort(key=lambda event: event[:2])
    first = [event[2] for event in events if event[0] < HALO_AT]
    rest = [event[2] for event in events if event[0] >= HALO_AT]
    for event in first:
        event()

    returned_ref[...] = jnp.zeros(returned_ref.shape, jnp.float32)
    for b in (0, 2):

        @pl.when(exists(me_y + 1 - b, ny))
        def _():
            side_copy(1, b).wait_recv()
            returned_ref[...] += side_land[1, b // 2].astype(jnp.float32)

    for a in (0, 2):

        @pl.when(exists(me_x + a - 1, nx))
        def _():
            for b in (0, 2):
                missing = jnp.logical_not(exists(me_y + 1 - b, ny))

                @pl.when(missing)
                def _():
                    side_land[a, b // 2] = jnp.zeros(side_land.shape[2:], side_land.dtype)

                @pl.when(jnp.logical_not(missing))
                def _():
                    side_copy(a, b).wait_recv()

            column[a // 2] = (
                borrowed_ref[3 * a + 1].astype(jnp.float32)
                + side_land[a, 0].astype(jnp.float32)
                + side_land[a, 1].astype(jnp.float32)
            ).astype(column.dtype)
            back_copy(a).start()

    for event in rest:
        event()

    for a in (0, 2):

        @pl.when(exists(me_x + 1 - a, nx))
        def _():
            back_copy(a).wait_recv()
            returned_ref[...] += x_land[a // 2].astype(jnp.float32)

    for g in range(groups):
        for step in range(1, ny):
            column_copy(step, g).wait_send()
        for s in range(steps):
            scatter_copy(g, s).wait_send()
            gather_copy(g, s, False).wait_send()
    sides(lambda a, b: side_copy(a, b).wait_send(), 1)
    for a in (0, 2):

        @pl.when(exists(me_x + a - 1, nx))
        def _():
            back_copy(a).wait_send()


def gather_kernel(
    nx,
    ny,
    send_in,
    feats_ref,
    weight_ref,
    bias_ref,
    table_ref,
    turned_ref,
    full_ref,
    pre_ref,
    grad_ref,
    send_ref,
    own,
    stage,
    bias,
    lsem,
    xsend,
    xrecv,
    hsend,
    hrecv,
    wsend,
    wrecv,
):
    me_x, me_y = lax.axis_index("gx"), lax.axis_index("gy")
    blocks, rows, width = feats_ref.shape
    shared_count = stage.shape[0]
    f32 = jnp.float32
    barrier = pltpu.get_barrier_semaphore()
    expected = greet_neighbours(barrier, me_x, me_y, nx, ny) + greet_column(
        barrier, me_x, me_y, ny
    )
    load = pltpu.make_async_copy(feats_ref, own, lsem.at[0])
    load.start()
    pick = pltpu.make_async_copy(send_in, send_ref, lsem.at[3])
    pick.start()
    file = pltpu.make_async_copy(feats_ref, table_ref.at[pl.ds(0, blocks)], lsem.at[4])
    file.start()
    shift = pltpu.make_async_copy(bias_ref, bias, lsem.at[2])
    shift.start()
    keep = pltpu.make_async_copy(weight_ref, full_ref.at[:, me_y], lsem.at[1])
    keep.start()
    pick.wait()
    load.wait()
    for s in range(shared_count):
        stage[s] = own[send_ref[s]]
    pl.semaphore_wait(barrier, expected)

    def first(a, b):
        d = 3 * a + b
        return blocks + shared_count * (d - (d > 4))

    def place(a, b):
        return table_ref.at[pl.ds(first(a, b), shared_count)]

    def x_copy(a, device_x):
        return pltpu.make_async_remote_copy(
            src_ref=stage,
            dst_ref=place(a, 1),
            send_sem=xsend.at[a // 2],
            recv_sem=xrecv.at[a // 2],
            device_id=(device_x, me_y),
            device_id_type=MESH,
        )

    def y_copy(a, b, device_y):
        return pltpu.make_async_remote_copy(
            src_ref=stage if a == 1 else place(a, 1),
            dst_ref=place(a, b),
            send_sem=hsend.at[a, b // 2],
            recv_sem=hrecv.at[a, b // 2],
            device_id=(me_x, device_y),
            device_id_type=MESH,
        )

    def weight_copy(step, owner):
        return pltpu.make_async_remote_copy(
            src_ref=weight_ref,
            dst_ref=full_ref.at[:, owner],
            send_sem=wsend.at[step],
            recv_sem=wrecv.at[step],
            device_id=(me_x, lax.rem(me_y + step, ny)),
            device_id_type=MESH,
        )

    def to_column(a, act):
        for b in (0, 2):
            target = me_y + 1 - b

            @pl.when(exists(target, ny))
            def _():
                act(y_copy(a, b, target))

    def turn(t, count):
        for at in range(t, t + count):
            turned_ref[at] = table_ref[at].T

    def clear(a, b):
        for at in range(first(a, b), first(a, b) + shared_count):
            table_ref[at] = jnp.zeros((rows, width), table_ref.dtype)

    for a in (0, 2):
        target = me_x + 1 - a

        @pl.when(exists(target, nx))
        def _():
            x_copy(a, target).start()

    to_column(1, lambda copy: copy.start())
    for step in range(1, ny):
        weight_copy(step, me_y).start()
    for a in (0, 2):

        @pl.when(jnp.logical_not(exists(me_x + a - 1, nx)))
        def _():
            clear(a, 1)

        for b in (0, 2):

            @pl.when(jnp.logical_not(exists(me_x + a - 1, nx) & exists(me_y + b - 1, ny)))
            def _():
                clear(a, b)

    for b in (0, 2):

        @pl.when(jnp.logical_not(exists(me_y + b - 1, ny)))
        def _():
            clear(1, b)

    file.wait()
    turn(0, blocks)
    shift.wait()
    for b in range(blocks):
        pre_ref[b] = jnp.broadcast_to(bias[...], (rows, width))
    pre_ref[blocks] = jnp.zeros((rows, width), f32)

    def blank(t, carry):
        grad_ref[t] = jnp.zeros((rows, width), f32)
        return carry

    lax.fori_loop(0, grad_ref.shape[0], blank, 0)

    def arrive(a, b):
        @pl.when(exists(me_x + a - 1, nx) & exists(me_y + b - 1, ny))
        def _():
            y_copy(a, b, me_y + b - 1).wait_recv()

        turn(first(a, b), shared_count)

    for b in (0, 2):
        arrive(1, b)
    for a in (0, 2):

        @pl.when(exists(me_x + a - 1, nx))
        def _():
            x_copy(a, me_x + a - 1).wait_recv()
            to_column(a, lambda copy: copy.start())

    for a in (0, 2):
        turn(first(a, 1), shared_count)
    for a in (0, 2):
        for b in (0, 2):
            arrive(a, b)

    for a in range(3):

        @pl.when(exists(me_x + a - 1, nx))
        def _():
            to_column(a, lambda copy: copy.wait_send())

    for a in (0, 2):
        target = me_x + 1 - a

        @pl.when(exists(target, nx))
        def _():
            x_copy(a, target).wait_send()

    for step in range(1, ny):
        weight_copy(step, lax.rem(me_y - step + ny, ny)).wait_recv()
        weight_copy(step, me_y).wait_send()
    keep.wait()


def layer_kernel(
    source_ref,
    target_ref,
    count_ref,
    table,
    weight_ref,
    cot_ref,
    pre_in,
    grad_in,
    out_ref,
    pre,
    grad,
    borrowed_ref,
    dpre_ref,
    out,
    osem,
):
    blocks, rows, width = cot_ref.shape
    slots = source_ref.shape[0]
    kvol = weight_ref.shape[0]
    total_blocks = table.shape[0]
    shared_count = borrowed_ref.shape[1]
    f32 = jnp.float32
    dpre_ref[blocks] = jnp.zeros((rows, width), dpre_ref.dtype)

    def forward(k, carry):
        live = count_ref[k]
        taken, targets = [], []
        for q in range(slots):
            taken.append(table[jnp.where(q < live, source_ref[q, k], 0)])
            targets.append(jnp.where(q < live, target_ref[q, k], blocks))
        made = jnp.dot(jnp.concatenate(taken, axis=0), weight_ref[k], preferred_element_type=f32)
        for q, target in enumerate(targets):
            pre[target] += made[q * rows : (q + 1) * rows]
        return carry

    lax.fori_loop(0, kvol, forward, 0, unroll=UNROLL)

    def activate(b, carry):
        value = pre[b]
        sig = jax.nn.sigmoid(value)
        out[b] = (value * sig).astype(out.dtype)
        dpre_ref[b] = (cot_ref[b].astype(f32) * sig * (1.0 + value * (1.0 - sig))).astype(
            dpre_ref.dtype
        )
        return carry

    lax.fori_loop(0, blocks, activate, 0, unroll=4)
    keep = pltpu.make_async_copy(out, out_ref, osem)
    keep.start()

    def backward(k, carry):
        live = count_ref[k]
        pulled, spread = [], []
        for q in range(slots):
            pulled.append(dpre_ref[jnp.where(q < live, target_ref[q, k], blocks)])
            spread.append(jnp.where(q < live, source_ref[q, k], total_blocks))
        back = lax.dot_general(
            jnp.concatenate(pulled, axis=0),
            weight_ref[k],
            (((1,), (1,)), ((), ())),
            preferred_element_type=f32,
        )
        for q, source in enumerate(spread):
            grad[source] += back[q * rows : (q + 1) * rows]
        return carry

    lax.fori_loop(0, kvol, backward, 0, unroll=UNROLL)
    at = blocks
    for d in range(9):
        for s in range(shared_count):
            if d != 4:
                borrowed_ref[d, s] = grad[at].astype(borrowed_ref.dtype)
                at += 1
    keep.wait()


def line_kernel(
    nx,
    ny,
    source_ref,
    target_ref,
    count_ref,
    send_in,
    turned_ref,
    dpre_ref,
    own_ref,
    borrowed_ref,
    wide_ref,
    feat_ref,
    send_ref,
    away,
    sums,
    back,
    work,
    yland,
    full_land,
    half_land,
    land,
    spare,
    side_land,
    column,
    x_land,
    ysend,
    csend,
    crecv,
    hsend,
    hrecv,
    bsend,
    brecv,
    picksem,
):
    me_x, me_y = lax.axis_index("gx"), lax.axis_index("gy")
    kvol, parts, deep, width = work.shape
    slots = source_ref.shape[0]
    blocks, rows = feat_ref.shape[:2]
    f32 = jnp.float32
    bit_x, bit_y, z = lax.rem(me_x, 2), lax.rem(me_x // 2, 2), me_x // 4
    high = z // 2
    beside = {"x": me_x + 1 - 2 * bit_x, "y": me_x + 2 - 4 * bit_y}
    inner = exists(z - 1, 2)
    near = jnp.where(inner, me_x - 4 + 8 * high, me_x + 4 - 8 * high)
    opposite = me_x + 12 - 8 * z

    pick = pltpu.make_async_copy(send_in, send_ref, picksem)
    pick.start()
    barrier = pltpu.get_barrier_semaphore()
    expected = greet_neighbours(barrier, me_x, me_y, nx, ny) + greet_column(
        barrier, me_x, me_y, ny
    )
    greeted = (beside["x"], beside["y"], near, opposite)
    for device in greeted:
        pl.semaphore_signal(barrier, inc=1, device_id=(device, me_y), device_id_type=MESH)

    def multiply(g, carry):
        live = count_ref[g]
        taken, pulled = [], []
        for q in range(slots):
            taken.append(turned_ref[jnp.where(q < live, source_ref[q, g], 0)])
            pulled.append(dpre_ref[jnp.where(q < live, target_ref[q, g], blocks)])
        part = jnp.dot(
            jnp.concatenate(taken, axis=1),
            jnp.concatenate(pulled, axis=0),
            preferred_element_type=f32,
        ).astype(work.dtype).reshape(ny, parts, deep, width)
        for y in range(ny):
            step = lax.rem(y - me_y + ny, ny)
            for d in range(ny):

                @pl.when(step == d)
                def _():
                    if d == 0:
                        work[g] = part[y]
                    else:
                        away[d - 1, g] = part[y]

        return carry

    lax.fori_loop(0, MAKE_FIRST, multiply, 0)

    pl.semaphore_wait(barrier, expected + len(greeted))

    pick.wait()

    def side_copy(a, b):
        return pltpu.make_async_remote_copy(
            src_ref=borrowed_ref.at[3 * a + b],
            dst_ref=side_land.at[a, b // 2],
            send_sem=hsend.at[a, b // 2],
            recv_sem=hrecv.at[a, b // 2],
            device_id=(me_x, me_y + b - 1),
            device_id_type=MESH,
        )

    def back_copy(a):
        return pltpu.make_async_remote_copy(
            src_ref=column.at[a // 2],
            dst_ref=x_land.at[a // 2],
            send_sem=bsend.at[a // 2],
            recv_sem=brecv.at[a // 2],
            device_id=(me_x + a - 1, me_y),
            device_id_type=MESH,
        )

    def sides(act, sign):
        for a in range(3):
            for b in (0, 2):

                @pl.when(exists(me_x + a - 1, nx) & exists(me_y + sign * (b - 1), ny))
                def _():
                    act(a, b)

    def column_copy(step, g):
        other = lax.rem(me_y + step, ny)
        return pltpu.make_async_remote_copy(
            src_ref=away.at[step - 1, g],
            dst_ref=yland.at[step - 1, g],
            send_sem=ysend.at[step - 1],
            recv_sem=crecv.at[4 + step - 1, g],
            device_id=(me_x, other),
            device_id_type=MESH,
        )

    def share(g, carry):
        for step in range(1, ny):
            column_copy(step, g).start()
        return carry

    def make(g, carry):
        return share(g, multiply(g, carry))

    lax.fori_loop(0, MAKE_FIRST, share, 0)
    sides(lambda a, b: side_copy(a, b).start(), 1)

    def give_back():
        back[...] = jnp.zeros(back.shape, f32)
        for b in (0, 2):

            @pl.when(exists(me_y + 1 - b, ny))
            def _():
                side_copy(1, b).wait_recv()
                back[...] += side_land[1, b // 2].astype(f32)

        for a in (0, 2):

            @pl.when(exists(me_x + a - 1, nx))
            def _():
                for b in (0, 2):
                    missing = jnp.logical_not(exists(me_y + 1 - b, ny))

                    @pl.when(missing)
                    def _():
                        side_land[a, b // 2] = jnp.zeros(side_land.shape[2:], side_land.dtype)

                    @pl.when(jnp.logical_not(missing))
                    def _():
                        side_copy(a, b).wait_recv()

                column[a // 2] = (
                    borrowed_ref[3 * a + 1].astype(f32)
                    + side_land[a, 0].astype(f32)
                    + side_land[a, 1].astype(f32)
                ).astype(column.dtype)
                back_copy(a).start()

    def take_back():
        for a in (0, 2):

            @pl.when(exists(me_x + 1 - a, nx))
            def _():
                back_copy(a).wait_recv()
                back[...] += x_land[a // 2].astype(f32)

        for b in range(blocks):
            value = own_ref[b]
            for s in range(back.shape[0]):
                value = value + jnp.where(send_ref[s] == b, back[s], 0.0)
            feat_ref[b] = value.astype(feat_ref.dtype)

    def own_sum(g):
        value = work[g].astype(f32)
        for step in range(1, ny):
            column_copy(step, g).wait_recv()
            value = value + yland[step - 1, g].astype(f32)
        return value

    def copy(g, src, dst, leave, arrive, device):
        return pltpu.make_async_remote_copy(
            src_ref=src,
            dst_ref=dst,
            send_sem=csend.at[leave],
            recv_sem=crecv.at[arrive, g],
            device_id=(device, me_y),
            device_id_type=MESH,
        )

    def program(order, inside):
        sent = {}
        made = MAKE_FIRST

        def send(g, src, dst, leave, arrive, device):
            copy(g, src, dst, leave, arrive, device).start()
            sent[leave] = sent.get(leave, 0) + math.prod(src.shape[:-2])

        def recv(g, dst, arrive):
            copy(g, dst, dst, 0, arrive, beside["x"]).wait_recv()

        def finish(g):
            wide_ref[g] = sums[g].reshape(parts * deep, width).astype(f32) * (1.0 / rows)

        def along(g, k):
            first = LINE_KINDS[g][1]
            second = "y" if first == "x" else "x"
            bits = {"x": bit_x, "y": bit_y}
            hb, qb = bits[first], bits[second]
            mine, other = 2 * hb + qb, 2 * hb + 1 - qb
            kept, gone = pl.ds(2 * hb, 2), pl.ds(2 - 2 * hb, 2)
            total, ours = sums.at[g], work.at[g]
            if k == 0:
                work[g] = own_sum(g).astype(work.dtype)
                send(g, ours.at[gone], half_land.at[g], 0, 0, beside[first])
            elif k == 1:
                recv(g, half_land.at[g], 0)
                work[g, kept] = (
                    work[g, kept].astype(f32) + half_land[g].astype(f32)
                ).astype(work.dtype)
                send(g, ours.at[other], land.at[0, g], 1, 1, beside[second])
            elif k == 2:
                recv(g, land.at[0, g], 1)
                work[g, mine] = (
                    work[g, mine].astype(f32) + land[0, g].astype(f32)
                ).astype(work.dtype)
                if not inside:
                    send(g, ours.at[mine], land.at[1, g], 2, 2, near)
            elif k == 3:
                recv(g, land.at[1, g], 2)
                work[g, mine] = (
                    work[g, mine].astype(f32) + land[1, g].astype(f32)
                ).astype(work.dtype)
                send(g, ours.at[mine], land.at[2, g], 3, 3, opposite)
            elif k == 4:
                recv(g, land.at[2, g], 3)
                sums[g, mine] = (
                    work[g, mine].astype(f32) + land[2, g].astype(f32)
                ).astype(sums.dtype)
                send(g, total.at[mine], total.at[mine], 2, 2, near)
                send(g, total.at[mine], total.at[mine], 4, 0, beside[second])
            elif k == 5:
                recv(g, total.at[mine], 2)
                send(g, total.at[mine], total.at[mine], 4, 0, beside[second])
            elif k == 6:
                recv(g, total.at[other], 0)
                send(g, total.at[kept], total.at[kept], 5, 4, beside[first])
            elif k == 7:
                recv(g, total.at[gone], 4)
                finish(g)

        def fold(g, k):
            first = LINE_KINDS[g][1]
            second = "y" if first == "x" else "x"
            bits = {"x": bit_x, "y": bit_y}
            hb, qb = high, bits[first]
            mine, other = 2 * hb + qb, 2 * hb + 1 - qb
            kept, gone = pl.ds(2 * hb, 2), pl.ds(2 - 2 * hb, 2)
            total, ours = sums.at[g], work.at[g]
            hub = inside if LINE_KINDS[g][0] == "B" else not inside
            if not hub:
                if k == 0:
                    work[g] = own_sum(g).astype(work.dtype)
                    send(g, ours, full_land.at[g], 6, 2, near)
                elif k == 6:
                    recv(g, total.at[kept], 2)
                elif k == 7:
                    recv(g, total.at[gone], 3)
                    finish(g)
            elif k == 1:
                value = own_sum(g)
                recv(g, full_land.at[g], 2)
                work[g] = (value + full_land[g].astype(f32)).astype(work.dtype)
                send(g, ours.at[gone], half_land.at[g], 7, 3, opposite)
            elif k == 2:
                recv(g, half_land.at[g], 3)
                work[g, kept] = (
                    work[g, kept].astype(f32) + half_land[g].astype(f32)
                ).astype(work.dtype)
                send(g, ours.at[other], land.at[0, g], 1, 0, beside[first])
            elif k == 3:
                recv(g, land.at[0, g], 0)
                work[g, mine] = (
                    work[g, mine].astype(f32) + land[0, g].astype(f32)
                ).astype(work.dtype)
                send(g, ours.at[mine], land.at[1, g], 1, 1, beside[second])
            elif k == 4:
                recv(g, land.at[1, g], 1)
                sums[g, mine] = (
                    work[g, mine].astype(f32) + land[1, g].astype(f32)
                ).astype(sums.dtype)
                send(g, total.at[mine], total.at[mine], 4, 4, beside[first])
            elif k == 5:
                recv(g, total.at[other], 4)
                send(g, total.at[kept], total.at[kept], 8, 2, opposite)
                send(g, total.at[kept], total.at[kept], 8, 2, near)
            elif k == 6:
                recv(g, total.at[gone], 2)
                send(g, total.at[gone], total.at[gone], 8, 3, near)
                finish(g)

        for event in order:
            g, k = divmod(event, 10)
            while made < kvol and g < kvol and made <= g + MAKE_LEAD:
                upto = min(kvol, made + MAKE_STEP)
                lax.fori_loop(made, upto, make, 0)
                made = upto
            if g == kvol:
                (give_back, take_back)[k]()
            elif LINE_KINDS[g][0] != "A":
                fold(g, k)
            else:
                along(g, k)
        for leave, pieces in sent.items():
            gone = spare.at[pl.ds(0, pieces)]
            copy(0, gone, gone, leave, 0, beside["x"]).wait_send()

    @pl.when(inner)
    def _():
        program(LINE_ORDERS[0], True)

    @pl.when(jnp.logical_not(inner))
    def _():
        program(LINE_ORDERS[1], False)

    for step in range(1, ny):
        other = lax.rem(me_y + step, ny)
        pltpu.make_async_remote_copy(
            src_ref=away.at[step - 1],
            dst_ref=yland.at[step - 1],
            send_sem=ysend.at[step - 1],
            recv_sem=crecv.at[4 + step - 1, 0],
            device_id=(me_x, other),
            device_id_type=MESH,
        ).wait_send()
    sides(lambda a, b: side_copy(a, b).wait_send(), 1)
    for a in (0, 2):

        @pl.when(exists(me_x + a - 1, nx))
        def _():
            back_copy(a).wait_send()


def finish_kernel(
    send_ref, total_ref, own_ref, returned_ref, weight_ref, feat_ref, wide, feats, wsem, fsem
):
    chunks = wsem.shape[0]
    kvol, share, width = wide.shape
    per = kvol // chunks
    blocks, rows = feat_ref.shape[:2]
    copies = []
    for c in range(chunks):
        at = pl.ds(c * per, per)
        for h in range(width // LANES):
            wide[at, :, h * LANES : (h + 1) * LANES] = total_ref[h, at].reshape(
                per, share, LANES
            ).astype(jnp.float32) * (1.0 / rows)
        copy = pltpu.make_async_copy(wide.at[at], weight_ref.at[at], wsem.at[c])
        copy.start()
        copies.append(copy)
    for b in range(blocks):
        value = own_ref[b]
        for s in range(returned_ref.shape[0]):
            value = value + jnp.where(send_ref[s] == b, returned_ref[s], 0.0)
        feats[b] = value.astype(feats.dtype)
        copy = pltpu.make_async_copy(feats.at[b], feat_ref.at[b], fsem.at[b])
        copy.start()
        copies.append(copy)
    for copy in copies:
        copy.wait()


def store_kernel(wide_ref, feat_ref, weight_out, feat_out, sem):
    chunks = sem.shape[0] - 1
    per = wide_ref.shape[0] // chunks
    copies = [pltpu.make_async_copy(feat_ref, feat_out, sem.at[chunks])]
    for c in range(chunks):
        at = pl.ds(c * per, per)
        copies.append(pltpu.make_async_copy(wide_ref.at[at], weight_out.at[at], sem.at[c]))
    for copy in copies:
        copy.start()
    for copy in copies:
        copy.wait()


def on_device(
    nx,
    ny,
    features,
    kernel_weight,
    channel_bias,
    send_list,
    rule_source,
    rule_target,
    live_counts,
    out_grad,
):
    feats = features[0, 0]
    blocks, rows, width = feats.shape
    shared = send_list[0, 0]
    shared_count = shared.shape[0]
    kvol, slots = rule_source.shape[2:]
    share = kernel_weight.shape[1]
    bf16, f32 = jnp.bfloat16, jnp.float32
    shape = jax.ShapeDtypeStruct
    vmem = pl.BlockSpec(memory_space=VMEM)
    smem = pl.BlockSpec(memory_space=SMEM)
    hbm = pl.BlockSpec(memory_space=pltpu.HBM)
    dma = pltpu.SemaphoreType.DMA
    squares = 9

    total_blocks = blocks + (squares - 1) * shared_count
    if nx == 4 * LINE_LENGTH and kvol == len(LINE_KINDS):
        stay = functools.partial(pltpu.with_memory_space_constraint, memory_space=pltpu.HBM)
        rules = (rule_source[0, 0].T, rule_target[0, 0].T, live_counts.reshape(-1))
        boundary = (shared_count, rows, width)
        quarters = (4, share // 4, width)
        table, turned, full, pre, grad = pl.pallas_call(
            functools.partial(gather_kernel, nx, ny),
            out_shape=(
                shape((total_blocks, rows, width), bf16),
                shape((total_blocks, width, rows), bf16),
                shape((kvol, ny, share, width), bf16),
                shape((blocks + 1, rows, width), f32),
                shape((total_blocks + 1, rows, width), f32),
            ),
            in_specs=[hbm] * 4,
            out_specs=(vmem,) * 5,
            scratch_shapes=[
                SMEM((shared_count,), jnp.int32),
                VMEM((blocks, rows, width), bf16),
                VMEM(boundary, bf16),
                VMEM((1, width), f32),
                dma((5,)),
                dma((2,)),
                dma((2,)),
                dma((3, 2)),
                dma((3, 2)),
                dma((ny,)),
                dma((ny,)),
            ],
            compiler_params=pltpu.CompilerParams(
                collective_id=3, has_side_effects=True, vmem_limit_bytes=GATHER_BYTES
            ),
        )(*(stay(v) for v in (shared, feats, kernel_weight, channel_bias.reshape(1, width))))
        outputs, _, grad, borrowed, dpre = pl.pallas_call(
            layer_kernel,
            out_shape=(
                shape((blocks, rows, width), bf16),
                shape((blocks + 1, rows, width), f32),
                shape((total_blocks + 1, rows, width), f32),
                shape((squares,) + boundary, bf16),
                shape((blocks + 1, rows, width), bf16),
            ),
            in_specs=[smem, smem, smem, vmem, vmem, vmem, vmem, vmem],
            out_specs=(hbm, vmem, vmem, vmem, vmem),
            scratch_shapes=[VMEM((blocks, rows, width), bf16), dma(())],
            input_output_aliases={6: 1, 7: 2},
            compiler_params=pltpu.CompilerParams(vmem_limit_bytes=LAYER_BYTES),
        )(
            *rules,
            table,
            full.reshape(kvol, width, width),
            out_grad[0, 0],
            pre,
            grad,
        )
        wide, feat = pl.pallas_call(
            functools.partial(line_kernel, nx, ny),
            out_shape=(shape((kvol, share, width), f32), shape((blocks, rows, width), bf16)),
            in_specs=[smem, smem, smem, hbm, vmem, vmem, vmem, vmem],
            out_specs=(vmem, vmem),
            scratch_shapes=[
                SMEM((shared_count,), jnp.int32),
                VMEM((max(ny - 1, 1), kvol) + quarters, bf16),
                VMEM((kvol,) + quarters, bf16),
                VMEM(boundary, f32),
                VMEM((kvol,) + quarters, bf16),
                VMEM((max(ny - 1, 1), kvol) + quarters, bf16),
                VMEM((kvol,) + quarters, bf16),
                VMEM((kvol, 2) + quarters[1:], bf16),
                VMEM((3, kvol) + quarters[1:], bf16),
                VMEM((8 * kvol,) + quarters[1:], bf16),
                VMEM((3, 2) + boundary, bf16),
                VMEM((2,) + boundary, bf16),
                VMEM((2,) + boundary, bf16),
                dma((max(ny - 1, 1),)),
                dma((9,)),
                dma((4 + max(ny - 1, 1), kvol)),
                dma((3, 2)),
                dma((3, 2)),
                dma((2,)),
                dma((2,)),
                dma(()),
            ],
            compiler_params=pltpu.CompilerParams(
                collective_id=2, has_side_effects=True, vmem_limit_bytes=LINE_BYTES
            ),
        )(*rules, stay(shared), turned, dpre, grad, borrowed)
        chunks = max(c for c in range(1, 10) if kvol % c == 0)
        weight_grad, feat_grad = pl.pallas_call(
            store_kernel,
            out_shape=(shape((kvol, share, width), f32), shape((blocks, rows, width), bf16)),
            in_specs=[vmem, vmem],
            out_specs=(hbm, hbm),
            scratch_shapes=[dma((chunks + 1,))],
            compiler_params=pltpu.CompilerParams(vmem_limit_bytes=VMEM_BYTES),
        )(wide, feat)
        return (outputs[None, None], feat_grad[None, None], weight_grad)

    halo, full = pl.pallas_call(
        functools.partial(exchange_kernel, nx, ny),
        out_shape=(
            shape((squares, shared_count, rows, width), bf16),
            shape((kvol, ny, share, width), bf16),
        ),
        in_specs=[smem, hbm, hbm],
        out_specs=(vmem, vmem),
        scratch_shapes=[
            VMEM((blocks, rows, width), bf16),
            dma((2,)),
            dma((2,)),
            dma((2,)),
            dma((3, 2)),
            dma((3, 2)),
            dma((ny,)),
            dma((ny,)),
        ],
        compiler_params=pltpu.CompilerParams(
            collective_id=0, has_side_effects=True, vmem_limit_bytes=EXCHANGE_BYTES
        ),
    )(shared, feats, kernel_weight)

    used = (width // LANES) * kvol * (share // TILE)
    groups = len(KINDS)
    unit = groups * nx
    tiles = -(-used // unit) * unit
    depth = tiles // unit
    outputs, own, borrowed, wpart = pl.pallas_call(
        compute_kernel,
        out_shape=(
            shape((blocks, rows, width), bf16),
            shape((blocks, rows, width), f32),
            shape((squares, shared_count, rows, width), bf16),
            shape((ny, tiles, TILE, LANES), bf16),
        ),
        in_specs=[smem, smem, smem, vmem, vmem, vmem, vmem, vmem],
        out_specs=(vmem, vmem, vmem, vmem),
        scratch_shapes=[
            VMEM((total_blocks, rows, width), bf16),
            VMEM((total_blocks, width, rows), bf16),
            VMEM((blocks + 1, rows, width), f32),
            VMEM((blocks + 1, rows, width), bf16),
            VMEM((total_blocks + 1, rows, width), f32),
        ],
        compiler_params=pltpu.CompilerParams(vmem_limit_bytes=VMEM_BYTES),
    )(
        rule_source[0, 0].T,
        rule_target[0, 0].T,
        live_counts.reshape(-1),
        feats,
        halo,
        full.reshape(kvol, width, width),
        channel_bias.reshape(1, width),
        out_grad[0, 0],
    )

    steps = nx.bit_length() - 1
    block = (depth, TILE, LANES)
    boundary = (shared_count, rows, width)
    total, returned = pl.pallas_call(
        functools.partial(reduce_kernel, nx, ny),
        out_shape=(
            shape((groups, nx) + block, bf16),
            shape(boundary, f32),
        ),
        in_specs=[vmem, vmem],
        out_specs=(vmem, vmem),
        scratch_shapes=[
            VMEM((groups, nx) + block, bf16),
            VMEM((max(ny - 1, 1), groups, nx) + block, bf16),
            VMEM((groups, nx) + block, bf16),
            VMEM((3, 2) + boundary, bf16),
            VMEM((2,) + boundary, bf16),
            VMEM((2,) + boundary, bf16),
            dma((max(ny - 1, 1), groups)),
            dma((max(ny - 1, 1), groups)),
            dma((steps, groups)),
            dma((steps, groups)),
            dma((steps, groups)),
            dma((steps, groups)),
            dma((3, 2)),
            dma((3, 2)),
            dma((2,)),
            dma((2,)),
        ],
        compiler_params=pltpu.CompilerParams(
            collective_id=1, has_side_effects=True, vmem_limit_bytes=VMEM_BYTES
        ),
    )(wpart.reshape((ny, groups, nx) + block), borrowed)

    halves, share_tiles = width // LANES, share // TILE
    chunks = max(c for c in range(1, 10) if kvol % c == 0)
    weight_grad, feat_grad = pl.pallas_call(
        finish_kernel,
        out_shape=(shape((kvol, share, width), f32), shape((blocks, rows, width), bf16)),
        in_specs=[smem, vmem, vmem, vmem],
        out_specs=(hbm, hbm),
        scratch_shapes=[
            VMEM((kvol, share, width), f32),
            VMEM((blocks, rows, width), bf16),
            dma((chunks,)),
            dma((blocks,)),
        ],
        compiler_params=pltpu.CompilerParams(vmem_limit_bytes=VMEM_BYTES),
    )(
        shared,
        total.reshape(tiles, TILE, LANES)[:used].reshape(halves, kvol, share_tiles, TILE, LANES),
        own,
        returned,
    )
    return (outputs[None, None], feat_grad[None, None], weight_grad)


def solution(mesh):
    return jax.shard_map(
        functools.partial(on_device, mesh.shape["gx"], mesh.shape["gy"]),
        mesh=mesh,
        in_specs=(
            P("gx", "gy", None, None, None),
            P(None, "gy", None),
            P(),
            P("gx", "gy", None),
            P("gx", "gy", None, None),
            P("gx", "gy", None, None),
            P("gx", "gy", None),
            P("gx", "gy", None, None, None),
        ),
        out_specs=(
            P("gx", "gy", None, None, None),
            P("gx", "gy", None, None, None),
            P(None, "gy", None),
        ),
        check_vma=False,
    )
```
